128 devices in a mesh: gx: 8 (over x, core), gy: 16 (over z, y).
Axes of the slice: x: 4, y: 4, z: 4, core: 2. Of those that a mesh axis runs over, the one named last changes fastest.
Arguments:
- fields: float32 [4, 128, 256, 128], P(None, 'gx', 'gy'), may hold values from -6 to 6
- lift: float32 [32, 4], replicated, may hold values from -3 to 3
- lift_bias: float32 [32], replicated, may hold values from -3 to 3
- spectral_in: float32 [256, 2, 8, 32, 64], P(('gx', 'gy')), may hold values from -0.015625 to 0.015625
- bypass_in: float32 [64, 32], replicated, may hold values from -1 to 1
- bias_in: float32 [64], replicated, may hold values from -3 to 3
- spectral_out: float32 [256, 2, 8, 64, 32], P(('gx', 'gy')), may hold values from -0.0234375 to 0.0234375
- bypass_out: float32 [32, 64], replicated, may hold values from -0.75 to 0.75
- bias_out: float32 [32], replicated, may hold values from -3 to 3
- project: float32 [4, 32], replicated, may hold values from -1 to 1
- project_bias: float32 [4], replicated, may hold values from -3 to 3
Outputs:
- result: float32 [4, 128, 256, 128], P(None, 'gx', 'gy')
The draws below stay inside these ranges and needn't reach their ends.
All inputs are finite; a program needn't handle non-finite values.
Results may differ from the reference program's by a relative error of at most 0.000058.
Values sent between devices are 32-bit elements; how exact they have to be, the bound alone decides.
No kernel may reach another device: no remote copies, remote signals or barrier semaphores. Data moves between devices by JAX's collectives and lax.ppermute only.
A program may use at most 64 MiB of HBM per device.

```python
import math
import jax
import jax.numpy as jnp
from jax import lax

CIN = 4
C1 = 32
C2 = 64
KX = 16
KY = 16
KZ = 8
NZ = 128
NX = 128
NY = 256


def wave_table(length, count, offset):
    places = jnp.arange(length, dtype=jnp.int32)
    frequency = jnp.arange(count, dtype=jnp.int32) - offset
    turns = places[:, None] * frequency[None, :] % length
    angle = turns.astype(jnp.float32) * (2.0 * math.pi / length)
    return (jnp.cos(angle), jnp.sin(angle), frequency.astype(jnp.float32))


def draw_fields(key, part):
    key_real = jax.random.fold_in(key, 101)
    key_imag = jax.random.fold_in(key, 202)
    key_rough = jax.random.fold_in(key, 303)
    x_cos, x_sin, freq_x = wave_table(NX, 2 * KX, KX)
    y_cos, y_sin, freq_y = wave_table(NY, 2 * KY, KY)
    z_cos, z_sin, freq_z = wave_table(NZ, 2 * KZ, 0)
    ratio = (freq_x[:, None, None] / KX) ** 2 + (freq_y[None, :, None] / KY) ** 2 + (freq_z[None, None, :] / KZ) ** 2
    amplitude = 1.0 / (1.0 + 2.0 * ratio)
    real_coef = jax.random.normal(key_real, (CIN, 2 * KX, 2 * KY, 2 * KZ), jnp.float32) * amplitude[None]
    imag_coef = jax.random.normal(key_imag, (CIN, 2 * KX, 2 * KY, 2 * KZ), jnp.float32) * amplitude[None]
    highest = lax.Precision.HIGHEST
    real_x = jnp.einsum('cijk,xi->cxjk', real_coef, x_cos, precision=highest) - jnp.einsum('cijk,xi->cxjk', imag_coef, x_sin, precision=highest)
    imag_x = jnp.einsum('cijk,xi->cxjk', real_coef, x_sin, precision=highest) + jnp.einsum('cijk,xi->cxjk', imag_coef, x_cos, precision=highest)
    real_y = jnp.einsum('cxjk,yj->cxyk', real_x, y_cos, precision=highest) - jnp.einsum('cxjk,yj->cxyk', imag_x, y_sin, precision=highest)
    imag_y = jnp.einsum('cxjk,yj->cxyk', real_x, y_sin, precision=highest) + jnp.einsum('cxjk,yj->cxyk', imag_x, y_cos, precision=highest)
    smooth = jnp.einsum('cxyk,zk->cxyz', real_y, z_cos, precision=highest) - jnp.einsum('cxyk,zk->cxyz', imag_y, z_sin, precision=highest)
    smooth = smooth / jnp.sqrt(jnp.sum(amplitude * amplitude))
    rough = jax.random.normal(key_rough, (CIN, NX, NY, NZ), jnp.float32)
    value = smooth + 0.5 * rough
    return jnp.clip(value, -6.0, 6.0)


def levels(rng, dims, pieces, least, top_value):
    level = 1.0
    for position, blocks in pieces:
        draws = jax.random.uniform(jax.random.fold_in(jax.random.fold_in(rng, 6), position), (blocks,), jnp.float32, least / len(pieces), top_value / len(pieces))
        level = level * jnp.repeat(jnp.exp(draws), dims[position] // blocks).reshape((-1,) + (1,) * (len(dims) - 1 - position))
    return level


def gaussian(own_key, extent, deviation, limit, split=(), held_as=jnp.bfloat16):
    values = jax.random.normal(own_key, extent, jnp.float32) * deviation
    if len(split) > 0:
        values = levels(own_key, extent, split, -0.22, 0.18) * values
    return jnp.clip(values, min=-limit, max=limit).astype(held_as)


def setup_inputs(seed: int = 0) -> dict:
    seeds = jax.random.split(jax.random.key(seed), 12)
    return {
        "fields": draw_fields(jax.random.fold_in(seeds[11], 71), 0),
        "lift": gaussian(seeds[1], (C1, CIN), CIN ** -0.5, 3.0, (), jnp.float32),
        "lift_bias": gaussian(seeds[2], (C1,), 0.5, 3.0, (), jnp.float32),
        "spectral_in": gaussian(seeds[3], (KX * KY, 2, KZ, C1, C2), (2 * C1 * NX * NY * NZ // (KX * KY * KZ)) ** -0.5, 0.015625, ((0, 128),), jnp.float32),
        "bypass_in": gaussian(seeds[4], (C2, C1), C1 ** -0.5, 1.0, (), jnp.float32),
        "bias_in": gaussian(seeds[5], (C2,), 0.5, 3.0, (), jnp.float32),
        "spectral_out": gaussian(seeds[6], (KX * KY, 2, KZ, C2, C1), (2 * C2 * NX * NY * NZ // (4 * KX * KY * KZ)) ** -0.5, 0.0234375, ((0, 128),), jnp.float32),
        "bypass_out": gaussian(seeds[7], (C1, C2), C2 ** -0.5, 0.75, (), jnp.float32),
        "bias_out": gaussian(seeds[8], (C1,), 0.5, 3.0, (), jnp.float32),
        "project": gaussian(seeds[9], (CIN, C1), C1 ** -0.5, 1.0, (), jnp.float32),
        "project_bias": gaussian(seeds[10], (CIN,), 0.5, 3.0, (), jnp.float32),
    }


def product(formula, left, right):
    return jnp.einsum(formula, left, right, precision=lax.Precision.HIGHEST)

def tables(places, length, count, centered):
    frequency = jnp.arange(count, dtype=jnp.int32)
    if centered:
        frequency = jnp.where(frequency < count // 2, frequency, frequency - count)
    turns = places.astype(jnp.int32)[:, None] * frequency[None, :] % length
    angle = turns.astype(jnp.float32) * (2.0 * math.pi / length)
    return (jnp.cos(angle), jnp.sin(angle))

def forward(field, x_places, y_places, x_length, y_length, scale):
    z_length = field.shape[3]
    z_cos, z_sin = tables(jnp.arange(z_length, dtype=jnp.int32), z_length, KZ, False)
    real_part = product('cxyz,zk->cxyk', field, z_cos)
    imag_part = -product('cxyz,zk->cxyk', field, z_sin)
    y_cos, y_sin = tables(y_places, y_length, KY, True)
    real_next = product('cxyk,yj->cxjk', real_part, y_cos) + product('cxyk,yj->cxjk', imag_part, y_sin)
    imag_next = product('cxyk,yj->cxjk', imag_part, y_cos) - product('cxyk,yj->cxjk', real_part, y_sin)
    x_cos, x_sin = tables(x_places, x_length, KX, True)
    real_last = product('cxjk,xi->ijkc', real_next, x_cos) + product('cxjk,xi->ijkc', imag_next, x_sin)
    imag_last = product('cxjk,xi->ijkc', imag_next, x_cos) - product('cxjk,xi->ijkc', real_next, x_sin)
    stacked = jnp.stack([real_last, imag_last], axis=2)
    return stacked.reshape((KX * KY, 2, KZ, stacked.shape[4])) * scale

def mix_modes(spectrum, weights):
    real_in = spectrum[:, 0]
    imag_in = spectrum[:, 1]
    real_weight = weights[:, 0]
    imag_weight = weights[:, 1]
    real_out = product('mkc,mkcd->mkd', real_in, real_weight) - product('mkc,mkcd->mkd', imag_in, imag_weight)
    imag_out = product('mkc,mkcd->mkd', real_in, imag_weight) + product('mkc,mkcd->mkd', imag_in, real_weight)
    return jnp.stack([real_out, imag_out], axis=1)

def inverse(spectrum, x_places, y_places, x_length, y_length, z_length, scale):
    grid = spectrum.reshape((KX, KY, 2, KZ, spectrum.shape[3]))
    real_part = grid[:, :, 0]
    imag_part = grid[:, :, 1]
    x_cos, x_sin = tables(x_places, x_length, KX, True)
    real_next = product('ijkc,xi->xjkc', real_part, x_cos) - product('ijkc,xi->xjkc', imag_part, x_sin)
    imag_next = product('ijkc,xi->xjkc', real_part, x_sin) + product('ijkc,xi->xjkc', imag_part, x_cos)
    y_cos, y_sin = tables(y_places, y_length, KY, True)
    real_last = product('xjkc,yj->xykc', real_next, y_cos) - product('xjkc,yj->xykc', imag_next, y_sin)
    imag_last = product('xjkc,yj->xykc', real_next, y_sin) + product('xjkc,yj->xykc', imag_next, y_cos)
    z_cos, z_sin = tables(jnp.arange(z_length, dtype=jnp.int32), z_length, KZ, False)
    return (product('xykc,zk->cxyz', real_last, z_cos) - product('xykc,zk->cxyz', imag_last, z_sin)) * scale

def reference(fields, lift, lift_bias, spectral_in, bypass_in, bias_in, spectral_out, bypass_out, bias_out, project, project_bias):
    back = math.sqrt(2.0 / (KX * KY * KZ))
    lifted = product('dc,cxyz->dxyz', lift, fields) + lift_bias[:, None, None, None]
    full_x = jnp.arange(NX, dtype=jnp.int32)
    full_y = jnp.arange(NY, dtype=jnp.int32)
    half_x = jnp.arange(NX // 2, dtype=jnp.int32)
    half_y = jnp.arange(NY // 2, dtype=jnp.int32)
    spectrum = forward(lifted, full_x, full_y, NX, NY, 1.0 / math.sqrt(NX * NY * NZ))
    mixed = mix_modes(spectrum, spectral_in)
    pooled = lifted.reshape((C1, NX // 2, 2, NY // 2, 2, NZ)).mean(axis=(2, 4))
    coarse = jax.nn.gelu(inverse(mixed, 2 * half_x, 2 * half_y, NX, NY, NZ, back) + product('ec,cxyz->exyz', bypass_in, pooled) + bias_in[:, None, None, None], approximate=False)
    spectrum = forward(coarse, half_x, half_y, NX // 2, NY // 2, 1.0 / math.sqrt(NX * NY * NZ / 4.0))
    mixed = mix_modes(spectrum, spectral_out)
    narrow = product('dc,cxyz->dxyz', bypass_out, coarse)
    widened = jnp.repeat(jnp.repeat(narrow, 2, axis=1), 2, axis=2)
    fine = jax.nn.gelu(inverse(mixed, full_x, full_y, NX, NY, NZ, back) + widened + bias_out[:, None, None, None], approximate=False)
    return product('oc,cxyz->oxyz', project, fine + lifted) + project_bias[:, None, None, None]
```

```python
import functools
import math

import jax
import jax.numpy as jnp
import numpy as np
from jax import lax
from jax.experimental import pallas as pl
from jax.experimental.pallas import tpu as pltpu
from jax.sharding import PartitionSpec as P

KX, KY, KZ = 16, 16, 8
NX, NY, NZ = 128, 256, 128
CIN, C1, C2 = 4, 32, 64
AXES = ("gx", "gy")
OWNERS = 128
TOTAL = NX * NY * NZ
BACK = math.sqrt(2.0 / (KX * KY * KZ))
F32 = jnp.float32
BF16 = jnp.bfloat16
VMEM = pl.BlockSpec(memory_space=pltpu.VMEM)
SMEM = pl.BlockSpec(memory_space=pltpu.SMEM)
PARAMS = pltpu.CompilerParams(vmem_limit_bytes=40 << 20)


def mode_frequencies():
    centered = np.where(np.arange(16) < 8, np.arange(16), np.arange(16) - 16)
    n = np.arange(OWNERS)
    fx = np.stack([centered[n // 8]] * 2)
    fy = np.stack([centered[2 * (n % 8) + s] for s in range(2)])
    return fx, fy


def place_angles(xs, ys, x_length, y_length):
    fx, fy = mode_frequencies()
    turns = (
        fx[:, :, None, None] * xs[None, None, :, None] / x_length
        + fy[:, :, None, None] * ys[None, None, None, :] / y_length
    )
    return 2.0 * np.pi * turns


def inverse_tables(angles, scale):
    out = []
    for shift in (0.0, 0.5 * np.pi):
        c, s = np.cos(angles + shift), np.sin(angles + shift)
        table = np.array([[c, -s], [s, c]])
        table = table.transpose(0, 4, 5, 2, 1, 3) * scale
        rows = 2 * angles.shape[2] * angles.shape[3]
        out.append(table.reshape(rows, 512).astype(np.float32))
    return out


def forward_tables(angles, scale):
    out = []
    for shift in (0.0, 0.5 * np.pi):
        c, s = np.cos(angles + shift), np.sin(angles + shift)
        table = np.array([[c, s], [-s, c]])
        table = table.transpose(2, 0, 3, 5, 4, 1) * scale
        out.append(table.reshape(512, -1).astype(np.float32))
    return out


def z_angles():
    return 2.0 * np.pi * (np.arange(NZ)[:, None] * np.arange(KZ)[None, :] % NZ) / NZ


def first_z_table():
    c, s = np.cos(z_angles()), np.sin(z_angles())
    parts = np.array([[c, -s], [-s, -c]])
    table = np.zeros((CIN, NZ, 2, 2, KZ, CIN))
    for ch in range(CIN):
        table[ch, :, :, :, :, ch] = parts.transpose(2, 0, 1, 3)
    return table.reshape(CIN, NZ, 128).astype(np.float32)


def first_places_table():
    angles = place_angles(np.arange(16), np.arange(16), NX, NY)
    table = np.stack([np.cos(angles), np.sin(angles)], axis=1) / math.sqrt(TOTAL)
    return table.reshape(512, 256).astype(np.float32)


def split_np(table):
    high = table.astype(BF16)
    low = (table - high.astype(np.float32)).astype(BF16)
    return high, low


def inverse_z_table():
    table = np.stack([np.cos(z_angles()), -np.sin(z_angles())], axis=2)
    high, low = split_np(table.reshape(NZ, 16).astype(np.float32))
    return np.concatenate([high, high, low], axis=1)


def forward_z_table():
    table = np.stack([np.cos(z_angles()).T, -np.sin(z_angles()).T], axis=0)
    return np.concatenate(split_np(table.reshape(16, NZ).astype(np.float32)), axis=0)


def split(x):
    high = x.astype(BF16)
    return high, (x - high.astype(F32)).astype(BF16)


def mm(a, b, dims=((1,), (0,))):
    return lax.dot_general(a, b, (dims, ((), ())), preferred_element_type=F32)


def mm3(a, b, dims=((1,), (0,))):
    ah, al = split(a)
    bh, bl = split(b)
    return mm(ah, bh, dims) + mm(ah, bl, dims) + mm(al, bh, dims)


def gelu(x):
    return 0.5 * x * (1.0 + lax.erf(x * math.sqrt(0.5)))


def half_swap(x):
    return pltpu.roll(x, 64, 1)


def first_spectrum(fields, ztab, ptab, phase, out):
    lane = lax.broadcasted_iota(jnp.int32, (128, 128), 1)
    low = lane < 64
    sign = jnp.where(low, 1.0, -1.0).astype(F32)
    transformed = mm3(fields[0].reshape(256, NZ), ztab[0])
    for ch in range(1, CIN):
        transformed += mm3(fields[ch].reshape(256, NZ), ztab[ch])
    both = mm3(ptab[...], transformed)
    rows = []
    for s in range(2):
        part_cos = both[256 * s : 256 * s + 128]
        part_sin = both[256 * s + 128 : 256 * s + 256]
        pair = part_cos + sign * half_swap(part_sin)
        turn = phase[:, 2 * s : 2 * s + 1], phase[:, 2 * s + 1 : 2 * s + 2]
        rows.append(turn[0] * pair + turn[1] * half_swap(pair))
    out[...] = jnp.where(low, rows[0], half_swap(rows[1]))


def mixed_row(columns, weights, wide):
    pieces = [[[None] * KZ for _ in range(2)] for _ in range(2)]
    for s in range(2):
        for k in range(KZ):
            real, imag = columns(s, 0, k), columns(s, 1, k)
            wr, wi = weights[s, 0, k], weights[s, 1, k]
            pieces[s][0][k] = jnp.sum(real * wr - imag * wi, axis=0, keepdims=True)
            pieces[s][1][k] = jnp.sum(real * wi + imag * wr, axis=0, keepdims=True)
    per = 128 // wide
    return [
        jnp.concatenate(pieces[s][part][k : k + per], axis=1)
        for s in range(2)
        for part in range(2)
        for k in range(0, KZ, per)
    ]


def first_mix(arrived, lift_wide, bias_column, weights, out):
    row = jnp.sum(arrived[...], axis=0, keepdims=True)
    source = lax.broadcasted_iota(jnp.int32, (128, 32), 0) // CIN
    pick = (source == lax.broadcasted_iota(jnp.int32, (128, 32), 1)).astype(F32)
    lifted = (
        lax.dot_general(
            lift_wide[...] * row, pick, (((1,), (0,)), ((), ())),
            precision=lax.Precision.HIGHEST, preferred_element_type=F32,
        )
        + bias_column[...]
    )

    def column(s, part, k):
        at = s * 16 + part * 8 + k
        return lifted[:, at : at + 1]

    for t, piece in enumerate(mixed_row(column, weights, C2)):
        out[:, 128 * t : 128 * t + 128] = jnp.broadcast_to(piece, (OWNERS, 128))


def second_mix(arrived, weights, out):
    rows = [
        jnp.sum(arrived[:, 128 * t : 128 * t + 128], axis=0, keepdims=True) for t in range(16)
    ]
    stacked = jnp.concatenate(rows + [jnp.zeros((112, 128), F32)], axis=0).T

    def column(s, part, k):
        at = (s * 2 + part) * 4 + k // 2
        return stacked[(k % 2) * 64 : (k % 2) * 64 + 64, at : at + 1]

    for t, piece in enumerate(mixed_row(column, weights, C1)):
        out[:, 128 * t : 128 * t + 128] = jnp.broadcast_to(piece, (OWNERS, 128))


def coarse_level(
    arrived, inv0, inv1, fwd0, fwd1, lane_phase, row_phase, fields, z_back, z_fwd,
    pool_mix, pool_bias, wide_mix, wide_bias, out, skip, y_s, rhs_s, g_s, t_s,
):
    low = lax.broadcasted_iota(jnp.int32, (16, 128), 1) < 64
    table = inv0[...] * lane_phase[0:1] + inv1[...] * lane_phase[1:2]
    modes = jnp.concatenate([arrived[:, 512 * t : 512 * t + 512] for t in range(4)], axis=0)
    made = mm3(table, modes)
    for t in range(4):
        y_s[t] = made[:, 128 * t : 128 * t + 128]
    for q in range(0, 8, 2):
        for k in range(0, 8, 2):
            first = y_s[k // 2, pl.ds(q, 16, stride=8), :]
            second = y_s[k // 2, pl.ds(q + 1, 16, stride=8), :]
            rhs_s[q // 2, 16 * k : 16 * k + 16] = jnp.where(low, first, half_swap(second))
            rhs_s[q // 2, 16 * k + 16 : 16 * k + 32] = jnp.where(low, half_swap(first), second)
    pool_h, pool_l = split(pool_mix[...])
    wide_h, wide_l = split(wide_mix[...])

    def step(p, carry):
        rows = [rhs_s[t, pl.ds(p, 16, stride=8), :] for t in range(4)]
        high, less = split(jnp.concatenate(rows, axis=1))
        pooled = []
        for ch in range(CIN):
            total = jnp.zeros((8, 128), F32)
            for dx in range(2):
                for dy in range(2):
                    total += fields[ch, 2 * p + dx, pl.ds(dy, 8, stride=2), :]
            pooled.append(total * 0.25)
        pool_t = jnp.concatenate(pooled, axis=0).T
        ph, pll = split(pool_t)
        before = mm(z_back[...], jnp.concatenate([high, less, high], axis=0))
        before += mm(ph, pool_h) + mm(ph, pool_l) + mm(pll, pool_h)
        value = gelu(before + pool_bias[...])
        vh, vl = split(value)
        both = mm(z_fwd[...], vh)
        both = both[:16] + both[16:] + mm(z_fwd[:16], vl)
        for t in range(4):
            at = slice(128 * t, 128 * t + 128)
            wide = mm(vh[:, at], wide_h) + mm(vh[:, at], wide_l) + mm(vl[:, at], wide_h)
            skip[p, :, at] = wide + wide_bias[...]
            g_s[t, pl.ds(pl.multiple_of(p * 16, 16), 16), :] = both[:, at]
        return carry

    lax.fori_loop(0, 8, step, 0)
    for q in range(0, 8, 2):
        for k in range(0, 8, 2):
            first = g_s[q // 2, pl.ds(k, 16, stride=8), :]
            second = g_s[q // 2, pl.ds(k + 1, 16, stride=8), :]
            at = slice(64 * k, 64 * k + 128)
            t_s[16 * q : 16 * q + 16, at] = jnp.where(low, first, half_swap(second))
            t_s[16 * q + 16 : 16 * q + 32, at] = jnp.where(low, half_swap(first), second)
    th, tl = split(t_s[...])
    for t in range(4):
        at = slice(128 * t, 128 * t + 128)
        turn = row_phase[at]
        ah, al = split(fwd0[at] * turn[:, 0:1] + fwd1[at] * turn[:, 1:2])
        out[:, 512 * t : 512 * t + 512] = mm(ah, th) + mm(ah, tl) + mm(al, th)


def fine_level(
    through, constant, arrived, inv0, inv1, lane_phase, fields, z_back, skip, project_wide,
    out, y_s, rhs_s,
):
    modes = jnp.concatenate([arrived[:, 256 * t : 256 * t + 256] for t in range(4)], axis=0)
    mh, ml = split(modes)
    for t in range(4):
        at = slice(128 * t, 128 * t + 128)
        th, tl = split(inv0[at] * lane_phase[0:1] + inv1[at] * lane_phase[1:2])
        made = mm(th, mh) + mm(th, ml) + mm(tl, mh)
        y_s[0, at] = made[:, :128]
        y_s[1, at] = made[:, 128:]
    quarter = lax.broadcasted_iota(jnp.int32, (32, 128), 1) // 32
    for y in range(0, 16, 4):
        for k in range(0, 8, 4):
            rows = [y_s[k // 4, pl.ds(y + u, 32, stride=16), :] for u in range(4)]
            for v in range(4):
                made = rows[v]
                for u in range(4):
                    if u != v:
                        moved = pltpu.roll(rows[u], ((u - v) % 4) * 32, 1)
                        made = jnp.where(quarter == u, moved, made)
                rhs_s[y // 4, 32 * (k + v) : 32 * (k + v) + 32] = made
    jh, jl = split(project_wide[...])

    def step(x, carry):
        rows = [rhs_s[t, pl.ds(x, 16, stride=16), :] for t in range(4)]
        high, less = split(jnp.concatenate(rows, axis=1))
        before = mm(z_back[...], jnp.concatenate([high, less, high], axis=0))
        value = gelu(before + skip[x // 2])
        vh, vl = split(value)
        made = (mm(vh, jh) + mm(vh, jl) + mm(vl, jh)).T
        for o in range(CIN):
            total = made[16 * o : 16 * o + 16] + constant[o]
            for ch in range(CIN):
                total += through[o, ch] * fields[ch, x]
            out[o, x] = total
        return carry

    lax.fori_loop(0, 16, step, 0)


def exchange(tiles):
    return lax.all_to_all(tiles, AXES, split_axis=0, concat_axis=0, tiled=True)


def product(formula, left, right):
    return jnp.einsum(formula, left, right, precision=lax.Precision.HIGHEST)


def on_device(
    fields, lift, lift_bias, spectral_in, bypass_in, bias_in, spectral_out, bypass_out, bias_out,
    project, project_bias,
):
    gx, gy = lax.axis_index("gx"), lax.axis_index("gy")
    fx, fy = mode_frequencies()
    turns = (jnp.asarray(2 * fx, jnp.int32) * gx + jnp.asarray(fy, jnp.int32) * gy) % 16
    angle = turns.astype(F32) * (2.0 * math.pi / 16)
    cos, sin = jnp.cos(angle), jnp.sin(angle)
    first_phase = jnp.stack([cos[0], sin[0], cos[1], sin[1]], axis=1)
    lanes = [jnp.repeat(v[:, None], 2, axis=1).reshape(1, 512) for v in (cos, sin)]
    lane_phase = jnp.concatenate(lanes, axis=0)
    row_phase = lane_phase.T

    eye8 = jnp.eye(8, dtype=F32)
    pool_mix = product("ed,dc->ce", bypass_in, lift)
    pool_mix = (pool_mix[:, None, None, :] * eye8[None, :, :, None]).reshape(32, 512)
    pool_bias = jnp.tile(bias_in + product("ed,d->e", bypass_in, lift_bias), 8)[None]
    same = np.arange(2)[:, None] == (np.arange(4) // 2)[None, :]
    wide_mix = (
        bypass_out.T[None, :, None, :] * jnp.asarray(same, F32)[:, None, :, None]
    ).reshape(128, 128)
    wide_bias = jnp.tile(bias_out, 4)[None]
    eye16 = jnp.eye(16, dtype=F32)
    project_wide = (project.T[None, :, :, None] * eye16[:, None, None, :]).reshape(512, 64)
    through = product("od,dc->oc", project, lift)
    constant = project_bias + product("od,d->o", project, lift_bias)
    at_zero = ((gx == 0) & (gy == 0)).astype(F32) * math.sqrt(TOTAL)
    bias_column = lift_bias[:, None] * (jnp.arange(32) == 0).astype(F32)[None, :] * at_zero
    lift_wide = jnp.tile(lift, (1, 32))

    call = functools.partial(pl.pallas_call, compiler_params=PARAMS)
    spectrum = call(
        first_spectrum,
        out_shape=jax.ShapeDtypeStruct((OWNERS, 128), F32),
        in_specs=[VMEM] * 4, out_specs=VMEM, name="first_spectrum",
    )(fields, first_z_table(), first_places_table(), first_phase)
    mixed = call(
        first_mix,
        out_shape=jax.ShapeDtypeStruct((OWNERS, 2048), F32),
        in_specs=[VMEM] * 4, out_specs=VMEM, name="first_mix",
    )(exchange(spectrum), lift_wide, bias_column, spectral_in)
    half = place_angles(np.arange(8), np.arange(8), NX // 2, NY // 2)
    whole = place_angles(np.arange(16), np.arange(16), NX, NY)
    z_back = inverse_z_table()
    spectrum, skip = call(
        coarse_level,
        out_shape=(
            jax.ShapeDtypeStruct((OWNERS, 2048), F32),
            jax.ShapeDtypeStruct((8, NZ, 512), F32),
        ),
        in_specs=[VMEM] * 14, out_specs=(VMEM, VMEM), name="coarse_level",
        scratch_shapes=[pltpu.VMEM((4, 128, 128), F32)] * 3 + [pltpu.VMEM((128, 512), F32)],
    )(
        exchange(mixed), *inverse_tables(half, BACK),
        *forward_tables(half, 1.0 / math.sqrt(TOTAL / 4.0)), lane_phase, row_phase, fields,
        z_back, forward_z_table(), pool_mix, pool_bias, wide_mix, wide_bias,
    )
    mixed = call(
        second_mix,
        out_shape=jax.ShapeDtypeStruct((OWNERS, 1024), F32),
        in_specs=[VMEM] * 2, out_specs=VMEM, name="second_mix",
    )(exchange(spectrum), spectral_out)
    return call(
        fine_level,
        out_shape=jax.ShapeDtypeStruct((CIN, 16, 16, NZ), F32),
        in_specs=[SMEM] * 2 + [VMEM] * 8, out_specs=VMEM, name="fine_level",
        scratch_shapes=[pltpu.VMEM((2, 512, 128), F32), pltpu.VMEM((4, 256, 128), F32)],
    )(
        through, constant, exchange(mixed), *inverse_tables(whole, BACK), lane_phase, fields,
        z_back, skip, project_wide,
    )


def solution(mesh):
    owned = P(AXES, None, None, None, None)
    grid = P(None, "gx", "gy", None)
    in_specs = (grid, P(), P(), owned, P(), P(), owned, P(), P(), P(), P())
    return jax.shard_map(
        on_device, mesh=mesh, in_specs=in_specs, out_specs=grid, check_vma=False
    )
```

```python
import functools
import math

import jax
import jax.numpy as jnp
import numpy as np
from jax import lax
from jax.experimental import pallas as pl
from jax.experimental.pallas import tpu as pltpu
from jax.sharding import PartitionSpec as P

KX, KY, KZ = 16, 16, 8
NX, NY, NZ = 128, 256, 128
CIN, C1, C2 = 4, 32, 64
AXES = ("gx", "gy")
OWNERS = 128
TOTAL = NX * NY * NZ
BACK = math.sqrt(2.0 / (KX * KY * KZ))
F32 = jnp.float32
BF16 = jnp.bfloat16
VMEM = pl.BlockSpec(memory_space=pltpu.VMEM)
SMEM = pl.BlockSpec(memory_space=pltpu.SMEM)
PARAMS = pltpu.CompilerParams(vmem_limit_bytes=40 << 20)


def mode_frequencies():
    centered = np.where(np.arange(16) < 8, np.arange(16), np.arange(16) - 16)
    n = np.arange(OWNERS)
    fx = np.stack([centered[n // 8]] * 2)
    fy = np.stack([centered[2 * (n % 8) + s] for s in range(2)])
    return fx, fy


def place_angles(xs, ys, x_length, y_length):
    fx, fy = mode_frequencies()
    turns = (
        fx[:, :, None, None] * xs[None, None, :, None] / x_length
        + fy[:, :, None, None] * ys[None, None, None, :] / y_length
    )
    return 2.0 * np.pi * turns


def wave_tables():
    fx, fy = mode_frequencies()
    ahead = np.array([0.0, 0.5 * np.pi])[None, None, :, None]
    places = np.arange(16)[:, None, None, None]
    along_x = 2.0 * np.pi * places * fx[None, :, None, :] / NX + ahead
    along_y = 2.0 * np.pi * places * fy[None, :, None, :] / NY + 0.0 * ahead
    tables = [np.cos(along_x), np.sin(along_x), np.cos(along_y), np.sin(along_y)]
    return np.stack(tables).reshape(4, 16, 512).astype(np.float32)


def phase_steps():
    fx, fy = mode_frequencies()
    steps = np.stack([np.stack([2 * fx, 2 * fx], axis=1), np.stack([fy, fy], axis=1)])
    return steps.reshape(2, 512).astype(np.int32)


def z_angles():
    return 2.0 * np.pi * (np.arange(NZ)[:, None] * np.arange(KZ)[None, :] % NZ) / NZ


def split_np(table):
    high = table.astype(BF16)
    low = (table - high.astype(np.float32)).astype(BF16)
    return high, low


def inverse_z_table():
    table = np.stack([np.cos(z_angles()), -np.sin(z_angles())], axis=2)
    high, low = split_np(table.reshape(NZ, 16).astype(np.float32))
    return np.concatenate([high, high, low], axis=1)


def forward_z_table():
    table = np.stack([np.cos(z_angles()).T, -np.sin(z_angles()).T], axis=0)
    return np.concatenate(split_np(table.reshape(16, NZ).astype(np.float32)), axis=0)


def split(x):
    high = x.astype(BF16)
    return high, (x - high.astype(F32)).astype(BF16)


def mm(a, b, dims=((1,), (0,))):
    return lax.dot_general(a, b, (dims, ((), ())), preferred_element_type=F32)


def mm3(a, b, dims=((1,), (0,))):
    ah, al = split(a)
    bh, bl = split(b)
    return mm(ah, bh, dims) + mm(ah, bl, dims) + mm(al, bh, dims)


def gelu(x):
    return 0.5 * x * (1.0 + lax.erf(x * math.sqrt(0.5)))


def half_swap(x):
    return pltpu.roll(x, 64, 1)


def device_waves(waves, steps, place):
    turns = (steps[0:1] * place[0] + steps[1:2] * place[1]) & 15
    angle = turns.astype(F32) * (2.0 * math.pi / 16)
    cos, sin = jnp.cos(angle), jnp.sin(angle)
    return waves[0] * cos - waves[1] * sin, waves[1] * cos + waves[0] * sin


def wave_rows(along_x, cos_y, sin_y, xs):
    cos_x, sin_x = along_x
    real = [cos_x[x : x + 1] * cos_y - sin_x[x : x + 1] * sin_y for x in xs]
    imag = [sin_x[x : x + 1] * cos_y + cos_x[x : x + 1] * sin_y for x in xs]
    return jnp.concatenate(real, axis=0), jnp.concatenate(imag, axis=0)


def first_spectrum(place, fields, waves, steps, z_fwd, out, fields_v, sems):
    copies = [
        pltpu.make_async_copy(fields.at[ch], fields_v.at[ch], sems.at[ch]) for ch in range(CIN)
    ]
    for copy in copies:
        copy.start()
    along_x = device_waves(waves, steps, place)
    real, imag = wave_rows(along_x, waves[2], waves[3], range(16))
    nt = ((1,), (1,))
    parts = [[], []]
    for ch in range(CIN):
        copies[ch].wait()
        fh, fl = split(fields_v[ch].reshape(256, NZ))
        both = mm(z_fwd[...], fh, nt)
        made = both[:16] + both[16:] + mm(z_fwd[:16], fl, nt)
        parts[0].append(made[:8])
        parts[1].append(made[8:])
    total = mm3(jnp.concatenate(parts[0], axis=0), real)
    total += mm3(jnp.concatenate(parts[1], axis=0), imag)
    total *= 1.0 / math.sqrt(TOTAL)
    tiles = [total[:, 128 * t : 128 * t + 128] for t in range(4)]
    out[...] = jnp.concatenate(tiles, axis=0).T


def mixed_row(columns, weights, wide):
    pieces = [[[None] * KZ for _ in range(2)] for _ in range(2)]
    for s in range(2):
        for k in range(KZ):
            real, imag = columns(s, 0, k), columns(s, 1, k)
            wr, wi = weights[s, 0, k], weights[s, 1, k]
            pieces[s][0][k] = jnp.sum(real * wr - imag * wi, axis=0, keepdims=True)
            pieces[s][1][k] = jnp.sum(real * wi + imag * wr, axis=0, keepdims=True)
    per = 128 // wide
    return [
        jnp.concatenate(pieces[s][part][k : k + per], axis=1)
        for s in range(2)
        for part in range(2)
        for k in range(0, KZ, per)
    ]


def first_mix(arrived, lift_wide, bias_column, weights, out):
    row = jnp.sum(arrived[...], axis=0, keepdims=True)
    source = lax.broadcasted_iota(jnp.int32, (128, 32), 0)
    source = source // 32 * 8 + source % 8
    pick = (source == lax.broadcasted_iota(jnp.int32, (128, 32), 1)).astype(F32)
    lifted = (
        lax.dot_general(
            lift_wide[...] * row, pick, (((1,), (0,)), ((), ())),
            precision=lax.Precision.HIGHEST, preferred_element_type=F32,
        )
        + bias_column[...]
    )

    def column(s, part, k):
        at = s * 16 + part * 8 + k
        return lifted[:, at : at + 1]

    block = jnp.concatenate(mixed_row(column, weights, C2), axis=0)
    for n in range(OWNERS):
        out[n] = block


def second_mix(arrived, weights, out):
    rows = arrived[0]
    for n in range(1, OWNERS):
        rows += arrived[n]
    stacked = jnp.concatenate([rows, jnp.zeros((112, 128), F32)], axis=0).T

    def column(s, part, k):
        at = (s * 2 + part) * 4 + k // 2
        return stacked[(k % 2) * 64 : (k % 2) * 64 + 64, at : at + 1]

    block = jnp.concatenate(mixed_row(column, weights, C1), axis=0)
    for n in range(OWNERS):
        out[n] = block


def coarse_level(
    place, arrived, waves, steps, fields, z_back, z_fwd,
    pool_mix, pool_bias, wide_mix, wide_bias, out, skip, y_s, rhs_s, g_s, t_s,
):
    low = lax.broadcasted_iota(jnp.int32, (16, 128), 1) < 64
    along_x = device_waves(waves, steps, place)
    cos_y = jnp.concatenate([waves[2, 2 * q : 2 * q + 1] for q in range(8)], axis=0)
    sin_y = jnp.concatenate([waves[3, 2 * q : 2 * q + 1] for q in range(8)], axis=0)
    table = jnp.concatenate(wave_rows(along_x, cos_y, sin_y, range(0, 16, 2)), axis=0)
    th, tl = split(table * BACK)
    made = None
    for t in range(4):
        tiles = [arrived[pl.ds(4 * t + u, OWNERS, stride=16), :] for u in range(4)]
        mh, ml = split(jnp.concatenate(tiles, axis=1))
        at = slice(128 * t, 128 * t + 128)
        term = mm(th[:, at], mh) + mm(th[:, at], ml) + mm(tl[:, at], mh)
        made = term if made is None else made + term
    for t in range(4):
        y_s[t] = made[:, 128 * t : 128 * t + 128]
    for q in range(0, 8, 2):
        for k in range(0, 8, 2):
            first = y_s[k // 2, pl.ds(q, 16, stride=8), :]
            second = y_s[k // 2, pl.ds(q + 1, 16, stride=8), :]
            rhs_s[q // 2, 16 * k : 16 * k + 16] = jnp.where(low, first, half_swap(second))
            rhs_s[q // 2, 16 * k + 16 : 16 * k + 32] = jnp.where(low, half_swap(first), second)
    pool_h, pool_l = split(pool_mix[...])
    wide_h, wide_l = split(wide_mix[...])

    def step(p, carry):
        rows = [rhs_s[t, pl.ds(p, 16, stride=8), :] for t in range(4)]
        high, less = split(jnp.concatenate(rows, axis=1))
        pooled = []
        for ch in range(CIN):
            total = jnp.zeros((8, 128), F32)
            for dx in range(2):
                for dy in range(2):
                    total += fields[ch, 2 * p + dx, pl.ds(dy, 8, stride=2), :]
            pooled.append(total * 0.25)
        pool_t = jnp.concatenate(pooled, axis=0).T
        ph, pll = split(pool_t)
        before = mm(z_back[...], jnp.concatenate([high, less, high], axis=0))
        before += mm(ph, pool_h) + mm(ph, pool_l) + mm(pll, pool_h)
        value = gelu(before + pool_bias[...])
        vh, vl = split(value)
        both = mm(z_fwd[...], vh)
        both = both[:16] + both[16:] + mm(z_fwd[:16], vl)
        for t in range(4):
            at = slice(128 * t, 128 * t + 128)
            wide = mm(vh[:, at], wide_h) + mm(vh[:, at], wide_l) + mm(vl[:, at], wide_h)
            skip[p, :, at] = wide + wide_bias[...]
            g_s[t, pl.ds(pl.multiple_of(p * 8, 8), 8), :] = both[:8, at]
            g_s[t, pl.ds(pl.multiple_of(p * 8 + 64, 8), 8), :] = both[8:, at]
        return carry

    lax.fori_loop(0, 8, step, 0)
    for q in range(0, 8, 2):
        for k in range(0, 8, 2):
            first = g_s[q // 2, pl.ds(k, 16, stride=8), :]
            second = g_s[q // 2, pl.ds(k + 1, 16, stride=8), :]
            t_s[k // 2, pl.ds(q, 16, stride=8), :] = jnp.where(low, first, half_swap(second))
            t_s[k // 2, pl.ds(q + 1, 16, stride=8), :] = jnp.where(low, half_swap(first), second)
    scale = 1.0 / math.sqrt(TOTAL / 4.0)
    th, tl = split(jnp.concatenate([t_s[t] for t in range(4)], axis=1) * scale)
    ah, al = split(table.T)
    for t in range(4):
        at = slice(128 * t, 128 * t + 128)
        made = mm(ah[at], th) + mm(ah[at], tl) + mm(al[at], th)
        for u in range(4):
            out[pl.ds(4 * t + u, OWNERS, stride=16), :] = made[:, 128 * u : 128 * u + 128]


def fine_level(
    place, through, constant, arrived, waves, steps, fields, z_back, skip, project_wide,
    out, y_s, rhs_s,
):
    modes = []
    for t in range(4):
        tiles = [arrived[pl.ds(2 * t + u, OWNERS, stride=8), :] for u in range(2)]
        modes.append(jnp.concatenate(tiles, axis=1))
    mh, ml = split(jnp.concatenate(modes, axis=0))
    along_x = device_waves(waves, steps, place)
    along_x = (along_x[0] * BACK, along_x[1] * BACK)
    for x in range(0, 16, 8):
        pair = wave_rows(along_x, waves[2], waves[3], range(x, x + 8))
        for part in range(2):
            th, tl = split(pair[part])
            made = mm(th, mh) + mm(th, ml) + mm(tl, mh)
            at = slice(256 * part + 16 * x, 256 * part + 16 * x + 128)
            y_s[0, at] = made[:, :128]
            y_s[1, at] = made[:, 128:]
    quarter = lax.broadcasted_iota(jnp.int32, (32, 128), 1) // 32
    for y in range(0, 16, 4):
        for k in range(0, 8, 4):
            rows = [y_s[k // 4, pl.ds(y + u, 32, stride=16), :] for u in range(4)]
            for v in range(4):
                made = rows[v]
                for u in range(4):
                    if u != v:
                        moved = pltpu.roll(rows[u], ((u - v) % 4) * 32, 1)
                        made = jnp.where(quarter == u, moved, made)
                rhs_s[y // 4, 32 * (k + v) : 32 * (k + v) + 32] = made
    jh, jl = split(project_wide[...])

    def step(x, carry):
        rows = [rhs_s[t, pl.ds(x, 16, stride=16), :] for t in range(4)]
        high, less = split(jnp.concatenate(rows, axis=1))
        before = mm(z_back[...], jnp.concatenate([high, less, high], axis=0))
        value = gelu(before + skip[x // 2])
        vh, vl = split(value)
        made = (mm(vh, jh) + mm(vh, jl) + mm(vl, jh)).T
        for o in range(CIN):
            total = made[16 * o : 16 * o + 16] + constant[o]
            for ch in range(CIN):
                total += through[o, ch] * fields[ch, x]
            out[o, x] = total
        return carry

    lax.fori_loop(0, 16, step, 0)


def exchange(tiles):
    return lax.all_to_all(tiles, AXES, split_axis=0, concat_axis=0, tiled=True)


def product(formula, left, right):
    return jnp.einsum(formula, left, right, precision=lax.Precision.HIGHEST)


def on_device(
    fields, lift, lift_bias, spectral_in, bypass_in, bias_in, spectral_out, bypass_out, bias_out,
    project, project_bias,
):
    gx, gy = lax.axis_index("gx"), lax.axis_index("gy")
    place = jnp.stack([gx, gy]).astype(jnp.int32)
    waves, steps = wave_tables(), phase_steps()
    z_back, z_fwd = inverse_z_table(), forward_z_table()

    eye8 = jnp.eye(8, dtype=F32)
    pool_mix = product("ed,dc->ce", bypass_in, lift)
    pool_mix = (pool_mix[:, None, None, :] * eye8[None, :, :, None]).reshape(32, 512)
    pool_bias = jnp.tile(bias_in + product("ed,d->e", bypass_in, lift_bias), 8)[None]
    same = np.arange(2)[:, None] == (np.arange(4) // 2)[None, :]
    wide_mix = (
        bypass_out.T[None, :, None, :] * jnp.asarray(same, F32)[:, None, :, None]
    ).reshape(128, 128)
    wide_bias = jnp.tile(bias_out, 4)[None]
    eye16 = jnp.eye(16, dtype=F32)
    project_wide = (project.T[None, :, :, None] * eye16[:, None, None, :]).reshape(512, 64)
    through = product("od,dc->oc", project, lift)
    constant = project_bias + product("od,d->o", project, lift_bias)
    at_zero = ((gx == 0) & (gy == 0)).astype(F32) * math.sqrt(TOTAL)
    bias_column = lift_bias[:, None] * (jnp.arange(32) == 0).astype(F32)[None, :] * at_zero
    lift_wide = jnp.tile(jnp.repeat(lift, KZ, axis=1), (1, 4))

    call = functools.partial(pl.pallas_call, compiler_params=PARAMS)
    spectrum = call(
        first_spectrum,
        out_shape=jax.ShapeDtypeStruct((OWNERS, 128), F32),
        in_specs=[SMEM, pl.BlockSpec(memory_space=pl.ANY)] + [VMEM] * 3, out_specs=VMEM,
        scratch_shapes=[
            pltpu.VMEM((CIN, 16, 16, NZ), F32), pltpu.SemaphoreType.DMA((CIN,)),
        ],
        name="first_spectrum",
    )(place, fields, waves, steps, z_fwd)
    mixed = call(
        first_mix,
        out_shape=jax.ShapeDtypeStruct((OWNERS, 16, 128), F32),
        in_specs=[VMEM] * 4, out_specs=VMEM, name="first_mix",
    )(exchange(spectrum), lift_wide, bias_column, spectral_in)
    spectrum, skip = call(
        coarse_level,
        out_shape=(
            jax.ShapeDtypeStruct((OWNERS * 16, 128), F32),
            jax.ShapeDtypeStruct((8, NZ, 512), F32),
        ),
        in_specs=[SMEM] + [VMEM] * 10, out_specs=(VMEM, VMEM), name="coarse_level",
        scratch_shapes=[pltpu.VMEM((4, 128, 128), F32)] * 4,
    )(
        place, exchange(mixed).reshape(OWNERS * 16, 128), waves, steps, fields,
        z_back, z_fwd, pool_mix, pool_bias, wide_mix, wide_bias,
    )
    mixed = call(
        second_mix,
        out_shape=jax.ShapeDtypeStruct((OWNERS, 8, 128), F32),
        in_specs=[VMEM] * 2, out_specs=VMEM, name="second_mix",
    )(exchange(spectrum.reshape(OWNERS, 16, 128)), spectral_out)
    return call(
        fine_level,
        out_shape=jax.ShapeDtypeStruct((CIN, 16, 16, NZ), F32),
        in_specs=[SMEM] * 3 + [VMEM] * 7, out_specs=VMEM, name="fine_level",
        scratch_shapes=[pltpu.VMEM((2, 512, 128), F32), pltpu.VMEM((4, 256, 128), F32)],
    )(
        place, through, constant, exchange(mixed).reshape(OWNERS * 8, 128), waves, steps,
        fields, z_back, skip, project_wide,
    )


def solution(mesh):
    owned = P(AXES, None, None, None, None)
    grid = P(None, "gx", "gy", None)
    in_specs = (grid, P(), P(), owned, P(), P(), owned, P(), P(), P(), P())
    return jax.shard_map(
        on_device, mesh=mesh, in_specs=in_specs, out_specs=grid, check_vma=False
    )
```

```python
import functools
import math

import jax
import jax.numpy as jnp
import numpy as np
from jax import lax
from jax.experimental import pallas as pl
from jax.experimental.pallas import tpu as pltpu
from jax.sharding import PartitionSpec as P

KX, KY, KZ = 16, 16, 8
NX, NY, NZ = 128, 256, 128
CIN, C1, C2 = 4, 32, 64
AXES = ("gx", "gy")
OWNERS = 128
TOTAL = NX * NY * NZ
BACK = math.sqrt(2.0 / (KX * KY * KZ))
F32 = jnp.float32
BF16 = jnp.bfloat16
UNROLL = 2
VMEM = pl.BlockSpec(memory_space=pltpu.VMEM)
HBM = pl.BlockSpec(memory_space=pltpu.HBM)
PARAMS = pltpu.CompilerParams(vmem_limit_bytes=40 << 20)


def mode_frequencies():
    centered = np.where(np.arange(16) < 8, np.arange(16), np.arange(16) - 16)
    n = np.arange(OWNERS)
    fx = np.stack([centered[n // 8]] * 2)
    fy = np.stack([centered[2 * (n % 8) + s] for s in range(2)])
    return fx, fy


def place_angles(xs, ys, x_length, y_length):
    fx, fy = mode_frequencies()
    turns = (
        fx[:, :, None, None] * xs[None, None, :, None] / x_length
        + fy[:, :, None, None] * ys[None, None, None, :] / y_length
    )
    return 2.0 * np.pi * turns


def wave_tables():
    fx, fy = mode_frequencies()
    ahead = np.array([0.0, 0.5 * np.pi])[None, None, :, None]
    places = np.arange(16)[:, None, None, None]
    along_x = 2.0 * np.pi * places * fx[None, :, None, :] / NX + ahead
    along_y = 2.0 * np.pi * places * fy[None, :, None, :] / NY + 0.0 * ahead
    tables = [np.cos(along_x), np.sin(along_x), np.cos(along_y), np.sin(along_y)]
    return np.stack(tables).reshape(4, 16, 512).astype(np.float32)


def phase_steps():
    fx, fy = mode_frequencies()
    steps = np.stack([np.stack([2 * fx, 2 * fx], axis=1), np.stack([fy, fy], axis=1)])
    return steps.reshape(2, 512).astype(np.int32)


def z_angles():
    return 2.0 * np.pi * (np.arange(NZ)[:, None] * np.arange(KZ)[None, :] % NZ) / NZ


def split_np(table):
    high = table.astype(BF16)
    low = (table - high.astype(np.float32)).astype(BF16)
    return high, low


def inverse_z_table():
    table = np.stack([np.cos(z_angles()), -np.sin(z_angles())], axis=2)
    high, low = split_np(table.reshape(NZ, 16).astype(np.float32))
    return np.concatenate([high.T, high.T, low.T], axis=0)


def forward_z_table():
    table = np.stack([np.cos(z_angles()).T, -np.sin(z_angles()).T], axis=0)
    high, low = split_np(table.reshape(16, NZ).astype(np.float32))
    return np.block([[high, high], [low, np.zeros_like(low)]])


def split(x):
    high = x.astype(BF16)
    return high, (x - high.astype(F32)).astype(BF16)


def mm(a, b, dims=((1,), (0,))):
    return lax.dot_general(a, b, (dims, ((), ())), preferred_element_type=F32)


def mm3(a, b, dims=((1,), (0,))):
    ah, al = split(a)
    bh, bl = split(b)
    return mm(ah, bh, dims) + mm(ah, bl, dims) + mm(al, bh, dims)


def exact(a, b, dims=((1,), (0,))):
    return lax.dot_general(
        a, b, (dims, ((), ())), precision=lax.Precision.HIGHEST, preferred_element_type=F32
    )


def iota(shape, dim):
    return lax.broadcasted_iota(jnp.int32, shape, dim)


def ones_where(condition):
    return jnp.where(condition, 1.0, 0.0).astype(F32)


def gelu(x):
    return 0.5 * x * (1.0 + lax.erf(x * math.sqrt(0.5)))


def regroup(rows):
    group = iota(rows[0].shape, 1) // 32
    made = []
    for v in range(4):
        total = rows[v]
        for u in range(4):
            if u != v:
                moved = pltpu.roll(rows[u], ((u - v) % 4) * 32, 1)
                total = jnp.where(group == u, moved, total)
        made.append(total)
    return made


def my_place():
    return lax.axis_index("gx"), lax.axis_index("gy")


def device_waves(waves, steps, place):
    turns = (steps[0:1] * place[0] + steps[1:2] * place[1]) & 15
    angle = turns.astype(F32) * (2.0 * math.pi / 16)
    cos, sin = jnp.cos(angle), jnp.sin(angle)
    return waves[0] * cos - waves[1] * sin, waves[1] * cos + waves[0] * sin


def wave_rows(along_x, cos_y, sin_y, xs):
    cos_x, sin_x = along_x
    real = [cos_x[x : x + 1] * cos_y - sin_x[x : x + 1] * sin_y for x in xs]
    imag = [sin_x[x : x + 1] * cos_y + cos_x[x : x + 1] * sin_y for x in xs]
    return jnp.concatenate(real, axis=0), jnp.concatenate(imag, axis=0)


def first_spectrum(fields, waves_h, steps_h, z_fwd_h, out, fields_v, waves, steps, z_fwd, sems):
    pairs = [(waves_h, waves), (steps_h, steps), (z_fwd_h, z_fwd)]
    pairs += [(fields.at[ch], fields_v.at[ch]) for ch in range(CIN)]
    copies = [
        pltpu.make_async_copy(source, target, sems.at[i])
        for i, (source, target) in enumerate(pairs)
    ]
    for copy in copies:
        copy.start()
    for copy in copies[:3]:
        copy.wait()
    along_x = device_waves(waves, steps, my_place())
    real, imag = wave_rows(along_x, waves[2], waves[3], range(16))
    nt = ((1,), (1,))
    parts = [[], []]
    for ch in range(CIN):
        copies[3 + ch].wait()
        fh, fl = split(fields_v[ch].reshape(256, NZ))
        made = mm(z_fwd[...], jnp.concatenate([fh, fl], axis=1), nt)
        made = made[:16] + made[16:]
        parts[0].append(made[:8])
        parts[1].append(made[8:])
    total = mm3(jnp.concatenate(parts[0], axis=0), real)
    total += mm3(jnp.concatenate(parts[1], axis=0), imag)
    total *= 1.0 / math.sqrt(TOTAL)
    tiles = [total[:, 128 * t : 128 * t + 128] for t in range(4)]
    out[...] = jnp.concatenate(tiles, axis=0).T


def prepare(
    after, waves, steps, fields, lift, lift_bias, bypass_in, bias_in, bypass_out, bias_out,
    project, project_bias, coarse_t, spread_t, fine_t, pool_mix, pool_bias, wide_mix, wide_bias,
    project_mix, base,
):
    nt = ((1,), (1,))
    gx, gy = my_place()
    own = device_waves(waves, steps, (gx, gy))
    mate = device_waves(waves, steps, (gx + 1 - 2 * (gx % 2), gy))
    cos_y = jnp.concatenate([waves[2, 2 * q : 2 * q + 1] for q in range(8)], axis=0)
    sin_y = jnp.concatenate([waves[3, 2 * q : 2 * q + 1] for q in range(8)], axis=0)
    tables = [
        jnp.concatenate(wave_rows(along, cos_y, sin_y, range(0, 16, 2)), axis=0)
        for along in (own, mate)
    ]
    coarse_t[0], coarse_t[1] = split(tables[0] * BACK)
    scale = 1.0 / math.sqrt(TOTAL / 4.0)
    for patch in range(2):
        at = slice(128 * patch, 128 * patch + 128)
        high, less = split(tables[patch].T * scale)
        spread_t[0, :, at] = high
        spread_t[1, :, at] = less
    scaled = (own[0] * BACK, own[1] * BACK)
    for x in range(0, 16, 8):
        pair = wave_rows(scaled, waves[2], waves[3], range(x, x + 8))
        for part in range(2):
            at = slice(256 * part + 16 * x, 256 * part + 16 * x + 128)
            high, less = split(pair[part])
            fine_t[0, at] = high
            fine_t[1, at] = less

    lanes = [
        ones_where(iota((C2, 128), 0) == 32 * h + iota((C2, 128), 1) % 32) for h in range(2)
    ]
    through = exact(lift[...], bypass_in[...], ((0,), (1,)))
    through = exact(ones_where(iota((32, CIN), 0) // 8 == iota((32, CIN), 1)), through)
    offset = bias_in[...] + exact(lift_bias[...], bypass_in[...], nt)
    for t in range(4):
        at = slice(128 * t, 128 * t + 128)
        same = iota((32, 128), 0) % 8 == 4 * (t // 2) + iota((32, 128), 1) // 32
        high, less = split(jnp.where(same, exact(through, lanes[t % 2]), 0.0))
        pool_mix[:, at] = jnp.concatenate([high, less, high], axis=0)
        pool_bias[:, at] = exact(offset, lanes[t % 2])
    spread_d = ones_where(iota((C1, 256), 0) == iota((C1, 256), 1) % 32)
    same = iota((128, 256), 0) // 32 == iota((128, 256), 1) // 64
    for h in range(2):
        pick = ones_where(iota((128, C2), 1) == 32 * h + iota((128, C2), 0) % 32)
        wide = exact(exact(pick, bypass_out[...], nt), spread_d)
        high, less = split(jnp.where(same, wide, 0.0))
        wide_mix[0, 128 * h : 128 * h + 128] = high
        wide_mix[1, 128 * h : 128 * h + 128] = less
    wide_bias[...] = exact(bias_out[...], spread_d)
    pick = ones_where(iota((512, C1), 1) == iota((512, C1), 0) % 32)
    onto = ones_where(iota((CIN, 128), 0) == iota((CIN, 128), 1) % 64 // 16)
    made = exact(exact(pick, project[...], nt), onto)
    lane = iota((512, 128), 1)
    made = jnp.where(iota((512, 128), 0) // 32 == lane % 16, made, 0.0)
    high = made.astype(BF16).astype(F32)
    project_mix[0] = jnp.where(lane < 64, high, made - high).astype(BF16)
    project_mix[1] = jnp.where(lane < 64, high, 0.0).astype(BF16)
    across = exact(project[...], lift[...])
    constant = project_bias[...] + exact(project[...], lift_bias[...], nt)

    def step(x, carry):
        for o in range(CIN):
            total = jnp.broadcast_to(constant[o : o + 1], (16, NZ))
            for ch in range(CIN):
                total += across[o : o + 1, ch : ch + 1] * fields[ch, x]
            base[o, x] = total
        return carry

    lax.fori_loop(0, 16, step, 0)


def mixed_row(columns, weights, wide):
    pieces = [[[None] * KZ for _ in range(2)] for _ in range(2)]
    for s in range(2):
        for k in range(KZ):
            real, imag = columns(s, 0, k), columns(s, 1, k)
            wr, wi = weights[s, 0, k], weights[s, 1, k]
            pieces[s][0][k] = jnp.sum(real * wr - imag * wi, axis=0, keepdims=True)
            pieces[s][1][k] = jnp.sum(real * wi + imag * wr, axis=0, keepdims=True)
    per = 128 // wide
    return [
        jnp.concatenate(
            [
                jnp.concatenate(
                    [v[:, at : at + wide] for v in pieces[s][part][k : k + per]], axis=1
                )
                for s in range(2)
                for part in range(2)
                for k in range(0, KZ, per)
            ],
            axis=0,
        )
        for at in range(0, weights.shape[-1], wide)
    ]


def first_mix(arrived, lift_wide, bias_column, weights, out):
    row = jnp.sum(arrived[...], axis=0, keepdims=True)
    source = lax.broadcasted_iota(jnp.int32, (128, 32), 0)
    source = source // 32 * 8 + source % 8
    pick = (source == lax.broadcasted_iota(jnp.int32, (128, 32), 1)).astype(F32)
    lifted = (
        lax.dot_general(
            lift_wide[...] * row, pick, (((1,), (0,)), ((), ())),
            precision=lax.Precision.HIGHEST, preferred_element_type=F32,
        )
        + bias_column[...]
    )

    def column(s, part, k):
        at = s * 16 + part * 8 + k
        return lifted[:, at : at + 1]

    halves = mixed_row(column, weights, 32)
    for n in range(OWNERS):
        out[n] = halves[n // 16 % 2]


def second_mix(arrived, weights, out):
    sums = [None, None]
    for n in range(OWNERS):
        half = n // 16 % 2
        sums[half] = arrived[n] if sums[half] is None else sums[half] + arrived[n]
    stacked = jnp.concatenate(sums + [jnp.zeros((112, 128), F32)], axis=0).T

    def column(s, part, k):
        at = (s * 2 + part) * 2 + k // 4
        rows = slice(k % 4 * 32, k % 4 * 32 + 32)
        return jnp.concatenate([stacked[rows, at : at + 1], stacked[rows, at + 8 : at + 9]], axis=0)

    (block,) = mixed_row(column, weights, 32)
    for n in range(OWNERS):
        out[n] = block


def coarse_level(
    mine, other, table, fields, z_back, z_fwd, pool_mix, pool_bias, wide_mix, wide_bias,
    kept, sent, skip, y_s, rhs_s, g_s, t_s, skip_v, sems,
):
    core = lax.axis_index("gx") % 2
    modes = []
    for t in range(4):
        tiles = [
            ref[pl.ds(2 * t + u, OWNERS, stride=8), :] for ref in (mine, other) for u in range(2)
        ]
        modes.append(jnp.concatenate(tiles, axis=1))
    mh, ml = split(jnp.concatenate(modes, axis=0))
    made = mm(table[0], mh) + mm(table[1], mh) + mm(table[0], ml)
    for u in range(2):
        for t in range(2):
            at = 128 * (2 * u + t)
            y_s[2 * ((core + u) % 2) + t] = made[:, at : at + 128]
    for h in range(2):
        for t in range(2):
            for q in range(2):
                made = regroup(
                    [y_s[2 * h + t, pl.ds(4 * q + u, 16, stride=8), :] for u in range(4)]
                )
                for v in range(4):
                    rhs_s[2 * q + h, pl.ds(16 * (4 * t + v), 16), :] = made[v]

    def step(p, carry):
        rows = [rhs_s[t, pl.ds(p, 16, stride=8), :] for t in range(4)]
        high, less = split(jnp.concatenate(rows, axis=1))
        pooled = []
        for ch in range(CIN):
            total = jnp.zeros((8, 128), F32)
            for dx in range(2):
                for dy in range(2):
                    total += fields[ch, 2 * p + dx, pl.ds(dy, 8, stride=2), :]
            pooled.append(total * 0.25)
        ph, pll = split(jnp.concatenate(pooled, axis=0))
        left = jnp.concatenate([z_back[...], ph, ph, pll], axis=0)
        right = jnp.concatenate([high, less, high, pool_mix[...]], axis=0)
        value = gelu(mm(left, right, ((0,), (0,))) + pool_bias[...])
        vh, vl = split(value)
        made = mm(z_fwd[...], jnp.concatenate([vh, vl], axis=0))
        made = made[:16] + made[16:]
        for t in range(4):
            at = slice(128 * t, 128 * t + 128)
            g_s[t, pl.ds(pl.multiple_of(p * 8, 8), 8), :] = made[:8, at]
            g_s[t, pl.ds(pl.multiple_of(p * 8 + 64, 8), 8), :] = made[8:, at]
        for q in range(2):
            at = slice(256 * q, 256 * q + 256)
            wide = mm(vh[:, at], wide_mix[0]) + mm(vh[:, at], wide_mix[1])
            skip_v[p, :, at] = wide + mm(vl[:, at], wide_mix[0]) + wide_bias[...]
        pltpu.make_async_copy(skip_v.at[p], skip.at[p], sems.at[p]).start()
        return carry

    lax.fori_loop(0, 8, step, 0, unroll=UNROLL)
    for h in range(2):
        for t in range(2):
            for q in range(2):
                made = regroup(
                    [g_s[2 * q + h, pl.ds(4 * t + v, 16, stride=8), :] for v in range(4)]
                )
                for u in range(4):
                    t_s[2 * h + t, pl.ds(4 * q + u, 16, stride=8), :] = made[u]
    for t in range(2):
        kept[t] = t_s[2 * core + t]
        sent[t] = t_s[2 * (1 - core) + t]
    for p in range(8):
        pltpu.make_async_copy(skip_v.at[p], skip.at[p], sems.at[p]).wait()


def spread(kept, got, table, out):
    rows = [jnp.concatenate([ref[0], ref[1]], axis=1) for ref in (kept, got)]
    th, tl = split(jnp.concatenate(rows, axis=0))
    for t in range(4):
        at = slice(128 * t, 128 * t + 128)
        made = mm(table[0, at], th) + mm(table[0, at], tl) + mm(table[1, at], th)
        for u in range(2):
            out[pl.ds(2 * t + u, OWNERS, stride=8), :] = made[:, 128 * u : 128 * u + 128]


def fine_level(
    arrived, table, z_back_h, skip, project_mix, base, out, y_s, rhs_s, skip_v, z_back, sems,
):
    copies = [pltpu.make_async_copy(skip.at[p], skip_v.at[p], sems.at[p]) for p in range(8)]
    copies.append(pltpu.make_async_copy(z_back_h, z_back, sems.at[8]))
    for copy in copies:
        copy.start()
    modes = []
    for t in range(4):
        tiles = [arrived[pl.ds(2 * t + u, OWNERS, stride=8), :] for u in range(2)]
        modes.append(jnp.concatenate(tiles, axis=1))
    mh, ml = split(jnp.concatenate(modes, axis=0))
    for t in range(4):
        at = slice(128 * t, 128 * t + 128)
        made = mm(table[0, at], mh) + mm(table[0, at], ml) + mm(table[1, at], mh)
        y_s[0, at] = made[:, :128]
        y_s[1, at] = made[:, 128:]
    for t in range(2):
        for y in range(4):
            made = regroup([y_s[t, pl.ds(4 * y + u, 32, stride=16), :] for u in range(4)])
            for v in range(4):
                rhs_s[y, pl.ds(32 * (4 * t + v), 32), :] = made[v]
    for copy in copies:
        copy.wait()

    def step(x, carry):
        rows = [rhs_s[t, pl.ds(x, 16, stride=16), :] for t in range(4)]
        high, less = split(jnp.concatenate(rows, axis=1))
        before = mm(z_back[...], jnp.concatenate([high, less, high], axis=0), ((0,), (0,)))
        vh, vl = split(gelu(before + skip_v[x // 2]))
        made = (mm(vh, project_mix[0]) + mm(vl, project_mix[1])).T
        made = made[:64] + made[64:]
        for o in range(CIN):
            out[o, x] = made[16 * o : 16 * o + 16] + base[o, x]
        return carry

    lax.fori_loop(0, 16, step, 0, unroll=UNROLL)


def exchange(tiles):
    return lax.all_to_all(tiles, AXES, split_axis=0, concat_axis=0, tiled=True)


def between_cores(array):
    return lax.ppermute(array, "gx", [(i, i ^ 1) for i in range(lax.axis_size("gx"))])


def on_device(
    fields, lift, lift_bias, spectral_in, bypass_in, bias_in, spectral_out, bypass_out, bias_out,
    project, project_bias,
):
    gx, gy = lax.axis_index("gx"), lax.axis_index("gy")
    waves, steps = wave_tables(), phase_steps()
    z_back, z_fwd = inverse_z_table(), forward_z_table()
    at_zero = ((gx == 0) & (gy == 0)).astype(F32) * math.sqrt(TOTAL)
    bias_column = lift_bias[:, None] * (jnp.arange(32) == 0).astype(F32)[None, :] * at_zero
    lift_wide = jnp.tile(jnp.repeat(lift, KZ, axis=1), (1, 4))

    call = functools.partial(pl.pallas_call, compiler_params=PARAMS)
    shape = jax.ShapeDtypeStruct
    dma = pltpu.SemaphoreType.DMA
    spectrum = call(
        first_spectrum,
        out_shape=shape((OWNERS, 128), F32),
        in_specs=[HBM] * 4, out_specs=VMEM,
        scratch_shapes=[
            pltpu.VMEM((CIN, 16, 16, NZ), F32), pltpu.VMEM((4, 16, 512), F32),
            pltpu.VMEM((2, 512), jnp.int32), pltpu.VMEM((32, 2 * NZ), BF16), dma((7,)),
        ],
        name="first_spectrum",
    )(fields, waves, steps, z_fwd)
    mixed = call(
        first_mix,
        out_shape=shape((OWNERS, 8, 128), F32),
        in_specs=[VMEM] * 4, out_specs=VMEM, name="first_mix",
    )(exchange(spectrum), lift_wide, bias_column, spectral_in)
    prepared = call(
        prepare,
        out_shape=(
            shape((2, 128, 512), BF16), shape((2, 512, 256), BF16), shape((2, 512, 512), BF16),
            shape((96, 512), BF16), shape((1, 512), F32), shape((2, 256, 256), BF16),
            shape((1, 256), F32), shape((2, 512, 128), BF16), shape((CIN, 16, 16, NZ), F32),
        ),
        in_specs=[HBM] + [VMEM] * 11, out_specs=(VMEM,) * 9, name="prepare",
        cost_estimate=pl.CostEstimate(
            flops=1 << 31, transcendentals=0, bytes_accessed=6 << 20
        ),
    )(
        mixed, waves, steps, fields, lift, lift_bias[None], bypass_in, bias_in[None], bypass_out,
        bias_out[None], project, project_bias[:, None],
    )
    coarse_t, spread_t, fine_t, pool_mix, pool_bias, wide_mix, wide_bias, project_mix, base = (
        prepared
    )
    mine = exchange(mixed)
    kept, sent, skip = call(
        coarse_level,
        out_shape=(
            shape((2, 128, 128), F32), shape((2, 128, 128), F32), shape((8, NZ, 512), F32),
        ),
        in_specs=[VMEM] * 10, out_specs=(VMEM, VMEM, HBM), name="coarse_level",
        scratch_shapes=[pltpu.VMEM((4, 128, 128), F32)] * 4
        + [pltpu.VMEM((8, NZ, 512), F32), dma((8,))],
    )(
        mine.reshape(OWNERS * 8, 128), between_cores(mine).reshape(OWNERS * 8, 128), coarse_t,
        fields, z_back, z_fwd, pool_mix, pool_bias, wide_mix, wide_bias,
    )
    spectrum = call(
        spread,
        out_shape=shape((OWNERS * 8, 128), F32),
        in_specs=[VMEM] * 3, out_specs=VMEM, name="spread",
    )(kept, between_cores(sent), spread_t)
    mixed = call(
        second_mix,
        out_shape=shape((OWNERS, 8, 128), F32),
        in_specs=[VMEM] * 2, out_specs=VMEM, name="second_mix",
    )(exchange(spectrum.reshape(OWNERS, 8, 128)), spectral_out)
    return call(
        fine_level,
        out_shape=shape((CIN, 16, 16, NZ), F32),
        in_specs=[VMEM, VMEM, HBM, HBM, VMEM, VMEM], out_specs=VMEM, name="fine_level",
        scratch_shapes=[
            pltpu.VMEM((2, 512, 128), F32), pltpu.VMEM((4, 256, 128), F32),
            pltpu.VMEM((8, NZ, 512), F32), pltpu.VMEM((48, NZ), BF16), dma((9,)),
        ],
    )(exchange(mixed).reshape(OWNERS * 8, 128), fine_t, z_back, skip, project_mix, base)


def solution(mesh):
    owned = P(AXES, None, None, None, None)
    grid = P(None, "gx", "gy", None)
    in_specs = (grid, P(), P(), owned, P(), P(), owned, P(), P(), P(), P())
    return jax.shard_map(
        on_device, mesh=mesh, in_specs=in_specs, out_specs=grid, check_vma=False
    )
```

```python
import functools
import math

import jax
import jax.numpy as jnp
import numpy as np
from jax import lax
from jax.experimental import pallas as pl
from jax.experimental.pallas import tpu as pltpu
from jax.sharding import PartitionSpec as P

KX, KY, KZ = 16, 16, 8
NX, NY, NZ = 128, 256, 128
CIN, C1, C2 = 4, 32, 64
AXES = ("gx", "gy")
OWNERS = 128
TOTAL = NX * NY * NZ
BACK = math.sqrt(2.0 / (KX * KY * KZ))
F32 = jnp.float32
BF16 = jnp.bfloat16
UNROLL = 2
VMEM = pl.BlockSpec(memory_space=pltpu.VMEM)
HBM = pl.BlockSpec(memory_space=pltpu.HBM)
PARAMS = pltpu.CompilerParams(vmem_limit_bytes=16 << 20)
ALONE = pltpu.CompilerParams(vmem_limit_bytes=60 << 20)


def mode_frequencies():
    centered = np.where(np.arange(16) < 8, np.arange(16), np.arange(16) - 16)
    n = np.arange(OWNERS)
    fx = np.stack([centered[n // 8]] * 2)
    fy = np.stack([centered[2 * (n % 8) + s] for s in range(2)])
    return fx, fy


def place_angles(xs, ys, x_length, y_length):
    fx, fy = mode_frequencies()
    turns = (
        fx[:, :, None, None] * xs[None, None, :, None] / x_length
        + fy[:, :, None, None] * ys[None, None, None, :] / y_length
    )
    return 2.0 * np.pi * turns


def wave_tables():
    fx, fy = mode_frequencies()
    ahead = np.array([0.0, 0.5 * np.pi])[None, None, :, None]
    places = np.arange(16)[:, None, None, None]
    along_x = 2.0 * np.pi * places * fx[None, :, None, :] / NX + ahead
    along_y = 2.0 * np.pi * places * fy[None, :, None, :] / NY + 0.0 * ahead
    tables = [np.cos(along_x), np.sin(along_x), np.cos(along_y), np.sin(along_y)]
    return np.stack(tables).reshape(4, 16, 512).astype(np.float32)


def phase_steps():
    fx, fy = mode_frequencies()
    steps = np.stack([np.stack([2 * fx, 2 * fx], axis=1), np.stack([fy, fy], axis=1)])
    return steps.reshape(2, 512).astype(np.int32)


def z_angles():
    return 2.0 * np.pi * (np.arange(NZ)[:, None] * np.arange(KZ)[None, :] % NZ) / NZ


def split_np(table):
    high = table.astype(BF16)
    low = (table - high.astype(np.float32)).astype(BF16)
    return high, low


def first_z_table():
    c, s = np.cos(z_angles()), np.sin(z_angles())
    parts = np.array([[c, -s], [-s, -c]])
    table = np.zeros((CIN, NZ, 2, 2, KZ, CIN))
    for ch in range(CIN):
        table[ch, :, :, :, :, ch] = parts.transpose(2, 0, 1, 3)
    high, low = split_np(table.reshape(CIN, NZ, 128).astype(np.float32))
    return np.concatenate([high, high, low], axis=1)


def first_places_table():
    fx, fy = mode_frequencies()
    places = np.arange(16)
    turns = (
        fx[:, :, None, None] * places[:, None] / NX + fy[:, :, None, None] * places[None, :] / NY
    )
    angles = 2.0 * np.pi * turns
    table = np.stack([np.cos(angles), np.sin(angles)], axis=1) / math.sqrt(TOTAL)
    return np.stack(split_np(table.reshape(512, 256).astype(np.float32)))


def inverse_z_table():
    table = np.stack([np.cos(z_angles()), -np.sin(z_angles())], axis=2)
    high, low = split_np(table.reshape(NZ, 16).astype(np.float32))
    ones = np.zeros((16, NZ), BF16)
    ones[:3] = 1.0
    return np.concatenate([high.T, high.T, low.T, ones], axis=0)


def forward_z_table():
    table = np.stack([np.cos(z_angles()).T, -np.sin(z_angles()).T], axis=0)
    high, low = split_np(table.reshape(16, NZ).astype(np.float32))
    return np.block([[high, high], [low, np.zeros_like(low)]])


def split(x):
    high = x.astype(BF16)
    return high, (x - high.astype(F32)).astype(BF16)


def bias_rows(bias):
    high, less = split(bias)
    least = (bias - high.astype(F32) - less.astype(F32)).astype(BF16)
    row = iota((16, bias.shape[1]), 0)
    rows = [v.astype(F32) for v in (high, less, least)]
    total = jnp.where(row == 0, rows[0], jnp.where(row == 1, rows[1], rows[2]))
    return jnp.where(row < 3, total, 0.0).astype(BF16)


def mm(a, b, dims=((1,), (0,))):
    return lax.dot_general(a, b, (dims, ((), ())), preferred_element_type=F32)


def mm3(a, b, dims=((1,), (0,))):
    ah, al = split(a)
    bh, bl = split(b)
    return mm(ah, bh, dims) + mm(ah, bl, dims) + mm(al, bh, dims)


def exact(a, b, dims=((1,), (0,))):
    return lax.dot_general(
        a, b, (dims, ((), ())), precision=lax.Precision.HIGHEST, preferred_element_type=F32
    )


def iota(shape, dim):
    return lax.broadcasted_iota(jnp.int32, shape, dim)


def ones_where(condition):
    return jnp.where(condition, 1.0, 0.0).astype(F32)


def gelu(x):
    return 0.5 * x * (1.0 + lax.erf(x * math.sqrt(0.5)))


def regroup(rows):
    group = iota(rows[0].shape, 1) // 32
    made = []
    for v in range(4):
        total = rows[v]
        for u in range(4):
            if u != v:
                moved = pltpu.roll(rows[u], ((u - v) % 4) * 32, 1)
                total = jnp.where(group == u, moved, total)
        made.append(total)
    return made


def my_place():
    return lax.axis_index("gx"), lax.axis_index("gy")


def phases(steps, place):
    turns = (steps[0:1] * place[0] + steps[1:2] * place[1]) & 15
    angle = turns.astype(F32) * (2.0 * math.pi / 16)
    return jnp.cos(angle), jnp.sin(angle)


def device_waves(waves, steps, place):
    cos, sin = phases(steps, place)
    return waves[0] * cos - waves[1] * sin, waves[1] * cos + waves[0] * sin


def wave_rows(along_x, cos_y, sin_y, xs):
    cos_x, sin_x = along_x
    real = [cos_x[x : x + 1] * cos_y - sin_x[x : x + 1] * sin_y for x in xs]
    imag = [sin_x[x : x + 1] * cos_y + cos_x[x : x + 1] * sin_y for x in xs]
    return jnp.concatenate(real, axis=0), jnp.concatenate(imag, axis=0)


def first_spectrum(
    fields, ztab_h, ptab_h, steps_h, out, fields_v, ztab, ptab, steps, sems,
):
    pairs = [(steps_h, steps)]
    for ch in range(CIN):
        pairs += [(fields.at[ch], fields_v.at[ch]), (ztab_h.at[ch], ztab.at[ch])]
    pairs.append((ptab_h, ptab))
    copies = [
        pltpu.make_async_copy(source, target, sems.at[i])
        for i, (source, target) in enumerate(pairs)
    ]
    for copy in copies:
        copy.start()
    copies[0].wait()
    cos, sin = phases(steps, my_place())
    turn = [v[:, at : at + 128] for at in (0, 256) for v in (cos, sin)]
    turn = jnp.concatenate(turn + [jnp.zeros((124, 128), F32)], axis=0).T
    total = None
    for ch in range(CIN):
        copies[1 + 2 * ch].wait()
        copies[2 + 2 * ch].wait()
        fh, fl = split(fields_v[ch].reshape(256, NZ))
        term = mm(jnp.concatenate([fh, fl], axis=1), ztab[ch, :256]) + mm(fh, ztab[ch, 256:])
        total = term if total is None else total + term
    copies[-1].wait()
    th, tl = split(total)
    both = mm(ptab[0], th) + mm(ptab[0], tl) + mm(ptab[1], th)
    low = iota((128, 128), 1) < 64
    rows = []
    for s in range(2):
        part_cos = both[256 * s : 256 * s + 128]
        part_sin = both[256 * s + 128 : 256 * s + 256]
        part_sin = pltpu.roll(part_sin, 64, 1)
        pair = jnp.where(low, part_cos + part_sin, part_cos - part_sin)
        cos_s, sin_s = turn[:, 2 * s : 2 * s + 1], turn[:, 2 * s + 1 : 2 * s + 2]
        rows.append(cos_s * pair + sin_s * pltpu.roll(pair, 64, 1))
    out[...] = jnp.where(low, rows[0], pltpu.roll(rows[1], 64, 1))


def prepare_mix(after, weights, lift, lift_bias, weights_v, lift_wide, bias_column, sem):
    copy = pltpu.make_async_copy(weights, weights_v, sem)
    copy.start()
    lift_wide[...] = exact(lift[...], ones_where(iota((CIN, 128), 0) == iota((CIN, 128), 1) % 4))
    gx, gy = my_place()
    at_zero = (iota((C1, 32), 1) + gx + gy) == 0
    bias_column[...] = jnp.where(at_zero, lift_bias[...] * math.sqrt(TOTAL), 0.0)
    copy.wait()


def prepare_coarse(
    after, waves, steps, lift, lift_bias, bypass_in, bias_in, bypass_out, spread_t, pack,
):
    nt = ((1,), (1,))
    gx, gy = my_place()
    own = device_waves(waves, steps, (gx, gy))
    mate = device_waves(waves, steps, (gx + 1 - 2 * (gx % 2), gy))
    cos_y = jnp.concatenate([waves[2, 2 * q : 2 * q + 1] for q in range(8)], axis=0)
    sin_y = jnp.concatenate([waves[3, 2 * q : 2 * q + 1] for q in range(8)], axis=0)
    tables = [
        jnp.concatenate(wave_rows(along, cos_y, sin_y, range(0, 16, 2)), axis=0)
        for along in (own, mate)
    ]
    pack[0:128], pack[128:256] = split(tables[0] * BACK)
    scale = 1.0 / math.sqrt(TOTAL / 4.0)
    for patch in range(2):
        at = slice(128 * patch, 128 * patch + 128)
        high, less = split(tables[patch].T * scale)
        spread_t[0, :, at] = high
        spread_t[1, :, at] = less
    lanes = [
        ones_where(iota((C2, 128), 0) == 32 * h + iota((C2, 128), 1) % 32) for h in range(2)
    ]
    through = exact(lift[...], bypass_in[...], ((0,), (1,)))
    through = exact(ones_where(iota((32, CIN), 0) // 8 == iota((32, CIN), 1)), through)
    offset = bias_in[...] + exact(lift_bias[...], bypass_in[...], nt)
    for t in range(4):
        at = slice(128 * t, 128 * t + 128)
        same = iota((32, 128), 0) % 8 == 4 * (t // 2) + iota((32, 128), 1) // 32
        high, less = split(jnp.where(same, exact(through, lanes[t % 2]), 0.0))
        rows = bias_rows(exact(offset, lanes[t % 2]))
        pack[256:368, at] = jnp.concatenate([rows, high, less, high], axis=0)
    spread_d = ones_where(iota((C1, 256), 0) == iota((C1, 256), 1) % 32)
    same = iota((128, 256), 0) // 32 == iota((128, 256), 1) // 64
    for h in range(2):
        pick = ones_where(iota((128, C2), 1) == 32 * h + iota((128, C2), 0) % 32)
        wide = exact(exact(pick, bypass_out[...], nt), spread_d)
        high, less = split(jnp.where(same, wide, 0.0))
        pack[368 + 128 * h : 496 + 128 * h] = jnp.concatenate([high, less], axis=1)


def prepare_fine(
    after, waves, steps, fields, lift, lift_bias, bias_out, project, project_bias,
    fine_t, project_mix, bias_mix, base,
):
    nt = ((1,), (1,))
    own = device_waves(waves, steps, my_place())
    scaled = (own[0] * BACK, own[1] * BACK)
    for x in range(0, 16, 8):
        pair = wave_rows(scaled, waves[2], waves[3], range(x, x + 8))
        for part in range(2):
            at = slice(256 * part + 16 * x, 256 * part + 16 * x + 128)
            high, less = split(pair[part])
            fine_t[0, at] = high
            fine_t[1, at] = less
    lanes = ones_where(iota((C1, 512), 0) == iota((C1, 512), 1) % 32)
    bias_mix[...] = bias_rows(exact(bias_out[...], lanes))
    pick = ones_where(iota((512, C1), 1) == iota((512, C1), 0) % 32)
    onto = ones_where(iota((CIN, 128), 0) == iota((CIN, 128), 1) % 64 // 16)
    made = exact(exact(pick, project[...], nt), onto)
    lane = iota((512, 128), 1)
    made = jnp.where(iota((512, 128), 0) // 32 == lane % 16, made, 0.0)
    high = made.astype(BF16).astype(F32)
    project_mix[0] = jnp.where(lane < 64, high, made - high).astype(BF16)
    project_mix[1] = jnp.where(lane < 64, high, 0.0).astype(BF16)
    across = exact(project[...], lift[...])
    constant = project_bias[...] + exact(project[...], lift_bias[...], nt)

    def step(x, carry):
        for o in range(CIN):
            total = jnp.broadcast_to(constant[o : o + 1], (16, NZ))
            for ch in range(CIN):
                total += across[o : o + 1, ch : ch + 1] * fields[ch, x]
            base[o, x] = total
        return carry

    lax.fori_loop(0, 16, step, 0)


def mixed_row(columns, weights, wide):
    pieces = [[[None] * KZ for _ in range(2)] for _ in range(2)]
    for s in range(2):
        for k in range(KZ):
            real, imag = columns(s, 0, k), columns(s, 1, k)
            wr, wi = weights[s, 0, k], weights[s, 1, k]
            pieces[s][0][k] = jnp.sum(real * wr - imag * wi, axis=0, keepdims=True)
            pieces[s][1][k] = jnp.sum(real * wi + imag * wr, axis=0, keepdims=True)
    per = 128 // wide
    return [
        jnp.concatenate(
            [
                jnp.concatenate(
                    [v[:, at : at + wide] for v in pieces[s][part][k : k + per]], axis=1
                )
                for s in range(2)
                for part in range(2)
                for k in range(0, KZ, per)
            ],
            axis=0,
        )
        for at in range(0, weights.shape[-1], wide)
    ]


def first_mix(arrived, lift_wide, bias_column, weights, out):
    row = jnp.sum(arrived[...], axis=0, keepdims=True)
    source = lax.broadcasted_iota(jnp.int32, (128, 32), 0) // CIN
    pick = (source == lax.broadcasted_iota(jnp.int32, (128, 32), 1)).astype(F32)
    lifted = (
        lax.dot_general(
            lift_wide[...] * row, pick, (((1,), (0,)), ((), ())),
            precision=lax.Precision.HIGHEST, preferred_element_type=F32,
        )
        + bias_column[...]
    )

    def column(s, part, k):
        at = s * 16 + part * 8 + k
        return lifted[:, at : at + 1]

    halves = mixed_row(column, weights, 32)
    for n in range(OWNERS):
        out[n] = halves[n // 16 % 2]


def second_mix(arrived_h, weights, out, arrived, sems):
    copies = [
        pltpu.make_async_copy(
            arrived_h.at[pl.ds(32 * i, 32)], arrived.at[pl.ds(32 * i, 32)], sems.at[i]
        )
        for i in range(4)
    ]
    for copy in copies:
        copy.start()
    sums = [None, None]
    for n in range(OWNERS):
        if n % 32 == 0:
            copies[n // 32].wait()
        half = n // 16 % 2
        sums[half] = arrived[n] if sums[half] is None else sums[half] + arrived[n]
    stacked = jnp.concatenate(sums + [jnp.zeros((112, 128), F32)], axis=0).T

    def column(s, part, k):
        at = (s * 2 + part) * 2 + k // 4
        rows = slice(k % 4 * 32, k % 4 * 32 + 32)
        return jnp.concatenate([stacked[rows, at : at + 1], stacked[rows, at + 8 : at + 9]], axis=0)

    (block,) = mixed_row(column, weights, 32)
    for n in range(OWNERS):
        out[n] = block


def coarse_level(
    mine, other, pack, fields, z_back, z_fwd,
    kept, sent, skip, y_s, rhs_s, g_s, t_s, skip_v, sems,
):
    core = lax.axis_index("gx") % 2
    modes = []
    for t in range(4):
        tiles = [
            ref[pl.ds(2 * t + u, OWNERS, stride=8), :] for ref in (mine, other) for u in range(2)
        ]
        modes.append(jnp.concatenate(tiles, axis=1))
    mh, ml = split(jnp.concatenate(modes, axis=0))
    th, tl = pack[0:128], pack[128:256]
    made = mm(th, mh) + mm(tl, mh) + mm(th, ml)
    for u in range(2):
        for t in range(2):
            at = 128 * (2 * u + t)
            y_s[2 * ((core + u) % 2) + t] = made[:, at : at + 128]
    for h in range(2):
        for t in range(2):
            for q in range(2):
                made = regroup(
                    [y_s[2 * h + t, pl.ds(4 * q + u, 16, stride=8), :] for u in range(4)]
                )
                for v in range(4):
                    rhs_s[2 * q + h, pl.ds(16 * (4 * t + v), 16), :] = made[v]

    def step(p, carry):
        rows = [rhs_s[t, pl.ds(p, 16, stride=8), :] for t in range(4)]
        high, less = split(jnp.concatenate(rows, axis=1))
        pooled = []
        for ch in range(CIN):
            total = jnp.zeros((8, 128), F32)
            for dx in range(2):
                for dy in range(2):
                    total += fields[ch, 2 * p + dx, pl.ds(dy, 8, stride=2), :]
            pooled.append(total * 0.25)
        ph, pll = split(jnp.concatenate(pooled, axis=0))
        left = jnp.concatenate([z_back[...], ph, ph, pll], axis=0)
        right = jnp.concatenate([high, less, high, pack[256:368]], axis=0)
        value = gelu(mm(left, right, ((0,), (0,))))
        vh, vl = split(value)
        made = mm(z_fwd[...], jnp.concatenate([vh, vl], axis=0))
        made = made[:16] + made[16:]
        for t in range(4):
            at = slice(128 * t, 128 * t + 128)
            g_s[t, pl.ds(pl.multiple_of(p * 8, 8), 8), :] = made[:8, at]
            g_s[t, pl.ds(pl.multiple_of(p * 8 + 64, 8), 8), :] = made[8:, at]
        for q in range(2):
            at = slice(256 * q, 256 * q + 256)
            wide = mm(vh[:, at], pack[368:624, 0:256]) + mm(vh[:, at], pack[368:624, 256:512])
            skip_v[p, :, at] = wide + mm(vl[:, at], pack[368:624, 0:256])
        pltpu.make_async_copy(skip_v.at[p], skip.at[p], sems.at[p]).start()
        return carry

    lax.fori_loop(0, 8, step, 0, unroll=UNROLL)
    for h in range(2):
        for t in range(2):
            for q in range(2):
                made = regroup(
                    [g_s[2 * q + h, pl.ds(4 * t + v, 16, stride=8), :] for v in range(4)]
                )
                for u in range(4):
                    t_s[2 * h + t, pl.ds(4 * q + u, 16, stride=8), :] = made[u]
    for t in range(2):
        kept[t] = t_s[2 * core + t]
        sent[t] = t_s[2 * (1 - core) + t]
    for p in range(8):
        pltpu.make_async_copy(skip_v.at[p], skip.at[p], sems.at[p]).wait()


def spread(kept, got, table, out):
    rows = [jnp.concatenate([ref[0], ref[1]], axis=1) for ref in (kept, got)]
    th, tl = split(jnp.concatenate(rows, axis=0))
    for t in range(4):
        at = slice(128 * t, 128 * t + 128)
        made = mm(table[0, at], th) + mm(table[0, at], tl) + mm(table[1, at], th)
        for u in range(2):
            out[pl.ds(2 * t + u, OWNERS, stride=8), :] = made[:, 128 * u : 128 * u + 128]


def fine_level(
    arrived, table, z_back_h, skip, project_mix, bias_mix, base_h, out, base,
    y_s, rhs_s, skip_v, z_back, sems,):
    copies = [pltpu.make_async_copy(skip.at[p], skip_v.at[p], sems.at[p]) for p in range(8)]
    copies.append(pltpu.make_async_copy(z_back_h, z_back, sems.at[8]))
    copies.append(pltpu.make_async_copy(base_h, base, sems.at[9]))
    for copy in copies:
        copy.start()
    modes = []
    for t in range(4):
        tiles = [arrived[pl.ds(2 * t + u, OWNERS, stride=8), :] for u in range(2)]
        modes.append(jnp.concatenate(tiles, axis=1))
    mh, ml = split(jnp.concatenate(modes, axis=0))
    for t in range(4):
        at = slice(128 * t, 128 * t + 128)
        made = mm(table[0, at], mh) + mm(table[0, at], ml) + mm(table[1, at], mh)
        y_s[0, at] = made[:, :128]
        y_s[1, at] = made[:, 128:]
    for t in range(2):
        for y in range(4):
            made = regroup([y_s[t, pl.ds(4 * y + u, 32, stride=16), :] for u in range(4)])
            for v in range(4):
                rhs_s[y, pl.ds(32 * (4 * t + v), 32), :] = made[v]
    for copy in copies:
        copy.wait()

    def step(x, carry):
        rows = [rhs_s[t, pl.ds(x, 16, stride=16), :] for t in range(4)]
        high, less = split(jnp.concatenate(rows, axis=1))
        right = jnp.concatenate([high, less, high, bias_mix[...]], axis=0)
        before = mm(z_back[...], right, ((0,), (0,)))
        vh, vl = split(gelu(before + skip_v[x // 2]))
        made = (mm(vh, project_mix[0]) + mm(vl, project_mix[1])).T
        made = made[:64] + made[64:]
        for o in range(CIN):
            out[o, x] = made[16 * o : 16 * o + 16] + base[o, x]
        return carry

    lax.fori_loop(0, 16, step, 0, unroll=UNROLL)


def exchange(tiles):
    return lax.all_to_all(tiles, AXES, split_axis=0, concat_axis=0, tiled=True)


def between_cores(array):
    return lax.ppermute(array, "gx", [(i, i ^ 1) for i in range(lax.axis_size("gx"))])


def stay(array):
    return pltpu.with_memory_space_constraint(array, pltpu.HBM)


def on_device(
    fields, lift, lift_bias, spectral_in, bypass_in, bias_in, spectral_out, bypass_out, bias_out,
    project, project_bias,
):
    waves, steps = wave_tables(), phase_steps()
    z_back, z_fwd = inverse_z_table(), forward_z_table()
    call = functools.partial(pl.pallas_call, compiler_params=PARAMS)
    shape = jax.ShapeDtypeStruct
    dma = pltpu.SemaphoreType.DMA
    work = pl.CostEstimate(flops=1 << 31, transcendentals=0, bytes_accessed=6 << 20)
    spectrum = pl.pallas_call(
        first_spectrum,
        out_shape=shape((OWNERS, 128), F32),
        in_specs=[HBM] * 4, out_specs=VMEM,
        scratch_shapes=[
            pltpu.VMEM((CIN, 16, 16, NZ), F32), pltpu.VMEM((CIN, 384, 128), BF16),
            pltpu.VMEM((2, 512, 256), BF16), pltpu.VMEM((2, 512), jnp.int32), dma((10,)),
        ],
        name="first_spectrum", compiler_params=ALONE,
    )(fields, first_z_table(), first_places_table(), steps)
    prepared = call(
        prepare_mix,
        out_shape=(
            shape((2, 2, KZ, C1, C2), F32), shape((C1, 128), F32), shape((C1, 32), F32),
        ),
        in_specs=[HBM] * 2 + [VMEM] * 2, out_specs=(VMEM,) * 3, name="prepare_mix",
        scratch_shapes=[dma(())], cost_estimate=work,
    )(spectrum, spectral_in, lift, lift_bias[:, None])
    arrived, prepared = lax.optimization_barrier((exchange(spectrum), prepared))
    weights, lift_wide, bias_column = prepared
    mixed = call(
        first_mix,
        out_shape=shape((OWNERS, 8, 128), F32),
        in_specs=[VMEM] * 4, out_specs=VMEM, name="first_mix",
    )(arrived, lift_wide, bias_column, weights)
    prepared = call(
        prepare_coarse,
        out_shape=(shape((2, 512, 256), BF16), shape((624, 512), BF16)),
        in_specs=[HBM] + [VMEM] * 7, out_specs=(VMEM,) * 2, name="prepare_coarse",
        cost_estimate=work,
    )(mixed, waves, steps, lift, lift_bias[None], bypass_in, bias_in[None], bypass_out)
    mine, prepared = lax.optimization_barrier((exchange(mixed), prepared))
    spread_t, pack = prepared
    kept, sent, skip = call(
        coarse_level,
        out_shape=(
            shape((2, 128, 128), F32), shape((2, 128, 128), F32),
            pltpu.HBM((8, NZ, 512), F32),
        ),
        in_specs=[VMEM] * 6, out_specs=(VMEM, VMEM, HBM), name="coarse_level",
        scratch_shapes=[pltpu.VMEM((4, 128, 128), F32)] * 4
        + [pltpu.VMEM((8, NZ, 512), F32), dma((8,))],
    )(
        mine.reshape(OWNERS * 8, 128), between_cores(mine).reshape(OWNERS * 8, 128), pack,
        fields, z_back, z_fwd,
    )
    spectrum = call(
        spread,
        out_shape=shape((OWNERS * 8, 128), F32),
        in_specs=[VMEM] * 3, out_specs=VMEM, name="spread",
    )(kept, between_cores(sent), spread_t)
    prepared = call(
        prepare_fine,
        out_shape=(
            pltpu.HBM((2, 512, 512), BF16), shape((2, 512, 128), BF16), shape((16, 512), BF16),
            pltpu.HBM((CIN, 16, 16, NZ), F32),
        ),
        in_specs=[HBM] + [VMEM] * 8, out_specs=(VMEM,) * 4, name="prepare_fine",
        cost_estimate=work,
    )(
        spectrum, waves, steps, fields, lift, lift_bias[None], bias_out[None], project,
        project_bias[:, None],
    )
    arrived, prepared = lax.optimization_barrier(
        (exchange(spectrum.reshape(OWNERS, 8, 128)), prepared)
    )
    fine_t, project_mix, bias_mix, base = prepared
    mixed = call(
        second_mix,
        out_shape=shape((OWNERS, 8, 128), F32),
        in_specs=[HBM, VMEM], out_specs=VMEM, name="second_mix",
        scratch_shapes=[pltpu.VMEM((OWNERS, 8, 128), F32), dma((4,))],
    )(arrived, spectral_out)
    return call(
        fine_level,
        out_shape=shape((CIN, 16, 16, NZ), F32),
        in_specs=[VMEM, VMEM, HBM, HBM, VMEM, VMEM, HBM], out_specs=VMEM, name="fine_level",
        scratch_shapes=[
            pltpu.VMEM((CIN, 16, 16, NZ), F32),
            pltpu.VMEM((2, 512, 128), F32), pltpu.VMEM((4, 256, 128), F32),
            pltpu.VMEM((8, NZ, 512), F32), pltpu.VMEM((64, NZ), BF16), dma((10,)),
        ],
    )(
        exchange(mixed).reshape(OWNERS * 8, 128), fine_t, stay(jnp.asarray(z_back)), stay(skip),
        project_mix, bias_mix, stay(base),
    )


def solution(mesh):
    owned = P(AXES, None, None, None, None)
    grid = P(None, "gx", "gy", None)
    in_specs = (grid, P(), P(), owned, P(), P(), owned, P(), P(), P(), P())
    return jax.shard_map(
        on_device, mesh=mesh, in_specs=in_specs, out_specs=grid, check_vma=False
    )
```

```python
import functools
import math

import jax
import jax.numpy as jnp
import numpy as np
from jax import lax
from jax.experimental import pallas as pl
from jax.experimental.pallas import tpu as pltpu
from jax.sharding import PartitionSpec as P

KX, KY, KZ = 16, 16, 8
NX, NY, NZ = 128, 256, 128
CIN, C1, C2 = 4, 32, 64
AXES = ("gx", "gy")
OWNERS = 128
TOTAL = NX * NY * NZ
BACK = math.sqrt(2.0 / (KX * KY * KZ))
F32 = jnp.float32
BF16 = jnp.bfloat16
UNROLL = 8
FINE_UNROLL = 1
VMEM = pl.BlockSpec(memory_space=pltpu.VMEM)
HBM = pl.BlockSpec(memory_space=pltpu.HBM)
PARAMS = pltpu.CompilerParams(vmem_limit_bytes=16 << 20)
ALONE = pltpu.CompilerParams(vmem_limit_bytes=60 << 20)


def mode_frequencies():
    centered = np.where(np.arange(16) < 8, np.arange(16), np.arange(16) - 16)
    n = np.arange(OWNERS)
    fx = np.stack([centered[n // 8]] * 2)
    fy = np.stack([centered[2 * (n % 8) + s] for s in range(2)])
    return fx, fy


def place_angles(xs, ys, x_length, y_length):
    fx, fy = mode_frequencies()
    turns = (
        fx[:, :, None, None] * xs[None, None, :, None] / x_length
        + fy[:, :, None, None] * ys[None, None, None, :] / y_length
    )
    return 2.0 * np.pi * turns


def wave_tables():
    fx, fy = mode_frequencies()
    ahead = np.array([0.0, 0.5 * np.pi])[None, None, :, None]
    places = np.arange(16)[:, None, None, None]
    along_x = 2.0 * np.pi * places * fx[None, :, None, :] / NX + ahead
    along_y = 2.0 * np.pi * places * fy[None, :, None, :] / NY + 0.0 * ahead
    tables = [np.cos(along_x), np.sin(along_x), np.cos(along_y), np.sin(along_y)]
    return np.stack(tables).reshape(4, 16, 512).astype(np.float32)


def phase_steps():
    fx, fy = mode_frequencies()
    steps = np.stack([np.stack([2 * fx, 2 * fx], axis=1), np.stack([fy, fy], axis=1)])
    return steps.reshape(2, 512).astype(np.int32)


def z_angles():
    return 2.0 * np.pi * (np.arange(NZ)[:, None] * np.arange(KZ)[None, :] % NZ) / NZ


def split_np(table):
    high = table.astype(BF16)
    low = (table - high.astype(np.float32)).astype(BF16)
    return high, low


def first_z_table():
    c, s = np.cos(z_angles()), np.sin(z_angles())
    parts = np.array([[c, -s], [-s, -c]])
    table = np.zeros((CIN, NZ, 2, 2, KZ, CIN))
    for ch in range(CIN):
        table[ch, :, :, :, :, ch] = parts.transpose(2, 0, 1, 3)
    high, low = split_np(table.reshape(CIN, NZ, 128).astype(np.float32))
    return np.concatenate([high, high, low], axis=1)


def first_places_table():
    fx, fy = mode_frequencies()
    places = np.arange(16)
    turns = (
        fx[:, :, None, None] * places[:, None] / NX + fy[:, :, None, None] * places[None, :] / NY
    )
    angles = 2.0 * np.pi * turns
    table = np.stack([np.cos(angles), np.sin(angles)], axis=1) / math.sqrt(TOTAL)
    return np.stack(split_np(table.reshape(512, 256).astype(np.float32)))


def inverse_z_table():
    table = np.stack([np.cos(z_angles()), -np.sin(z_angles())], axis=2)
    high, low = split_np(table.reshape(NZ, 16).astype(np.float32))
    ones = np.zeros((16, NZ), BF16)
    ones[:3] = 1.0
    return np.concatenate([high.T, high.T, low.T, ones], axis=0)


def forward_z_table():
    table = np.stack([np.cos(z_angles()).T, -np.sin(z_angles()).T], axis=0)
    high, low = split_np(table.reshape(16, NZ).astype(np.float32))
    return np.block([[high, high], [low, np.zeros_like(low)]])


def split(x):
    high = x.astype(BF16)
    return high, (x - high.astype(F32)).astype(BF16)


def bias_rows(bias):
    high, less = split(bias)
    least = (bias - high.astype(F32) - less.astype(F32)).astype(BF16)
    row = iota((16, bias.shape[1]), 0)
    rows = [v.astype(F32) for v in (high, less, least)]
    total = jnp.where(row == 0, rows[0], jnp.where(row == 1, rows[1], rows[2]))
    return jnp.where(row < 3, total, 0.0).astype(BF16)


def mm(a, b, dims=((1,), (0,))):
    return lax.dot_general(a, b, (dims, ((), ())), preferred_element_type=F32)


def mm3(a, b, dims=((1,), (0,))):
    ah, al = split(a)
    bh, bl = split(b)
    return mm(ah, bh, dims) + mm(ah, bl, dims) + mm(al, bh, dims)


def exact(a, b, dims=((1,), (0,))):
    return lax.dot_general(
        a, b, (dims, ((), ())), precision=lax.Precision.HIGHEST, preferred_element_type=F32
    )


def iota(shape, dim):
    return lax.broadcasted_iota(jnp.int32, shape, dim)


def ones_where(condition):
    return jnp.where(condition, 1.0, 0.0).astype(F32)


def gelu(x):
    return 0.5 * x * (1.0 + lax.erf(x * math.sqrt(0.5)))


def regroup(rows):
    group = iota(rows[0].shape, 1) // 32
    made = []
    for v in range(4):
        total = rows[v]
        for u in range(4):
            if u != v:
                moved = pltpu.roll(rows[u], ((u - v) % 4) * 32, 1)
                total = jnp.where(group == u, moved, total)
        made.append(total)
    return made


def my_place():
    return lax.axis_index("gx"), lax.axis_index("gy")


def phases(steps, place):
    turns = (steps[0:1] * place[0] + steps[1:2] * place[1]) & 15
    angle = turns.astype(F32) * (2.0 * math.pi / 16)
    return jnp.cos(angle), jnp.sin(angle)


def device_waves(waves, steps, place):
    cos, sin = phases(steps, place)
    return waves[0] * cos - waves[1] * sin, waves[1] * cos + waves[0] * sin


def wave_rows(along_x, cos_y, sin_y, xs):
    cos_x, sin_x = along_x
    real = [cos_x[x : x + 1] * cos_y - sin_x[x : x + 1] * sin_y for x in xs]
    imag = [sin_x[x : x + 1] * cos_y + cos_x[x : x + 1] * sin_y for x in xs]
    return jnp.concatenate(real, axis=0), jnp.concatenate(imag, axis=0)


def first_spectrum(
    fields, ztab_h, ptab_h, steps_h, out, token, fields_v, ztab, ptab, steps, sems,
):
    pairs = [(steps_h, steps)]
    for ch in range(CIN):
        pairs += [(fields.at[ch], fields_v.at[ch]), (ztab_h.at[ch], ztab.at[ch])]
    pairs.append((ptab_h, ptab))
    copies = [
        pltpu.make_async_copy(source, target, sems.at[i])
        for i, (source, target) in enumerate(pairs)
    ]
    for copy in copies:
        copy.start()
    copies[0].wait()
    cos, sin = phases(steps, my_place())
    turn = [v[:, at : at + 128] for at in (0, 256) for v in (cos, sin)]
    turn = jnp.concatenate(turn + [jnp.zeros((124, 128), F32)], axis=0).T
    total = None
    for ch in range(CIN):
        copies[1 + 2 * ch].wait()
        copies[2 + 2 * ch].wait()
        fh, fl = split(fields_v[ch].reshape(256, NZ))
        term = mm(jnp.concatenate([fh, fl], axis=1), ztab[ch, :256]) + mm(fh, ztab[ch, 256:])
        total = term if total is None else total + term
    copies[-1].wait()
    th, tl = split(total)
    both = mm(ptab[0], th) + mm(ptab[0], tl) + mm(ptab[1], th)
    low = iota((128, 128), 1) < 64
    rows = []
    for s in range(2):
        part_cos = both[256 * s : 256 * s + 128]
        part_sin = both[256 * s + 128 : 256 * s + 256]
        part_sin = pltpu.roll(part_sin, 64, 1)
        pair = jnp.where(low, part_cos + part_sin, part_cos - part_sin)
        cos_s, sin_s = turn[:, 2 * s : 2 * s + 1], turn[:, 2 * s + 1 : 2 * s + 2]
        rows.append(cos_s * pair + sin_s * pltpu.roll(pair, 64, 1))
    out[...] = jnp.where(low, rows[0], pltpu.roll(rows[1], 64, 1))
    token[...] = rows[0][:8]


def prepare_mix(after, weights, lift, lift_bias, weights_v, lift_wide, bias_column, sem):
    copy = pltpu.make_async_copy(weights, weights_v, sem)
    copy.start()
    lift_wide[...] = exact(lift[...], ones_where(iota((CIN, 128), 0) == iota((CIN, 128), 1) % 4))
    gx, gy = my_place()
    at_zero = (iota((C1, 32), 1) + gx + gy) == 0
    bias_column[...] = jnp.where(at_zero, lift_bias[...] * math.sqrt(TOTAL), 0.0)
    copy.wait()


def prepare(
    after, waves, steps, lift, lift_bias, bypass_in, bias_in, bypass_out, bias_out, project,
    spread_t, pack, fine_t, wide_mix, project_mix, bias_mix,
):
    nt = ((1,), (1,))
    gx, gy = my_place()
    own = device_waves(waves, steps, (gx, gy))
    mate = device_waves(waves, steps, (gx + 1 - 2 * (gx % 2), gy))
    cos_y = jnp.concatenate([waves[2, 2 * q : 2 * q + 1] for q in range(8)], axis=0)
    sin_y = jnp.concatenate([waves[3, 2 * q : 2 * q + 1] for q in range(8)], axis=0)
    tables = [
        jnp.concatenate(wave_rows(along, cos_y, sin_y, range(0, 16, 2)), axis=0)
        for along in (own, mate)
    ]
    pack[0:128], pack[128:256] = split(tables[0] * BACK)
    scale = 1.0 / math.sqrt(TOTAL / 4.0)
    for patch in range(2):
        at = slice(128 * patch, 128 * patch + 128)
        high, less = split(tables[patch].T * scale)
        spread_t[0, :, at] = high
        spread_t[1, :, at] = less
    lanes = [
        ones_where(iota((C2, 128), 0) == 32 * h + iota((C2, 128), 1) % 32) for h in range(2)
    ]
    through = exact(lift[...], bypass_in[...], ((0,), (1,)))
    through = exact(ones_where(iota((32, CIN), 0) // 8 == iota((32, CIN), 1)), through)
    offset = bias_in[...] + exact(lift_bias[...], bypass_in[...], nt)
    for t in range(4):
        at = slice(128 * t, 128 * t + 128)
        same = iota((32, 128), 0) % 8 == 4 * (t // 2) + iota((32, 128), 1) // 32
        high, less = split(jnp.where(same, exact(through, lanes[t % 2]), 0.0))
        rows = bias_rows(exact(offset, lanes[t % 2]))
        pack[256:368, at] = jnp.concatenate([rows, high, less, high], axis=0)
    spread_d = ones_where(iota((C1, 256), 0) == iota((C1, 256), 1) % 32)
    same = iota((128, 256), 0) // 32 == iota((128, 256), 1) // 64
    for h in range(2):
        pick = ones_where(iota((128, C2), 1) == 32 * h + iota((128, C2), 0) % 32)
        wide = exact(exact(pick, bypass_out[...], nt), spread_d)
        high, less = split(jnp.where(same, wide, 0.0))
        wide_mix[128 * h : 128 * h + 128] = jnp.concatenate([high, less], axis=1)
    scaled = (own[0] * BACK, own[1] * BACK)
    for x in range(0, 16, 8):
        pair = wave_rows(scaled, waves[2], waves[3], range(x, x + 8))
        for part in range(2):
            at = slice(256 * part + 16 * x, 256 * part + 16 * x + 128)
            high, less = split(pair[part])
            fine_t[0, at] = high
            fine_t[1, at] = less
    lanes = ones_where(iota((C1, 512), 0) == iota((C1, 512), 1) % 32)
    bias_mix[...] = bias_rows(exact(bias_out[...], lanes))
    pick = ones_where(iota((512, C1), 1) == iota((512, C1), 0) % 32)
    onto = ones_where(iota((CIN, 128), 0) == iota((CIN, 128), 1) % 64 // 16)
    made = exact(exact(pick, project[...], nt), onto)
    lane = iota((512, 128), 1)
    made = jnp.where(iota((512, 128), 0) // 32 == lane % 16, made, 0.0)
    high = made.astype(BF16).astype(F32)
    project_mix[0] = jnp.where(lane < 64, high, made - high).astype(BF16)
    project_mix[1] = jnp.where(lane < 64, high, 0.0).astype(BF16)


def bypass(
    after, values, wide_mix_h, fields, lift, lift_bias, project, project_bias, skip, base,
    values_v, skip_v, wide_mix, in_sems, out_sems,
):
    def taken(p):
        return pltpu.make_async_copy(values.at[p], values_v.at[p], in_sems.at[p])

    def given(p):
        return pltpu.make_async_copy(skip_v.at[p], skip.at[p], out_sems.at[p])

    mix_copy = pltpu.make_async_copy(wide_mix_h, wide_mix, in_sems.at[8])
    mix_copy.start()
    for p in range(8):
        taken(p).start()
    across = exact(project[...], lift[...])
    constant = project_bias[...] + exact(project[...], lift_bias[...], ((1,), (1,)))
    mix_copy.wait()

    def step(x, carry):
        for o in range(CIN):
            total = jnp.broadcast_to(constant[o : o + 1], (16, NZ))
            for ch in range(CIN):
                total += across[o : o + 1, ch : ch + 1] * fields[ch, x]
            base[o, x] = total
        return carry

    lax.fori_loop(0, 16, step, 0)

    def wide_step(p, carry):
        taken(p).wait()
        for q in range(2):
            at = slice(256 * q, 256 * q + 256)
            high, less = values_v[p, 0, :, at], values_v[p, 1, :, at]
            wide = mm(high, wide_mix[:, :256]) + mm(high, wide_mix[:, 256:])
            skip_v[p, :, at] = wide + mm(less, wide_mix[:, :256])
        given(p).start()
        return carry

    lax.fori_loop(0, 8, wide_step, 0, unroll=2)
    for p in range(8):
        given(p).wait()


def mixed_row(columns, weights, wide):
    pieces = [[[None] * KZ for _ in range(2)] for _ in range(2)]
    for s in range(2):
        for k in range(KZ):
            real, imag = columns(s, 0, k), columns(s, 1, k)
            wr, wi = weights[s, 0, k], weights[s, 1, k]
            pieces[s][0][k] = jnp.sum(real * wr - imag * wi, axis=0, keepdims=True)
            pieces[s][1][k] = jnp.sum(real * wi + imag * wr, axis=0, keepdims=True)
    per = 128 // wide
    return [
        jnp.concatenate(
            [
                jnp.concatenate(
                    [v[:, at : at + wide] for v in pieces[s][part][k : k + per]], axis=1
                )
                for s in range(2)
                for part in range(2)
                for k in range(0, KZ, per)
            ],
            axis=0,
        )
        for at in range(0, weights.shape[-1], wide)
    ]


def first_mix(arrived, lift_wide, bias_column, weights, out, token):
    row = jnp.sum(arrived[...], axis=0, keepdims=True)
    source = lax.broadcasted_iota(jnp.int32, (128, 32), 0) // CIN
    pick = (source == lax.broadcasted_iota(jnp.int32, (128, 32), 1)).astype(F32)
    lifted = (
        lax.dot_general(
            lift_wide[...] * row, pick, (((1,), (0,)), ((), ())),
            precision=lax.Precision.HIGHEST, preferred_element_type=F32,
        )
        + bias_column[...]
    )

    def column(s, part, k):
        at = s * 16 + part * 8 + k
        return lifted[:, at : at + 1]

    halves = mixed_row(column, weights, 32)
    token[...] = halves[0]
    for n in range(OWNERS):
        out[n] = halves[n // 16 % 2]


def second_mix(arrived, weights, out):
    sums = [None, None]
    for n in range(OWNERS):
        half = n // 16 % 2
        sums[half] = arrived[n] if sums[half] is None else sums[half] + arrived[n]
    stacked = jnp.concatenate(sums + [jnp.zeros((112, 128), F32)], axis=0).T

    def column(s, part, k):
        at = (s * 2 + part) * 2 + k // 4
        rows = slice(k % 4 * 32, k % 4 * 32 + 32)
        return jnp.concatenate([stacked[rows, at : at + 1], stacked[rows, at + 8 : at + 9]], axis=0)

    (block,) = mixed_row(column, weights, 32)
    for n in range(OWNERS):
        out[n] = block


def coarse_level(
    mine, other, pack, fields, z_back, z_fwd,
    kept, sent, values, y_s, rhs_s, g_s, t_s, values_v, sems,
):
    core = lax.axis_index("gx") % 2
    modes = []
    for t in range(4):
        tiles = [
            ref[pl.ds(2 * t + u, OWNERS, stride=8), :] for ref in (mine, other) for u in range(2)
        ]
        modes.append(jnp.concatenate(tiles, axis=1))
    mh, ml = split(jnp.concatenate(modes, axis=0))
    th, tl = pack[0:128], pack[128:256]
    made = mm(th, mh) + mm(tl, mh) + mm(th, ml)
    for u in range(2):
        for t in range(2):
            at = 128 * (2 * u + t)
            y_s[2 * ((core + u) % 2) + t] = made[:, at : at + 128]
    for h in range(2):
        for t in range(2):
            for q in range(2):
                made = regroup(
                    [y_s[2 * h + t, pl.ds(4 * q + u, 16, stride=8), :] for u in range(4)]
                )
                for v in range(4):
                    rhs_s[2 * q + h, pl.ds(16 * (4 * t + v), 16), :] = made[v]

    def step(p, carry):
        rows = [rhs_s[t, pl.ds(p, 16, stride=8), :] for t in range(4)]
        high, less = split(jnp.concatenate(rows, axis=1))
        pooled = []
        for ch in range(CIN):
            total = jnp.zeros((8, 128), F32)
            for dx in range(2):
                for dy in range(2):
                    total += fields[ch, 2 * p + dx, pl.ds(dy, 8, stride=2), :]
            pooled.append(total * 0.25)
        ph, pll = split(jnp.concatenate(pooled, axis=0))
        left = jnp.concatenate([z_back[...], ph, ph, pll], axis=0)
        right = jnp.concatenate([high, less, high, pack[256:368]], axis=0)
        value = gelu(mm(left, right, ((0,), (0,))))
        vh, vl = split(value)
        made = mm(z_fwd[...], jnp.concatenate([vh, vl], axis=0))
        made = made[:16] + made[16:]
        for t in range(4):
            at = slice(128 * t, 128 * t + 128)
            g_s[t, pl.ds(pl.multiple_of(p * 8, 8), 8), :] = made[:8, at]
            g_s[t, pl.ds(pl.multiple_of(p * 8 + 64, 8), 8), :] = made[8:, at]
        values_v[p, 0] = vh
        values_v[p, 1] = vl
        pltpu.make_async_copy(values_v.at[p], values.at[p], sems.at[p]).start()
        return carry

    lax.fori_loop(0, 8, step, 0, unroll=UNROLL)
    for h in range(2):
        for t in range(2):
            for q in range(2):
                made = regroup(
                    [g_s[2 * q + h, pl.ds(4 * t + v, 16, stride=8), :] for v in range(4)]
                )
                for u in range(4):
                    t_s[2 * h + t, pl.ds(4 * q + u, 16, stride=8), :] = made[u]
    for t in range(2):
        kept[t] = t_s[2 * core + t]
        sent[t] = t_s[2 * (1 - core) + t]
    for p in range(8):
        pltpu.make_async_copy(values_v.at[p], values.at[p], sems.at[p]).wait()


def spread(kept, got, table, out, token):
    rows = [jnp.concatenate([ref[0], ref[1]], axis=1) for ref in (kept, got)]
    th, tl = split(jnp.concatenate(rows, axis=0))
    for t in range(4):
        at = slice(128 * t, 128 * t + 128)
        made = mm(table[0, at], th) + mm(table[0, at], tl) + mm(table[1, at], th)
        for u in range(2):
            out[pl.ds(2 * t + u, OWNERS, stride=8), :] = made[:, 128 * u : 128 * u + 128]
    token[...] = made[:8, :128]


def fine_level(
    arrived, table, z_back_h, skip, project_h, bias_h, base_h, out, base, out_v,
    y_s, rhs_s, skip_v, z_back, project_mix, bias_mix, sems, base_sems, out_sems,):
    def taken(p):
        rows = pl.ds(2 * p, 2)
        return (
            pltpu.make_async_copy(skip.at[p], skip_v.at[p], sems.at[p]),
            pltpu.make_async_copy(base_h.at[:, rows], base.at[:, rows], base_sems.at[p]),
        )

    def given(p):
        rows = pl.ds(2 * p, 2)
        return pltpu.make_async_copy(out_v.at[:, rows], out.at[:, rows], out_sems.at[p])

    small = [
        pltpu.make_async_copy(source, target, sems.at[i])
        for i, source, target in (
            (8, z_back_h, z_back), (9, project_h, project_mix), (10, bias_h, bias_mix)
        )
    ]
    for copy in small:
        copy.start()
    for p in range(8):
        for copy in taken(p):
            copy.start()
    modes = []
    for t in range(4):
        tiles = [arrived[pl.ds(2 * t + u, OWNERS, stride=8), :] for u in range(2)]
        modes.append(jnp.concatenate(tiles, axis=1))
    mh, ml = split(jnp.concatenate(modes, axis=0))
    for t in range(4):
        at = slice(128 * t, 128 * t + 128)
        made = mm(table[0, at], mh) + mm(table[0, at], ml) + mm(table[1, at], mh)
        y_s[0, at] = made[:, :128]
        y_s[1, at] = made[:, 128:]
    for t in range(2):
        for y in range(4):
            made = regroup([y_s[t, pl.ds(4 * y + u, 32, stride=16), :] for u in range(4)])
            for v in range(4):
                rhs_s[y, pl.ds(32 * (4 * t + v), 32), :] = made[v]
    for copy in small:
        copy.wait()

    def step(p, carry):
        for copy in taken(p):
            copy.wait()
        for x in (2 * p, 2 * p + 1):
            rows = [rhs_s[t, pl.ds(x, 16, stride=16), :] for t in range(4)]
            high, less = split(jnp.concatenate(rows, axis=1))
            right = jnp.concatenate([high, less, high, bias_mix[...]], axis=0)
            before = mm(z_back[...], right, ((0,), (0,)))
            vh, vl = split(gelu(before + skip_v[p]))
            made = (mm(vh, project_mix[0]) + mm(vl, project_mix[1])).T
            made = made[:64] + made[64:]
            for o in range(CIN):
                out_v[o, x] = made[16 * o : 16 * o + 16] + base[o, x]
        given(p).start()
        return carry

    lax.fori_loop(0, 8, step, 0, unroll=FINE_UNROLL)
    for p in range(8):
        given(p).wait()


def exchange(tiles):
    return lax.all_to_all(tiles, AXES, split_axis=0, concat_axis=0, tiled=True)


def between_cores(array):
    return lax.ppermute(array, "gx", [(i, i ^ 1) for i in range(lax.axis_size("gx"))])


def stay(array):
    return pltpu.with_memory_space_constraint(array, pltpu.HBM)


def on_device(
    fields, lift, lift_bias, spectral_in, bypass_in, bias_in, spectral_out, bypass_out, bias_out,
    project, project_bias,
):
    waves, steps = wave_tables(), phase_steps()
    z_back, z_fwd = inverse_z_table(), forward_z_table()
    call = functools.partial(pl.pallas_call, compiler_params=PARAMS)
    shape = jax.ShapeDtypeStruct
    dma = pltpu.SemaphoreType.DMA
    work = pl.CostEstimate(flops=1 << 31, transcendentals=0, bytes_accessed=6 << 20)
    spectrum, token = pl.pallas_call(
        first_spectrum,
        out_shape=(shape((OWNERS, 128), F32), shape((8, 128), F32)),
        in_specs=[HBM] * 4, out_specs=(VMEM, VMEM),
        scratch_shapes=[
            pltpu.VMEM((CIN, 16, 16, NZ), F32), pltpu.VMEM((CIN, 384, 128), BF16),
            pltpu.VMEM((2, 512, 256), BF16), pltpu.VMEM((2, 512), jnp.int32), dma((10,)),
        ],
        name="first_spectrum", compiler_params=ALONE,
    )(fields, first_z_table(), first_places_table(), steps)
    prepared = call(
        prepare_mix,
        out_shape=(
            shape((2, 2, KZ, C1, C2), F32), shape((C1, 128), F32), shape((C1, 32), F32),
        ),
        in_specs=[VMEM, HBM, VMEM, VMEM], out_specs=(VMEM,) * 3, name="prepare_mix",
        scratch_shapes=[dma(())], cost_estimate=work,
    )(token, stay(spectral_in), lift, lift_bias[:, None])
    arrived, prepared = lax.optimization_barrier((exchange(spectrum), prepared))
    weights, lift_wide, bias_column = prepared
    mixed, token = call(
        first_mix,
        out_shape=(shape((OWNERS, 8, 128), F32), shape((8, 128), F32)),
        in_specs=[VMEM] * 4, out_specs=(VMEM, VMEM), name="first_mix",
    )(arrived, lift_wide, bias_column, weights)
    prepared = call(
        prepare,
        out_shape=(
            shape((2, 512, 256), BF16), shape((368, 512), BF16), pltpu.HBM((2, 512, 512), BF16),
            pltpu.HBM((256, 512), BF16), pltpu.HBM((2, 512, 128), BF16),
            pltpu.HBM((16, 512), BF16),
        ),
        in_specs=[VMEM] * 10, out_specs=(VMEM,) * 6, name="prepare", cost_estimate=work,
    )(
        token, waves, steps, lift, lift_bias[None], bypass_in, bias_in[None], bypass_out,
        bias_out[None], project,
    )
    mine, prepared = lax.optimization_barrier((exchange(mixed), prepared))
    spread_t, pack, fine_t, wide_mix, project_mix, bias_mix = prepared
    kept, sent, values = call(
        coarse_level,
        out_shape=(
            shape((2, 128, 128), F32), shape((2, 128, 128), F32),
            pltpu.HBM((8, 2, NZ, 512), BF16),
        ),
        in_specs=[VMEM] * 6, out_specs=(VMEM, VMEM, HBM), name="coarse_level",
        scratch_shapes=[pltpu.VMEM((4, 128, 128), F32)] * 4
        + [pltpu.VMEM((8, 2, NZ, 512), BF16), dma((8,))],
    )(
        mine.reshape(OWNERS * 8, 128), between_cores(mine).reshape(OWNERS * 8, 128), pack,
        fields, z_back, z_fwd,
    )
    spectrum, token = call(
        spread,
        out_shape=(shape((OWNERS * 8, 128), F32), shape((8, 128), F32)),
        in_specs=[VMEM] * 3, out_specs=(VMEM, VMEM), name="spread",
    )(kept, between_cores(sent), spread_t)
    prepared = call(
        bypass,
        out_shape=(pltpu.HBM((8, NZ, 512), F32), pltpu.HBM((CIN, 16, 16, NZ), F32)),
        in_specs=[VMEM, HBM, HBM] + [VMEM] * 5, out_specs=(HBM, VMEM), name="bypass",
        scratch_shapes=[
            pltpu.VMEM((8, 2, NZ, 512), BF16), pltpu.VMEM((8, NZ, 512), F32),
            pltpu.VMEM((256, 512), BF16), dma((9,)), dma((8,)),
        ],
        cost_estimate=work,
    )(
        token, stay(values), stay(wide_mix), fields, lift, lift_bias[None], project,
        project_bias[:, None],
    )
    arrived, prepared = lax.optimization_barrier(
        (exchange(spectrum.reshape(OWNERS, 8, 128)), prepared)
    )
    skip, base = prepared
    mixed = call(
        second_mix,
        out_shape=shape((OWNERS, 8, 128), F32),
        in_specs=[VMEM, VMEM], out_specs=VMEM, name="second_mix",
    )(arrived, spectral_out)
    return call(
        fine_level,
        out_shape=shape((CIN, 16, 16, NZ), F32),
        in_specs=[VMEM, VMEM] + [HBM] * 5, out_specs=HBM, name="fine_level",
        scratch_shapes=[
            pltpu.VMEM((CIN, 16, 16, NZ), F32), pltpu.VMEM((CIN, 16, 16, NZ), F32),
            pltpu.VMEM((2, 512, 128), F32), pltpu.VMEM((4, 256, 128), F32),
            pltpu.VMEM((8, NZ, 512), F32), pltpu.VMEM((64, NZ), BF16),
            pltpu.VMEM((2, 512, 128), BF16), pltpu.VMEM((16, 512), BF16), dma((11,)), dma((8,)),
            dma((8,)),
        ],
    )(
        exchange(mixed).reshape(OWNERS * 8, 128), fine_t, stay(jnp.asarray(z_back)), stay(skip),
        stay(project_mix), stay(bias_mix), stay(base),
    )


def solution(mesh):
    owned = P(AXES, None, None, None, None)
    grid = P(None, "gx", "gy", None)
    in_specs = (grid, P(), P(), owned, P(), P(), owned, P(), P(), P(), P())
    return jax.shard_map(
        on_device, mesh=mesh, in_specs=in_specs, out_specs=grid, check_vma=False
    )
```

```python
import functools
import math

import jax
import jax.numpy as jnp
import numpy as np
from jax import lax
from jax.experimental import pallas as pl
from jax.experimental.pallas import tpu as pltpu
from jax.sharding import PartitionSpec as P

KX, KY, KZ = 16, 16, 8
NX, NY, NZ = 128, 256, 128
CIN, C1, C2 = 4, 32, 64
AXES = ("gx", "gy")
OWNERS = 128
TOTAL = NX * NY * NZ
BACK = math.sqrt(2.0 / (KX * KY * KZ))
F32 = jnp.float32
BF16 = jnp.bfloat16
UNROLL = 8
FINE_UNROLL = 1
VMEM = pl.BlockSpec(memory_space=pltpu.VMEM)
HBM = pl.BlockSpec(memory_space=pltpu.HBM)
PARAMS = pltpu.CompilerParams(vmem_limit_bytes=16 << 20)
ALONE = pltpu.CompilerParams(vmem_limit_bytes=60 << 20)


def mode_frequencies():
    centered = np.where(np.arange(16) < 8, np.arange(16), np.arange(16) - 16)
    n = np.arange(OWNERS)
    fx = np.stack([centered[n // 8]] * 2)
    fy = np.stack([centered[2 * (n % 8) + s] for s in range(2)])
    return fx, fy


def place_angles(xs, ys, x_length, y_length):
    fx, fy = mode_frequencies()
    turns = (
        fx[:, :, None, None] * xs[None, None, :, None] / x_length
        + fy[:, :, None, None] * ys[None, None, None, :] / y_length
    )
    return 2.0 * np.pi * turns


def wave_tables():
    fx, fy = mode_frequencies()
    ahead = np.array([0.0, 0.5 * np.pi])[None, None, :, None]
    places = np.arange(16)[:, None, None, None]
    along_x = 2.0 * np.pi * places * fx[None, :, None, :] / NX + ahead
    along_y = 2.0 * np.pi * places * fy[None, :, None, :] / NY + 0.0 * ahead
    tables = [np.cos(along_x), np.sin(along_x), np.cos(along_y), np.sin(along_y)]
    return np.stack(tables).reshape(4, 16, 512).astype(np.float32)


def phase_steps():
    fx, fy = mode_frequencies()
    steps = np.stack([np.stack([2 * fx, 2 * fx], axis=1), np.stack([fy, fy], axis=1)])
    return steps.reshape(2, 512).astype(np.int32)


def z_angles():
    return 2.0 * np.pi * (np.arange(NZ)[:, None] * np.arange(KZ)[None, :] % NZ) / NZ


def split_np(table):
    high = table.astype(BF16)
    low = (table - high.astype(np.float32)).astype(BF16)
    return high, low


def first_z_table():
    c, s = np.cos(z_angles()), np.sin(z_angles())
    parts = np.array([[c, -s], [-s, -c]])
    table = np.zeros((CIN, NZ, 2, 2, KZ, CIN))
    for ch in range(CIN):
        table[ch, :, :, :, :, ch] = parts.transpose(2, 0, 1, 3)
    high, low = split_np(table.reshape(CIN, NZ, 128).astype(np.float32))
    return np.concatenate([high, high, low], axis=1)


def first_places_table():
    fx, fy = mode_frequencies()
    places = np.arange(16)
    turns = (
        fx[:, :, None, None] * places[:, None] / NX + fy[:, :, None, None] * places[None, :] / NY
    )
    angles = 2.0 * np.pi * turns
    table = np.stack([np.cos(angles), np.sin(angles)], axis=1) / math.sqrt(TOTAL)
    return np.stack(split_np(table.reshape(512, 256).astype(np.float32)))


def inverse_z_table():
    table = np.stack([np.cos(z_angles()), -np.sin(z_angles())], axis=2)
    high, low = split_np(table.reshape(NZ, 16).astype(np.float32))
    ones = np.zeros((16, NZ), BF16)
    ones[:3] = 1.0
    return np.concatenate([high.T, high.T, low.T, ones], axis=0)


def forward_z_table():
    table = np.stack([np.cos(z_angles()).T, -np.sin(z_angles()).T], axis=0)
    high, low = split_np(table.reshape(16, NZ).astype(np.float32))
    return np.block([[high, high], [low, np.zeros_like(low)]])


def split(x):
    high = x.astype(BF16)
    return high, (x - high.astype(F32)).astype(BF16)


def bias_rows(bias):
    high, less = split(bias)
    least = (bias - high.astype(F32) - less.astype(F32)).astype(BF16)
    row = iota((16, bias.shape[1]), 0)
    rows = [v.astype(F32) for v in (high, less, least)]
    total = jnp.where(row == 0, rows[0], jnp.where(row == 1, rows[1], rows[2]))
    return jnp.where(row < 3, total, 0.0).astype(BF16)


def mm(a, b, dims=((1,), (0,))):
    return lax.dot_general(a, b, (dims, ((), ())), preferred_element_type=F32)


def mm3(a, b, dims=((1,), (0,))):
    ah, al = split(a)
    bh, bl = split(b)
    return mm(ah, bh, dims) + mm(ah, bl, dims) + mm(al, bh, dims)


def exact(a, b, dims=((1,), (0,))):
    return lax.dot_general(
        a, b, (dims, ((), ())), precision=lax.Precision.HIGHEST, preferred_element_type=F32
    )


def iota(shape, dim):
    return lax.broadcasted_iota(jnp.int32, shape, dim)


def ones_where(condition):
    return jnp.where(condition, 1.0, 0.0).astype(F32)


def gelu(x):
    return 0.5 * x * (1.0 + lax.erf(x * math.sqrt(0.5)))


def regroup(rows):
    group = iota(rows[0].shape, 1) // 32
    made = []
    for v in range(4):
        total = rows[v]
        for u in range(4):
            if u != v:
                moved = pltpu.roll(rows[u], ((u - v) % 4) * 32, 1)
                total = jnp.where(group == u, moved, total)
        made.append(total)
    return made


def my_place():
    return lax.axis_index("gx"), lax.axis_index("gy")


def phases(steps, place):
    turns = (steps[0:1] * place[0] + steps[1:2] * place[1]) & 15
    angle = turns.astype(F32) * (2.0 * math.pi / 16)
    return jnp.cos(angle), jnp.sin(angle)


def device_waves(waves, steps, place):
    cos, sin = phases(steps, place)
    return waves[0] * cos - waves[1] * sin, waves[1] * cos + waves[0] * sin


def wave_rows(along_x, cos_y, sin_y, xs):
    cos_x, sin_x = along_x
    real = [cos_x[x : x + 1] * cos_y - sin_x[x : x + 1] * sin_y for x in xs]
    imag = [sin_x[x : x + 1] * cos_y + cos_x[x : x + 1] * sin_y for x in xs]
    return jnp.concatenate(real, axis=0), jnp.concatenate(imag, axis=0)


def first_spectrum(
    fields, ztab_h, ptab_h, steps_h, out, token, fields_v, ztab, ptab, steps, sems,
):
    pairs = [(steps_h, steps)]
    for ch in range(CIN):
        pairs += [(fields.at[ch], fields_v.at[ch]), (ztab_h.at[ch], ztab.at[ch])]
    pairs.append((ptab_h, ptab))
    copies = [
        pltpu.make_async_copy(source, target, sems.at[i])
        for i, (source, target) in enumerate(pairs)
    ]
    for copy in copies:
        copy.start()
    copies[0].wait()
    cos, sin = phases(steps, my_place())
    turn = [v[:, at : at + 128] for at in (0, 256) for v in (cos, sin)]
    turn = jnp.concatenate(turn + [jnp.zeros((124, 128), F32)], axis=0).T
    total = None
    for ch in range(CIN):
        copies[1 + 2 * ch].wait()
        copies[2 + 2 * ch].wait()
        fh, fl = split(fields_v[ch].reshape(256, NZ))
        term = mm(jnp.concatenate([fh, fl], axis=1), ztab[ch, :256]) + mm(fh, ztab[ch, 256:])
        total = term if total is None else total + term
    copies[-1].wait()
    th, tl = split(total)
    both = mm(ptab[0], th) + mm(ptab[0], tl) + mm(ptab[1], th)
    low = iota((128, 128), 1) < 64
    rows = []
    for s in range(2):
        part_cos = both[256 * s : 256 * s + 128]
        part_sin = both[256 * s + 128 : 256 * s + 256]
        part_sin = pltpu.roll(part_sin, 64, 1)
        pair = jnp.where(low, part_cos + part_sin, part_cos - part_sin)
        cos_s, sin_s = turn[:, 2 * s : 2 * s + 1], turn[:, 2 * s + 1 : 2 * s + 2]
        rows.append(cos_s * pair + sin_s * pltpu.roll(pair, 64, 1))
    out[...] = jnp.where(low, rows[0], pltpu.roll(rows[1], 64, 1))
    token[...] = rows[0][:8]


def prepare_mix(after, weights, lift, lift_bias, weights_v, lift_wide, bias_column, sem):
    copy = pltpu.make_async_copy(weights, weights_v, sem)
    copy.start()
    lift_wide[...] = exact(lift[...], ones_where(iota((CIN, 128), 0) == iota((CIN, 128), 1) % 4))
    gx, gy = my_place()
    at_zero = (iota((C1, 32), 1) + gx + gy) == 0
    bias_column[...] = jnp.where(at_zero, lift_bias[...] * math.sqrt(TOTAL), 0.0)
    copy.wait()


def prepare(
    after, waves, steps, lift, lift_bias, bypass_in, bias_in, bypass_out, bias_out, project,
    own_t, mate_t, spread_t, pack, fine_t, wide_mix, project_mix, bias_mix,
):
    nt = ((1,), (1,))
    gx, gy = my_place()
    own = device_waves(waves, steps, (gx, gy))
    mate = device_waves(waves, steps, (gx + 1 - 2 * (gx % 2), gy))
    cos_y = jnp.concatenate([waves[2, 2 * q : 2 * q + 1] for q in range(8)], axis=0)
    sin_y = jnp.concatenate([waves[3, 2 * q : 2 * q + 1] for q in range(8)], axis=0)
    tables = [
        jnp.concatenate(wave_rows(along, cos_y, sin_y, range(0, 16, 2)), axis=0)
        for along in (own, mate)
    ]
    own_t[0:128], own_t[128:256] = split(tables[0] * BACK)
    mate_t[0:128], mate_t[128:256] = split(tables[1] * BACK)
    scale = 1.0 / math.sqrt(TOTAL / 4.0)
    for patch in range(2):
        at = slice(128 * patch, 128 * patch + 128)
        high, less = split(tables[patch].T * scale)
        spread_t[0, :, at] = high
        spread_t[1, :, at] = less
    lanes = [
        ones_where(iota((C2, 128), 0) == 32 * h + iota((C2, 128), 1) % 32) for h in range(2)
    ]
    through = exact(lift[...], bypass_in[...], ((0,), (1,)))
    through = exact(ones_where(iota((32, CIN), 0) // 8 == iota((32, CIN), 1)), through)
    offset = bias_in[...] + exact(lift_bias[...], bypass_in[...], nt)
    for t in range(4):
        at = slice(128 * t, 128 * t + 128)
        same = iota((32, 128), 0) % 8 == 4 * (t // 2) + iota((32, 128), 1) // 32
        high, less = split(jnp.where(same, exact(through, lanes[t % 2]), 0.0))
        rows = bias_rows(exact(offset, lanes[t % 2]))
        pack[:, at] = jnp.concatenate([rows, high, less, high], axis=0)
    spread_d = ones_where(iota((C1, 256), 0) == iota((C1, 256), 1) % 32)
    same = iota((128, 256), 0) // 32 == iota((128, 256), 1) // 64
    for h in range(2):
        pick = ones_where(iota((128, C2), 1) == 32 * h + iota((128, C2), 0) % 32)
        wide = exact(exact(pick, bypass_out[...], nt), spread_d)
        high, less = split(jnp.where(same, wide, 0.0))
        wide_mix[128 * h : 128 * h + 128] = jnp.concatenate([high, less], axis=1)
    scaled = (own[0] * BACK, own[1] * BACK)
    for x in range(0, 16, 8):
        pair = wave_rows(scaled, waves[2], waves[3], range(x, x + 8))
        for part in range(2):
            at = slice(256 * part + 16 * x, 256 * part + 16 * x + 128)
            high, less = split(pair[part])
            fine_t[0, at] = high
            fine_t[1, at] = less
    lanes = ones_where(iota((C1, 512), 0) == iota((C1, 512), 1) % 32)
    bias_mix[...] = bias_rows(exact(bias_out[...], lanes))
    pick = ones_where(iota((512, C1), 1) == iota((512, C1), 0) % 32)
    onto = ones_where(iota((CIN, 128), 0) == iota((CIN, 128), 1) % 64 // 16)
    made = exact(exact(pick, project[...], nt), onto)
    lane = iota((512, 128), 1)
    made = jnp.where(iota((512, 128), 0) // 32 == lane % 16, made, 0.0)
    high = made.astype(BF16).astype(F32)
    project_mix[...] = jnp.where(lane < 64, high, made - high).T.astype(BF16)


def bypass(
    after, values, wide_mix_h, fields, lift, lift_bias, project, project_bias, skip, base,
    values_v, skip_v, wide_mix, in_sems, out_sems,
):
    def taken(p):
        return pltpu.make_async_copy(values.at[p], values_v.at[p], in_sems.at[p])

    def given(p):
        return pltpu.make_async_copy(skip_v.at[p], skip.at[p], out_sems.at[p])

    mix_copy = pltpu.make_async_copy(wide_mix_h, wide_mix, in_sems.at[8])
    mix_copy.start()
    for p in range(8):
        taken(p).start()
    across = exact(project[...], lift[...])
    constant = project_bias[...] + exact(project[...], lift_bias[...], ((1,), (1,)))
    mix_copy.wait()

    def step(x, carry):
        for o in range(CIN):
            total = jnp.broadcast_to(constant[o : o + 1], (16, NZ))
            for ch in range(CIN):
                total += across[o : o + 1, ch : ch + 1] * fields[ch, x]
            base[o, x] = total
        return carry

    lax.fori_loop(0, 16, step, 0)

    def wide_step(p, carry):
        taken(p).wait()
        for q in range(2):
            at = slice(256 * q, 256 * q + 256)
            high, less = values_v[p, 0, :, at], values_v[p, 1, :, at]
            wide = mm(high, wide_mix[:, :256]) + mm(high, wide_mix[:, 256:])
            skip_v[p, :, at] = wide + mm(less, wide_mix[:, :256])
        given(p).start()
        return carry

    lax.fori_loop(0, 8, wide_step, 0, unroll=2)
    for p in range(8):
        given(p).wait()


def mixed_row(columns, weights, wide):
    pieces = [[[None] * KZ for _ in range(2)] for _ in range(2)]
    for s in range(2):
        for k in range(KZ):
            real, imag = columns(s, 0, k), columns(s, 1, k)
            wr, wi = weights[s, 0, k], weights[s, 1, k]
            pieces[s][0][k] = jnp.sum(real * wr - imag * wi, axis=0, keepdims=True)
            pieces[s][1][k] = jnp.sum(real * wi + imag * wr, axis=0, keepdims=True)
    per = 128 // wide
    return [
        jnp.concatenate(
            [
                jnp.concatenate(
                    [v[:, at : at + wide] for v in pieces[s][part][k : k + per]], axis=1
                )
                for s in range(2)
                for part in range(2)
                for k in range(0, KZ, per)
            ],
            axis=0,
        )
        for at in range(0, weights.shape[-1], wide)
    ]


def first_mix(arrived, lift_wide, bias_column, weights, out, token, blocks, sems):
    row = jnp.sum(arrived[...], axis=0, keepdims=True)
    source = lax.broadcasted_iota(jnp.int32, (128, 32), 0) // CIN
    pick = (source == lax.broadcasted_iota(jnp.int32, (128, 32), 1)).astype(F32)
    lifted = (
        lax.dot_general(
            lift_wide[...] * row, pick, (((1,), (0,)), ((), ())),
            precision=lax.Precision.HIGHEST, preferred_element_type=F32,
        )
        + bias_column[...]
    )

    def column(s, part, k):
        at = s * 16 + part * 8 + k
        return lifted[:, at : at + 1]

    halves = mixed_row(column, weights, 32)
    token[...] = halves[0]
    copies = []
    for half in range(2):
        for i in range(16):
            blocks[half, i] = halves[half]
        for i in range(half, 8, 2):
            copies.append(
                pltpu.make_async_copy(blocks.at[half], out.at[pl.ds(16 * i, 16)], sems.at[i])
            )
            copies[-1].start()
    for copy in copies:
        copy.wait()


def second_mix(arrived, weights, out):
    sums = [None, None]
    for n in range(OWNERS):
        half = n // 16 % 2
        sums[half] = arrived[n] if sums[half] is None else sums[half] + arrived[n]
    stacked = jnp.concatenate(sums + [jnp.zeros((112, 128), F32)], axis=0).T

    def column(s, part, k):
        at = (s * 2 + part) * 2 + k // 4
        rows = slice(k % 4 * 32, k % 4 * 32 + 32)
        return jnp.concatenate([stacked[rows, at : at + 1], stacked[rows, at + 8 : at + 9]], axis=0)

    (block,) = mixed_row(column, weights, 32)
    for n in range(OWNERS):
        out[n] = block


def invert(arrived, table, out):
    modes = []
    for t in range(4):
        tiles = [arrived[pl.ds(2 * t + u, OWNERS, stride=8), :] for u in range(2)]
        modes.append(jnp.concatenate(tiles, axis=1))
    mh, ml = split(jnp.concatenate(modes, axis=0))
    made = mm(table[...], mh)
    made = made[:128] + made[128:] + mm(table[:128], ml)
    out[0] = made[:, :128]
    out[1] = made[:, 128:]


def coarse_level(
    own, got, pack, fields, z_back, z_fwd,
    kept, sent, values, y_s, rhs_s, g_s, t_s, values_v, sems,
):
    core = lax.axis_index("gx") % 2
    for t in range(2):
        y_s[2 * core + t] = own[t]
        y_s[2 * (1 - core) + t] = got[t]
    for h in range(2):
        for t in range(2):
            for q in range(2):
                made = regroup(
                    [y_s[2 * h + t, pl.ds(4 * q + u, 16, stride=8), :] for u in range(4)]
                )
                for v in range(4):
                    rhs_s[2 * q + h, pl.ds(16 * (4 * t + v), 16), :] = made[v]

    def step(p, carry):
        rows = [rhs_s[t, pl.ds(p, 16, stride=8), :] for t in range(4)]
        high, less = split(jnp.concatenate(rows, axis=1))
        pooled = []
        for ch in range(CIN):
            total = jnp.zeros((8, 128), F32)
            for dx in range(2):
                for dy in range(2):
                    total += fields[ch, 2 * p + dx, pl.ds(dy, 8, stride=2), :]
            pooled.append(total * 0.25)
        ph, pll = split(jnp.concatenate(pooled, axis=0))
        left = jnp.concatenate([z_back[...], ph, ph, pll], axis=0)
        right = jnp.concatenate([high, less, high, pack[...]], axis=0)
        value = gelu(mm(left, right, ((0,), (0,))))
        vh, vl = split(value)
        made = mm(z_fwd[...], jnp.concatenate([vh, vl], axis=0))
        made = made[:16] + made[16:]
        for t in range(4):
            at = slice(128 * t, 128 * t + 128)
            g_s[t, pl.ds(pl.multiple_of(p * 8, 8), 8), :] = made[:8, at]
            g_s[t, pl.ds(pl.multiple_of(p * 8 + 64, 8), 8), :] = made[8:, at]
        values_v[p, 0] = vh
        values_v[p, 1] = vl
        pltpu.make_async_copy(values_v.at[p], values.at[p], sems.at[p]).start()
        return carry

    lax.fori_loop(0, 8, step, 0, unroll=UNROLL)
    for h in range(2):
        for t in range(2):
            for q in range(2):
                made = regroup(
                    [g_s[2 * q + h, pl.ds(4 * t + v, 16, stride=8), :] for v in range(4)]
                )
                for u in range(4):
                    t_s[2 * h + t, pl.ds(4 * q + u, 16, stride=8), :] = made[u]
    for t in range(2):
        kept[t] = t_s[2 * core + t]
        sent[t] = t_s[2 * (1 - core) + t]
    for p in range(8):
        pltpu.make_async_copy(values_v.at[p], values.at[p], sems.at[p]).wait()


def spread(kept, got, table, out, token, out_v, sems):
    rows = [jnp.concatenate([ref[0], ref[1]], axis=1) for ref in (kept, got)]
    th, tl = split(jnp.concatenate(rows, axis=0))
    copies = []
    for j in range(4):
        ah, al = [
            jnp.concatenate([table[i, pl.ds(128 * t + 32 * j, 32)] for t in range(4)], axis=0)
            for i in range(2)
        ]
        made = mm(ah, th) + mm(ah, tl) + mm(al, th)
        for t in range(4):
            for u in range(2):
                piece = made[32 * t : 32 * t + 32, 128 * u : 128 * u + 128]
                out_v[pl.ds(256 * j + 2 * t + u, 32, stride=8), :] = piece
        rows = pl.ds(256 * j, 256)
        copies.append(pltpu.make_async_copy(out_v.at[rows], out.at[rows], sems.at[j]))
        copies[-1].start()
    token[...] = out_v[:8]
    for copy in copies:
        copy.wait()


def fine_level(
    arrived, table, z_back_h, skip, project_h, bias_h, base_h, out, base, out_v,
    y_s, rhs_s, skip_v, z_back, project_mix, bias_mix, sems, base_sems, out_sems,):
    def taken(p):
        rows = pl.ds(2 * p, 2)
        return (
            pltpu.make_async_copy(skip.at[p], skip_v.at[p], sems.at[p]),
            pltpu.make_async_copy(base_h.at[:, rows], base.at[:, rows], base_sems.at[p]),
        )

    def given(p):
        rows = pl.ds(2 * p, 2)
        return pltpu.make_async_copy(out_v.at[:, rows], out.at[:, rows], out_sems.at[p])

    small = [
        pltpu.make_async_copy(source, target, sems.at[i])
        for i, source, target in (
            (8, z_back_h, z_back), (9, project_h, project_mix), (10, bias_h, bias_mix)
        )
    ]
    for copy in small:
        copy.start()
    for p in range(8):
        for copy in taken(p):
            copy.start()
    modes = []
    for t in range(4):
        tiles = [arrived[pl.ds(2 * t + u, OWNERS, stride=8), :] for u in range(2)]
        modes.append(jnp.concatenate(tiles, axis=1))
    mh, ml = split(jnp.concatenate(modes, axis=0))
    for t in range(4):
        at = slice(128 * t, 128 * t + 128)
        made = mm(table[0, at], mh) + mm(table[0, at], ml) + mm(table[1, at], mh)
        y_s[0, at] = made[:, :128]
        y_s[1, at] = made[:, 128:]
    for t in range(2):
        for y in range(4):
            made = regroup([y_s[t, pl.ds(4 * y + u, 32, stride=16), :] for u in range(4)])
            for v in range(4):
                rhs_s[y, pl.ds(32 * (4 * t + v), 32), :] = made[v]
    for copy in small:
        copy.wait()

    def step(p, carry):
        for copy in taken(p):
            copy.wait()
        for x in (2 * p, 2 * p + 1):
            rows = [rhs_s[t, pl.ds(x, 16, stride=16), :] for t in range(4)]
            high, less = split(jnp.concatenate(rows, axis=1))
            right = jnp.concatenate([high, less, high, bias_mix[...]], axis=0)
            before = mm(z_back[...], right)
            vh, vl = split(gelu(before + skip_v[p]))
            made = mm(project_mix[...], vh, ((1,), (1,)))
            made = made[:64] + made[64:] + mm(project_mix[:64], vl, ((1,), (1,)))
            for o in range(CIN):
                out_v[o, x] = made[16 * o : 16 * o + 16] + base[o, x]
        given(p).start()
        return carry

    lax.fori_loop(0, 8, step, 0, unroll=FINE_UNROLL)
    for p in range(8):
        given(p).wait()


def exchange(tiles):
    return lax.all_to_all(tiles, AXES, split_axis=0, concat_axis=0, tiled=True)


def between_cores(array):
    return lax.ppermute(array, "gx", [(i, i ^ 1) for i in range(lax.axis_size("gx"))])


def stay(array):
    return pltpu.with_memory_space_constraint(array, pltpu.HBM)


def on_device(
    fields, lift, lift_bias, spectral_in, bypass_in, bias_in, spectral_out, bypass_out, bias_out,
    project, project_bias,
):
    waves, steps = wave_tables(), phase_steps()
    z_back, z_fwd = inverse_z_table(), forward_z_table()
    call = functools.partial(pl.pallas_call, compiler_params=PARAMS)
    shape = jax.ShapeDtypeStruct
    dma = pltpu.SemaphoreType.DMA
    work = pl.CostEstimate(flops=1 << 31, transcendentals=0, bytes_accessed=6 << 20)
    spectrum, token = pl.pallas_call(
        first_spectrum,
        out_shape=(shape((OWNERS, 128), F32), shape((8, 128), F32)),
        in_specs=[HBM] * 4, out_specs=(VMEM, VMEM),
        scratch_shapes=[
            pltpu.VMEM((CIN, 16, 16, NZ), F32), pltpu.VMEM((CIN, 384, 128), BF16),
            pltpu.VMEM((2, 512, 256), BF16), pltpu.VMEM((2, 512), jnp.int32), dma((10,)),
        ],
        name="first_spectrum", compiler_params=ALONE,
    )(fields, first_z_table(), first_places_table(), steps)
    prepared = call(
        prepare_mix,
        out_shape=(
            shape((2, 2, KZ, C1, C2), F32), shape((C1, 128), F32), shape((C1, 32), F32),
        ),
        in_specs=[VMEM, HBM, VMEM, VMEM], out_specs=(VMEM,) * 3, name="prepare_mix",
        scratch_shapes=[dma(())], cost_estimate=work,
    )(token, stay(spectral_in), lift, lift_bias[:, None])
    arrived, prepared = lax.optimization_barrier((exchange(spectrum), prepared))
    weights, lift_wide, bias_column = prepared
    mixed, token = call(
        first_mix,
        out_shape=(pltpu.HBM((OWNERS, 8, 128), F32), shape((8, 128), F32)),
        in_specs=[VMEM] * 4, out_specs=(HBM, VMEM), name="first_mix",
        scratch_shapes=[pltpu.VMEM((2, 16, 8, 128), F32), dma((8,))],
    )(arrived, lift_wide, bias_column, weights)
    prepared = call(
        prepare,
        out_shape=(
            shape((256, 512), BF16), shape((256, 512), BF16), shape((2, 512, 256), BF16),
            shape((112, 512), BF16), pltpu.HBM((2, 512, 512), BF16), pltpu.HBM((256, 512), BF16),
            pltpu.HBM((128, 512), BF16), pltpu.HBM((16, 512), BF16),
        ),
        in_specs=[VMEM] * 10, out_specs=(VMEM,) * 8, name="prepare", cost_estimate=work,
    )(
        token, waves, steps, lift, lift_bias[None], bypass_in, bias_in[None], bypass_out,
        bias_out[None], project,
    )
    mine, prepared = lax.optimization_barrier((exchange(mixed), prepared))
    own_t, mate_t, spread_t, pack, fine_t, wide_mix, project_mix, bias_mix = prepared
    mine = mine.reshape(OWNERS * 8, 128)
    own, got = [
        call(
            invert, out_shape=shape((2, 128, 128), F32), in_specs=[VMEM] * 2, out_specs=VMEM,
            name=name, cost_estimate=work,
        )(mine, table)
        for name, table in (("invert_own", own_t), ("invert_mate", mate_t))
    ]
    kept, sent, values = call(
        coarse_level,
        out_shape=(
            shape((2, 128, 128), F32), shape((2, 128, 128), F32),
            pltpu.HBM((8, 2, NZ, 512), BF16),
        ),
        in_specs=[VMEM] * 6, out_specs=(VMEM, VMEM, HBM), name="coarse_level",
        scratch_shapes=[pltpu.VMEM((4, 128, 128), F32)] * 4
        + [pltpu.VMEM((8, 2, NZ, 512), BF16), dma((8,))],
    )(
        own, between_cores(got), pack, fields, z_back, z_fwd,
    )
    spectrum, token = call(
        spread,
        out_shape=(pltpu.HBM((OWNERS * 8, 128), F32), shape((8, 128), F32)),
        in_specs=[VMEM] * 3, out_specs=(HBM, VMEM), name="spread",
        scratch_shapes=[pltpu.VMEM((OWNERS * 8, 128), F32), dma((4,))],
    )(kept, between_cores(sent), spread_t)
    prepared = call(
        bypass,
        out_shape=(pltpu.HBM((8, NZ, 512), F32), pltpu.HBM((CIN, 16, 16, NZ), F32)),
        in_specs=[VMEM, HBM, HBM] + [VMEM] * 5, out_specs=(HBM, VMEM), name="bypass",
        scratch_shapes=[
            pltpu.VMEM((8, 2, NZ, 512), BF16), pltpu.VMEM((8, NZ, 512), F32),
            pltpu.VMEM((256, 512), BF16), dma((9,)), dma((8,)),
        ],
        cost_estimate=work,
    )(
        token, stay(values), stay(wide_mix), fields, lift, lift_bias[None], project,
        project_bias[:, None],
    )
    arrived, prepared = lax.optimization_barrier(
        (exchange(spectrum.reshape(OWNERS, 8, 128)), prepared)
    )
    skip, base = prepared
    mixed = call(
        second_mix,
        out_shape=shape((OWNERS, 8, 128), F32),
        in_specs=[VMEM, VMEM], out_specs=VMEM, name="second_mix",
    )(arrived, spectral_out)
    return call(
        fine_level,
        out_shape=shape((CIN, 16, 16, NZ), F32),
        in_specs=[VMEM, VMEM] + [HBM] * 5, out_specs=HBM, name="fine_level",
        scratch_shapes=[
            pltpu.VMEM((CIN, 16, 16, NZ), F32), pltpu.VMEM((CIN, 16, 16, NZ), F32),
            pltpu.VMEM((2, 512, 128), F32), pltpu.VMEM((4, 256, 128), F32),
            pltpu.VMEM((8, NZ, 512), F32), pltpu.VMEM((NZ, 64), BF16),
            pltpu.VMEM((128, 512), BF16), pltpu.VMEM((16, 512), BF16), dma((11,)), dma((8,)),
            dma((8,)),
        ],
    )(
        exchange(mixed).reshape(OWNERS * 8, 128), fine_t, stay(jnp.asarray(z_back.T)), stay(skip),
        stay(project_mix), stay(bias_mix), stay(base),
    )


def solution(mesh):
    owned = P(AXES, None, None, None, None)
    grid = P(None, "gx", "gy", None)
    in_specs = (grid, P(), P(), owned, P(), P(), owned, P(), P(), P(), P())
    return jax.shard_map(
        on_device, mesh=mesh, in_specs=in_specs, out_specs=grid, check_vma=False
    )
```

```python
import functools
import math

import jax
import jax.numpy as jnp
import numpy as np
from jax import lax
from jax.experimental import pallas as pl
from jax.experimental.pallas import tpu as pltpu
from jax.sharding import PartitionSpec as P

KX, KY, KZ = 16, 16, 8
NX, NY, NZ = 128, 256, 128
CIN, C1, C2 = 4, 32, 64
AXES = ("gx", "gy")
OWNERS = 128
TOTAL = NX * NY * NZ
BACK = math.sqrt(2.0 / (KX * KY * KZ))
F32 = jnp.float32
BF16 = jnp.bfloat16
UNROLL = 8
FINE_GROUP = 4
VMEM = pl.BlockSpec(memory_space=pltpu.VMEM)
HBM = pl.BlockSpec(memory_space=pltpu.HBM)
PARAMS = pltpu.CompilerParams(vmem_limit_bytes=16 << 20)
ALONE = pltpu.CompilerParams(vmem_limit_bytes=60 << 20)


def mode_frequencies():
    centered = np.where(np.arange(16) < 8, np.arange(16), np.arange(16) - 16)
    n = np.arange(OWNERS)
    fx = np.stack([centered[n // 8]] * 2)
    fy = np.stack([centered[2 * (n % 8) + s] for s in range(2)])
    return fx, fy


def place_angles(xs, ys, x_length, y_length):
    fx, fy = mode_frequencies()
    turns = (
        fx[:, :, None, None] * xs[None, None, :, None] / x_length
        + fy[:, :, None, None] * ys[None, None, None, :] / y_length
    )
    return 2.0 * np.pi * turns


def wave_tables():
    fx, fy = mode_frequencies()
    ahead = np.array([0.0, 0.5 * np.pi])[None, None, :, None]
    places = np.arange(16)[:, None, None, None]
    along_x = 2.0 * np.pi * places * fx[None, :, None, :] / NX + ahead
    along_y = 2.0 * np.pi * places * fy[None, :, None, :] / NY + 0.0 * ahead
    tables = [np.cos(along_x), np.sin(along_x), np.cos(along_y), np.sin(along_y)]
    return np.stack(tables).reshape(4, 16, 512).astype(np.float32)


def phase_steps():
    fx, fy = mode_frequencies()
    steps = np.stack([np.stack([2 * fx, 2 * fx], axis=1), np.stack([fy, fy], axis=1)])
    return steps.reshape(2, 512).astype(np.int32)


def z_angles():
    return 2.0 * np.pi * (np.arange(NZ)[:, None] * np.arange(KZ)[None, :] % NZ) / NZ


def split_np(table):
    high = table.astype(BF16)
    low = (table - high.astype(np.float32)).astype(BF16)
    return high, low


def first_z_table():
    c, s = np.cos(z_angles()), np.sin(z_angles())
    parts = np.array([[c, -s], [-s, -c]])
    table = np.zeros((CIN, NZ, 2, 2, KZ, CIN))
    for ch in range(CIN):
        table[ch, :, :, :, :, ch] = parts.transpose(2, 0, 1, 3)
    high, low = split_np(table.reshape(CIN, NZ, 128).astype(np.float32))
    return np.concatenate([high, high, low], axis=1)


def first_places_table():
    fx, fy = mode_frequencies()
    places = np.arange(16)
    turns = (
        fx[:, :, None, None] * places[:, None] / NX + fy[:, :, None, None] * places[None, :] / NY
    )
    angles = 2.0 * np.pi * turns
    table = np.stack([np.cos(angles), np.sin(angles)], axis=1) / math.sqrt(TOTAL)
    return np.stack(split_np(table.reshape(512, 256).astype(np.float32)))


def inverse_z_table():
    table = np.stack([np.cos(z_angles()), -np.sin(z_angles())], axis=2)
    high, low = split_np(table.reshape(NZ, 16).astype(np.float32))
    ones = np.zeros((16, NZ), BF16)
    ones[:3] = 1.0
    return np.concatenate([high.T, high.T, low.T, ones], axis=0)


def fine_z_table():
    table = np.kron(np.eye(FINE_GROUP), inverse_z_table().T.astype(np.float32))
    return table.astype(BF16)


def forward_z_table():
    table = np.stack([np.cos(z_angles()).T, -np.sin(z_angles()).T], axis=0)
    high, low = split_np(table.reshape(16, NZ).astype(np.float32))
    return np.block([[high, high], [low, np.zeros_like(low)]])


def split(x):
    high = x.astype(BF16)
    return high, (x - high.astype(F32)).astype(BF16)


def bias_rows(bias):
    high, less = split(bias)
    least = (bias - high.astype(F32) - less.astype(F32)).astype(BF16)
    row = iota((16, bias.shape[1]), 0)
    rows = [v.astype(F32) for v in (high, less, least)]
    total = jnp.where(row == 0, rows[0], jnp.where(row == 1, rows[1], rows[2]))
    return jnp.where(row < 3, total, 0.0).astype(BF16)


def mm(a, b, dims=((1,), (0,))):
    return lax.dot_general(a, b, (dims, ((), ())), preferred_element_type=F32)


def mm3(a, b, dims=((1,), (0,))):
    ah, al = split(a)
    bh, bl = split(b)
    return mm(ah, bh, dims) + mm(ah, bl, dims) + mm(al, bh, dims)


def exact(a, b, dims=((1,), (0,))):
    return lax.dot_general(
        a, b, (dims, ((), ())), precision=lax.Precision.HIGHEST, preferred_element_type=F32
    )


def iota(shape, dim):
    return lax.broadcasted_iota(jnp.int32, shape, dim)


def ones_where(condition):
    return jnp.where(condition, 1.0, 0.0).astype(F32)


def gelu(x):
    return 0.5 * x * (1.0 + lax.erf(x * math.sqrt(0.5)))


def regroup(rows):
    group = iota(rows[0].shape, 1) // 32
    made = []
    for v in range(4):
        total = rows[v]
        for u in range(4):
            if u != v:
                moved = pltpu.roll(rows[u], ((u - v) % 4) * 32, 1)
                total = jnp.where(group == u, moved, total)
        made.append(total)
    return made


def my_place():
    return lax.axis_index("gx"), lax.axis_index("gy")


def phases(steps, place):
    turns = (steps[0:1] * place[0] + steps[1:2] * place[1]) & 15
    angle = turns.astype(F32) * (2.0 * math.pi / 16)
    return jnp.cos(angle), jnp.sin(angle)


def device_waves(waves, steps, place):
    cos, sin = phases(steps, place)
    return waves[0] * cos - waves[1] * sin, waves[1] * cos + waves[0] * sin


def wave_rows(along_x, cos_y, sin_y, xs):
    cos_x, sin_x = along_x
    real = [cos_x[x : x + 1] * cos_y - sin_x[x : x + 1] * sin_y for x in xs]
    imag = [sin_x[x : x + 1] * cos_y + cos_x[x : x + 1] * sin_y for x in xs]
    return jnp.concatenate(real, axis=0), jnp.concatenate(imag, axis=0)


def first_spectrum(
    fields, ztab_h, ptab_h, steps_h, out, token, fields_v, ztab, ptab, steps, sems,
):
    pairs = [(steps_h, steps)]
    for ch in range(CIN):
        pairs += [(fields.at[ch], fields_v.at[ch]), (ztab_h.at[ch], ztab.at[ch])]
    pairs.append((ptab_h, ptab))
    copies = [
        pltpu.make_async_copy(source, target, sems.at[i])
        for i, (source, target) in enumerate(pairs)
    ]
    for copy in copies:
        copy.start()
    copies[0].wait()
    cos, sin = phases(steps, my_place())
    turn = [v[:, at : at + 128] for at in (0, 256) for v in (cos, sin)]
    turn = jnp.concatenate(turn + [jnp.zeros((124, 128), F32)], axis=0).T
    total = None
    for ch in range(CIN):
        copies[1 + 2 * ch].wait()
        copies[2 + 2 * ch].wait()
        fh, fl = split(fields_v[ch].reshape(256, NZ))
        term = mm(jnp.concatenate([fh, fl], axis=1), ztab[ch, :256]) + mm(fh, ztab[ch, 256:])
        total = term if total is None else total + term
    copies[-1].wait()
    th, tl = split(total)
    both = mm(ptab[0], th) + mm(ptab[0], tl) + mm(ptab[1], th)
    low = iota((128, 128), 1) < 64
    rows = []
    for s in range(2):
        part_cos = both[256 * s : 256 * s + 128]
        part_sin = both[256 * s + 128 : 256 * s + 256]
        part_sin = pltpu.roll(part_sin, 64, 1)
        pair = jnp.where(low, part_cos + part_sin, part_cos - part_sin)
        cos_s, sin_s = turn[:, 2 * s : 2 * s + 1], turn[:, 2 * s + 1 : 2 * s + 2]
        rows.append(cos_s * pair + sin_s * pltpu.roll(pair, 64, 1))
    out[...] = jnp.where(low, rows[0], pltpu.roll(rows[1], 64, 1))
    token[...] = rows[0][:8]


def prepare_mix(after, weights, lift, lift_bias, weights_v, lift_wide, bias_column, sem):
    copy = pltpu.make_async_copy(weights, weights_v, sem)
    copy.start()
    lift_wide[...] = exact(lift[...], ones_where(iota((CIN, 128), 0) == iota((CIN, 128), 1) % 4))
    gx, gy = my_place()
    at_zero = (iota((C1, 32), 1) + gx + gy) == 0
    bias_column[...] = jnp.where(at_zero, lift_bias[...] * math.sqrt(TOTAL), 0.0)
    copy.wait()


def prepare(
    after, waves, steps, lift, lift_bias, bypass_in, bias_in, bypass_out, bias_out, project,
    own_t, mate_t, spread_t, pack, fine_t, wide_mix, project_mix, bias_mix,
):
    nt = ((1,), (1,))
    gx, gy = my_place()
    own = device_waves(waves, steps, (gx, gy))
    mate = device_waves(waves, steps, (gx + 1 - 2 * (gx % 2), gy))
    cos_y = jnp.concatenate([waves[2, 2 * q : 2 * q + 1] for q in range(8)], axis=0)
    sin_y = jnp.concatenate([waves[3, 2 * q : 2 * q + 1] for q in range(8)], axis=0)
    tables = [
        jnp.concatenate(wave_rows(along, cos_y, sin_y, range(0, 16, 2)), axis=0)
        for along in (own, mate)
    ]
    own_t[0:128], own_t[128:256] = split(tables[0] * BACK)
    mate_t[0:128], mate_t[128:256] = split(tables[1] * BACK)
    scale = 1.0 / math.sqrt(TOTAL / 4.0)
    for patch in range(2):
        at = slice(128 * patch, 128 * patch + 128)
        high, less = split(tables[patch].T * scale)
        spread_t[0, :, at] = high
        spread_t[1, :, at] = less
    lanes = [
        ones_where(iota((C2, 128), 0) == 32 * h + iota((C2, 128), 1) % 32) for h in range(2)
    ]
    through = exact(lift[...], bypass_in[...], ((0,), (1,)))
    through = exact(ones_where(iota((32, CIN), 0) // 8 == iota((32, CIN), 1)), through)
    offset = bias_in[...] + exact(lift_bias[...], bypass_in[...], nt)
    for t in range(4):
        at = slice(128 * t, 128 * t + 128)
        same = iota((32, 128), 0) % 8 == 4 * (t // 2) + iota((32, 128), 1) // 32
        high, less = split(jnp.where(same, exact(through, lanes[t % 2]), 0.0))
        rows = bias_rows(exact(offset, lanes[t % 2]))
        pack[:, at] = jnp.concatenate([rows, high, less, high], axis=0)
    spread_d = ones_where(iota((C1, 256), 0) == iota((C1, 256), 1) % 32)
    same = iota((128, 256), 0) // 32 == iota((128, 256), 1) // 64
    for h in range(2):
        pick = ones_where(iota((128, C2), 1) == 32 * h + iota((128, C2), 0) % 32)
        wide = exact(exact(pick, bypass_out[...], nt), spread_d)
        high, less = split(jnp.where(same, wide, 0.0))
        wide_mix[128 * h : 128 * h + 128] = jnp.concatenate([high, less], axis=1)
    scaled = (own[0] * BACK, own[1] * BACK)
    for x in range(0, 16, 8):
        pair = wave_rows(scaled, waves[2], waves[3], range(x, x + 8))
        for part in range(2):
            at = slice(256 * part + 16 * x, 256 * part + 16 * x + 128)
            high, less = split(pair[part])
            fine_t[0, at] = high
            fine_t[1, at] = less
    lanes = ones_where(iota((C1, 512), 0) == iota((C1, 512), 1) % 32)
    bias_mix[...] = bias_rows(exact(bias_out[...], lanes))
    pick = ones_where(iota((512, C1), 1) == iota((512, C1), 0) % 32)
    onto = ones_where(iota((CIN, 128), 0) == iota((CIN, 128), 1) % 64 // 16)
    made = exact(exact(pick, project[...], nt), onto)
    lane = iota((512, 128), 1)
    made = jnp.where(iota((512, 128), 0) // 32 == lane % 16, made, 0.0)
    high = made.astype(BF16).astype(F32)
    project_mix[...] = jnp.where(lane < 64, high, made - high).T.astype(BF16)


def bypass(
    after, values, wide_mix_h, fields, lift, lift_bias, project, project_bias, skip, base,
    values_v, skip_v, wide_mix, in_sems, out_sems,
):
    def taken(p):
        return pltpu.make_async_copy(values.at[p], values_v.at[p], in_sems.at[p])

    def given(p):
        return pltpu.make_async_copy(skip_v.at[p], skip.at[p], out_sems.at[p])

    mix_copy = pltpu.make_async_copy(wide_mix_h, wide_mix, in_sems.at[8])
    mix_copy.start()
    for p in range(8):
        taken(p).start()
    across = exact(project[...], lift[...])
    constant = project_bias[...] + exact(project[...], lift_bias[...], ((1,), (1,)))
    mix_copy.wait()

    def step(x, carry):
        for o in range(CIN):
            total = jnp.broadcast_to(constant[o : o + 1], (16, NZ))
            for ch in range(CIN):
                total += across[o : o + 1, ch : ch + 1] * fields[ch, x]
            base[o, x] = total
        return carry

    lax.fori_loop(0, 16, step, 0)

    def wide_step(p, carry):
        taken(p).wait()
        for q in range(2):
            at = slice(256 * q, 256 * q + 256)
            high, less = values_v[p, 0, :, at], values_v[p, 1, :, at]
            wide = mm(high, wide_mix[:, :256]) + mm(high, wide_mix[:, 256:])
            skip_v[p, :, at] = wide + mm(less, wide_mix[:, :256])
        given(p).start()
        return carry

    lax.fori_loop(0, 8, wide_step, 0, unroll=2)
    for p in range(8):
        given(p).wait()


def mixed_row(columns, weights, wide):
    pieces = [[[None] * KZ for _ in range(2)] for _ in range(2)]
    for s in range(2):
        for k in range(KZ):
            real, imag = columns(s, 0, k), columns(s, 1, k)
            wr, wi = weights[s, 0, k], weights[s, 1, k]
            pieces[s][0][k] = jnp.sum(real * wr - imag * wi, axis=0, keepdims=True)
            pieces[s][1][k] = jnp.sum(real * wi + imag * wr, axis=0, keepdims=True)
    per = 128 // wide
    return [
        jnp.concatenate(
            [
                jnp.concatenate(
                    [v[:, at : at + wide] for v in pieces[s][part][k : k + per]], axis=1
                )
                for s in range(2)
                for part in range(2)
                for k in range(0, KZ, per)
            ],
            axis=0,
        )
        for at in range(0, weights.shape[-1], wide)
    ]


def first_mix(arrived, lift_wide, bias_column, weights, out, token, blocks, sems):
    row = jnp.sum(arrived[...], axis=0, keepdims=True)
    source = lax.broadcasted_iota(jnp.int32, (128, 32), 0) // CIN
    pick = (source == lax.broadcasted_iota(jnp.int32, (128, 32), 1)).astype(F32)
    lifted = (
        lax.dot_general(
            lift_wide[...] * row, pick, (((1,), (0,)), ((), ())),
            precision=lax.Precision.HIGHEST, preferred_element_type=F32,
        )
        + bias_column[...]
    )

    def column(s, part, k):
        at = s * 16 + part * 8 + k
        return lifted[:, at : at + 1]

    halves = mixed_row(column, weights, 32)
    token[...] = halves[0]
    copies = []
    for half in range(2):
        for i in range(16):
            blocks[half, i] = halves[half]
        for i in range(half, 8, 2):
            copies.append(
                pltpu.make_async_copy(blocks.at[half], out.at[pl.ds(16 * i, 16)], sems.at[i])
            )
            copies[-1].start()
    for copy in copies:
        copy.wait()


def second_mix(arrived, weights, out):
    sums = [None, None]
    for n in range(OWNERS):
        half = n // 16 % 2
        sums[half] = arrived[n] if sums[half] is None else sums[half] + arrived[n]
    stacked = jnp.concatenate(sums + [jnp.zeros((112, 128), F32)], axis=0).T

    def column(s, part, k):
        at = (s * 2 + part) * 2 + k // 4
        rows = slice(k % 4 * 32, k % 4 * 32 + 32)
        return jnp.concatenate([stacked[rows, at : at + 1], stacked[rows, at + 8 : at + 9]], axis=0)

    (block,) = mixed_row(column, weights, 32)
    for n in range(OWNERS):
        out[n] = block


def invert(arrived, table, out):
    modes = []
    for t in range(4):
        tiles = [arrived[pl.ds(2 * t + u, OWNERS, stride=8), :] for u in range(2)]
        modes.append(jnp.concatenate(tiles, axis=1))
    mh, ml = split(jnp.concatenate(modes, axis=0))
    made = mm(table[...], mh)
    made = made[:128] + made[128:] + mm(table[:128], ml)
    out[0] = made[:, :128]
    out[1] = made[:, 128:]


def coarse_level(
    own, got, pack, fields, z_back, z_fwd,
    kept, sent, values, y_s, rhs_s, g_s, t_s, values_v, sems,
):
    core = lax.axis_index("gx") % 2
    for t in range(2):
        y_s[2 * core + t] = own[t]
        y_s[2 * (1 - core) + t] = got[t]
    for h in range(2):
        for t in range(2):
            for q in range(2):
                made = regroup(
                    [y_s[2 * h + t, pl.ds(4 * q + u, 16, stride=8), :] for u in range(4)]
                )
                for v in range(4):
                    rhs_s[2 * q + h, pl.ds(16 * (4 * t + v), 16), :] = made[v]

    def step(p, carry):
        rows = [rhs_s[t, pl.ds(p, 16, stride=8), :] for t in range(4)]
        high, less = split(jnp.concatenate(rows, axis=1))
        pooled = []
        for ch in range(CIN):
            total = jnp.zeros((8, 128), F32)
            for dx in range(2):
                for dy in range(2):
                    total += fields[ch, 2 * p + dx, pl.ds(dy, 8, stride=2), :]
            pooled.append(total * 0.25)
        ph, pll = split(jnp.concatenate(pooled, axis=0))
        left = jnp.concatenate([z_back[...], ph, ph, pll], axis=0)
        right = jnp.concatenate([high, less, high, pack[...]], axis=0)
        value = gelu(mm(left, right, ((0,), (0,))))
        vh, vl = split(value)
        made = mm(z_fwd[...], jnp.concatenate([vh, vl], axis=0))
        made = made[:16] + made[16:]
        for t in range(4):
            at = slice(128 * t, 128 * t + 128)
            g_s[t, pl.ds(pl.multiple_of(p * 8, 8), 8), :] = made[:8, at]
            g_s[t, pl.ds(pl.multiple_of(p * 8 + 64, 8), 8), :] = made[8:, at]
        values_v[p, 0] = vh
        values_v[p, 1] = vl
        pltpu.make_async_copy(values_v.at[p], values.at[p], sems.at[p]).start()
        return carry

    lax.fori_loop(0, 8, step, 0, unroll=UNROLL)
    for h in range(2):
        for t in range(2):
            for q in range(2):
                made = regroup(
                    [g_s[2 * q + h, pl.ds(4 * t + v, 16, stride=8), :] for v in range(4)]
                )
                for u in range(4):
                    t_s[2 * h + t, pl.ds(4 * q + u, 16, stride=8), :] = made[u]
    for t in range(2):
        kept[t] = t_s[2 * core + t]
        sent[t] = t_s[2 * (1 - core) + t]
    for p in range(8):
        pltpu.make_async_copy(values_v.at[p], values.at[p], sems.at[p]).wait()


def spread(kept, got, table, out, token, out_v, sems):
    rows = [jnp.concatenate([ref[0], ref[1]], axis=1) for ref in (kept, got)]
    th, tl = split(jnp.concatenate(rows, axis=0))
    copies = []
    for j in range(4):
        ah, al = [
            jnp.concatenate([table[i, pl.ds(128 * t + 32 * j, 32)] for t in range(4)], axis=0)
            for i in range(2)
        ]
        made = mm(ah, th) + mm(ah, tl) + mm(al, th)
        for t in range(4):
            for u in range(2):
                piece = made[32 * t : 32 * t + 32, 128 * u : 128 * u + 128]
                out_v[pl.ds(256 * j + 2 * t + u, 32, stride=8), :] = piece
        rows = pl.ds(256 * j, 256)
        copies.append(pltpu.make_async_copy(out_v.at[rows], out.at[rows], sems.at[j]))
        copies[-1].start()
    token[...] = out_v[:8]
    for copy in copies:
        copy.wait()


def fine_level(
    arrived, table, z_back_h, skip, project_h, bias_h, base_h, out, base, out_v,
    y_s, rhs_s, skip_v, z_back, project_mix, bias_mix, sems, base_sems, out_sems,):
    def taken(p):
        rows = pl.ds(2 * p, 2)
        return (
            pltpu.make_async_copy(skip.at[p], skip_v.at[p], sems.at[p]),
            pltpu.make_async_copy(base_h.at[:, rows], base.at[:, rows], base_sems.at[p]),
        )

    def given(p):
        rows = pl.ds(2 * p, 2)
        return pltpu.make_async_copy(out_v.at[:, rows], out.at[:, rows], out_sems.at[p])

    small = [
        pltpu.make_async_copy(source, target, sems.at[i])
        for i, source, target in (
            (8, z_back_h, z_back), (9, project_h, project_mix), (10, bias_h, bias_mix)
        )
    ]
    for copy in small:
        copy.start()
    for p in range(8):
        for copy in taken(p):
            copy.start()
    modes = []
    for t in range(4):
        tiles = [arrived[pl.ds(2 * t + u, OWNERS, stride=8), :] for u in range(2)]
        modes.append(jnp.concatenate(tiles, axis=1))
    mh, ml = split(jnp.concatenate(modes, axis=0))
    for t in range(4):
        at = slice(128 * t, 128 * t + 128)
        made = mm(table[0, at], mh) + mm(table[0, at], ml) + mm(table[1, at], mh)
        y_s[0, at] = made[:, :128]
        y_s[1, at] = made[:, 128:]
    for t in range(2):
        for y in range(4):
            made = regroup([y_s[t, pl.ds(4 * y + u, 32, stride=16), :] for u in range(4)])
            for v in range(4):
                rhs_s[y, pl.ds(32 * (4 * t + v), 32), :] = made[v]
    for copy in small:
        copy.wait()

    def step(i, carry):
        rights = []
        for u in range(FINE_GROUP):
            x = FINE_GROUP * i + u
            rows = [rhs_s[t, pl.ds(x, 16, stride=16), :] for t in range(4)]
            high, less = split(jnp.concatenate(rows, axis=1))
            rights += [high, less, high, bias_mix[...]]
        before = mm(z_back[...], jnp.concatenate(rights, axis=0))
        for v in range(FINE_GROUP // 2):
            p = FINE_GROUP // 2 * i + v
            for copy in taken(p):
                copy.wait()
        skips = [skip_v[FINE_GROUP // 2 * i + u // 2] for u in range(FINE_GROUP)]
        vh, vl = split(gelu(before + jnp.concatenate(skips, axis=0)))
        made = mm(project_mix[...], vh, ((1,), (1,)))
        made = made[:64] + made[64:] + mm(project_mix[:64], vl, ((1,), (1,)))
        for u in range(FINE_GROUP):
            x = FINE_GROUP * i + u
            for o in range(CIN):
                piece = made[16 * o : 16 * o + 16, 128 * u : 128 * u + 128]
                out_v[o, x] = piece + base[o, x]
        for v in range(FINE_GROUP // 2):
            given(FINE_GROUP // 2 * i + v).start()
        return carry

    lax.fori_loop(0, 16 // FINE_GROUP, step, 0)
    for p in range(8):
        given(p).wait()


def exchange(tiles):
    return lax.all_to_all(tiles, AXES, split_axis=0, concat_axis=0, tiled=True)


def between_cores(array):
    return lax.ppermute(array, "gx", [(i, i ^ 1) for i in range(lax.axis_size("gx"))])


def stay(array):
    return pltpu.with_memory_space_constraint(array, pltpu.HBM)


def on_device(
    fields, lift, lift_bias, spectral_in, bypass_in, bias_in, spectral_out, bypass_out, bias_out,
    project, project_bias,
):
    waves, steps = wave_tables(), phase_steps()
    z_back, z_fwd = inverse_z_table(), forward_z_table()
    call = functools.partial(pl.pallas_call, compiler_params=PARAMS)
    shape = jax.ShapeDtypeStruct
    dma = pltpu.SemaphoreType.DMA
    work = pl.CostEstimate(flops=1 << 31, transcendentals=0, bytes_accessed=6 << 20)
    spectrum, token = pl.pallas_call(
        first_spectrum,
        out_shape=(shape((OWNERS, 128), F32), shape((8, 128), F32)),
        in_specs=[HBM] * 4, out_specs=(VMEM, VMEM),
        scratch_shapes=[
            pltpu.VMEM((CIN, 16, 16, NZ), F32), pltpu.VMEM((CIN, 384, 128), BF16),
            pltpu.VMEM((2, 512, 256), BF16), pltpu.VMEM((2, 512), jnp.int32), dma((10,)),
        ],
        name="first_spectrum", compiler_params=ALONE,
    )(fields, first_z_table(), first_places_table(), steps)
    prepared = call(
        prepare_mix,
        out_shape=(
            shape((2, 2, KZ, C1, C2), F32), shape((C1, 128), F32), shape((C1, 32), F32),
        ),
        in_specs=[VMEM, HBM, VMEM, VMEM], out_specs=(VMEM,) * 3, name="prepare_mix",
        scratch_shapes=[dma(())], cost_estimate=work,
    )(token, stay(spectral_in), lift, lift_bias[:, None])
    arrived, prepared = lax.optimization_barrier((exchange(spectrum), prepared))
    weights, lift_wide, bias_column = prepared
    mixed, token = call(
        first_mix,
        out_shape=(pltpu.HBM((OWNERS, 8, 128), F32), shape((8, 128), F32)),
        in_specs=[VMEM] * 4, out_specs=(HBM, VMEM), name="first_mix",
        scratch_shapes=[pltpu.VMEM((2, 16, 8, 128), F32), dma((8,))],
    )(arrived, lift_wide, bias_column, weights)
    prepared = call(
        prepare,
        out_shape=(
            shape((256, 512), BF16), shape((256, 512), BF16), shape((2, 512, 256), BF16),
            shape((112, 512), BF16), pltpu.HBM((2, 512, 512), BF16), pltpu.HBM((256, 512), BF16),
            pltpu.HBM((128, 512), BF16), pltpu.HBM((16, 512), BF16),
        ),
        in_specs=[VMEM] * 10, out_specs=(VMEM,) * 8, name="prepare", cost_estimate=work,
    )(
        token, waves, steps, lift, lift_bias[None], bypass_in, bias_in[None], bypass_out,
        bias_out[None], project,
    )
    mine, prepared = lax.optimization_barrier((exchange(mixed), prepared))
    own_t, mate_t, spread_t, pack, fine_t, wide_mix, project_mix, bias_mix = prepared
    mine = mine.reshape(OWNERS * 8, 128)
    own, got = [
        call(
            invert, out_shape=shape((2, 128, 128), F32), in_specs=[VMEM] * 2, out_specs=VMEM,
            name=name, cost_estimate=work,
        )(mine, table)
        for name, table in (("invert_own", own_t), ("invert_mate", mate_t))
    ]
    kept, sent, values = call(
        coarse_level,
        out_shape=(
            shape((2, 128, 128), F32), shape((2, 128, 128), F32),
            pltpu.HBM((8, 2, NZ, 512), BF16),
        ),
        in_specs=[VMEM] * 6, out_specs=(VMEM, VMEM, HBM), name="coarse_level",
        scratch_shapes=[pltpu.VMEM((4, 128, 128), F32)] * 4
        + [pltpu.VMEM((8, 2, NZ, 512), BF16), dma((8,))],
    )(
        own, between_cores(got), pack, fields, z_back, z_fwd,
    )
    spectrum, token = call(
        spread,
        out_shape=(pltpu.HBM((OWNERS * 8, 128), F32), shape((8, 128), F32)),
        in_specs=[VMEM] * 3, out_specs=(HBM, VMEM), name="spread",
        scratch_shapes=[pltpu.VMEM((OWNERS * 8, 128), F32), dma((4,))],
    )(kept, between_cores(sent), spread_t)
    prepared = call(
        bypass,
        out_shape=(pltpu.HBM((8, NZ, 512), F32), pltpu.HBM((CIN, 16, 16, NZ), F32)),
        in_specs=[VMEM, HBM, HBM] + [VMEM] * 5, out_specs=(HBM, VMEM), name="bypass",
        scratch_shapes=[
            pltpu.VMEM((8, 2, NZ, 512), BF16), pltpu.VMEM((8, NZ, 512), F32),
            pltpu.VMEM((256, 512), BF16), dma((9,)), dma((8,)),
        ],
        cost_estimate=work,
    )(
        token, stay(values), stay(wide_mix), fields, lift, lift_bias[None], project,
        project_bias[:, None],
    )
    arrived, prepared = lax.optimization_barrier(
        (exchange(spectrum.reshape(OWNERS, 8, 128)), prepared)
    )
    skip, base = prepared
    mixed = call(
        second_mix,
        out_shape=shape((OWNERS, 8, 128), F32),
        in_specs=[VMEM, VMEM], out_specs=VMEM, name="second_mix",
    )(arrived, spectral_out)
    return call(
        fine_level,
        out_shape=shape((CIN, 16, 16, NZ), F32),
        in_specs=[VMEM, VMEM] + [HBM] * 5, out_specs=HBM, name="fine_level",
        scratch_shapes=[
            pltpu.VMEM((CIN, 16, 16, NZ), F32), pltpu.VMEM((CIN, 16, 16, NZ), F32),
            pltpu.VMEM((2, 512, 128), F32), pltpu.VMEM((4, 256, 128), F32),
            pltpu.VMEM((8, NZ, 512), F32), pltpu.VMEM((NZ * FINE_GROUP, 64 * FINE_GROUP), BF16),
            pltpu.VMEM((128, 512), BF16), pltpu.VMEM((16, 512), BF16), dma((11,)), dma((8,)),
            dma((8,)),
        ],
    )(
        exchange(mixed).reshape(OWNERS * 8, 128), fine_t, stay(jnp.asarray(fine_z_table())), stay(skip),
        stay(project_mix), stay(bias_mix), stay(base),
    )


def solution(mesh):
    owned = P(AXES, None, None, None, None)
    grid = P(None, "gx", "gy", None)
    in_specs = (grid, P(), P(), owned, P(), P(), owned, P(), P(), P(), P())
    return jax.shard_map(
        on_device, mesh=mesh, in_specs=in_specs, out_specs=grid, check_vma=False
    )
```

```python
import functools
import math

import jax
import jax.numpy as jnp
import numpy as np
from jax import lax
from jax.experimental import pallas as pl
from jax.experimental.pallas import tpu as pltpu
from jax.sharding import PartitionSpec as P

KX, KY, KZ = 16, 16, 8
NX, NY, NZ = 128, 256, 128
CIN, C1, C2 = 4, 32, 64
AXES = ("gx", "gy")
OWNERS = 128
TOTAL = NX * NY * NZ
BACK = math.sqrt(2.0 / (KX * KY * KZ))
F32 = jnp.float32
BF16 = jnp.bfloat16
UNROLL = 8
FINE_GROUP = 16
VMEM = pl.BlockSpec(memory_space=pltpu.VMEM)
HBM = pl.BlockSpec(memory_space=pltpu.HBM)
PARAMS = pltpu.CompilerParams(vmem_limit_bytes=16 << 20)
ALONE = pltpu.CompilerParams(vmem_limit_bytes=60 << 20)


def mode_frequencies():
    centered = np.where(np.arange(16) < 8, np.arange(16), np.arange(16) - 16)
    n = np.arange(OWNERS)
    fx = np.stack([centered[n // 8]] * 2)
    fy = np.stack([centered[2 * (n % 8) + s] for s in range(2)])
    return fx, fy


def place_angles(xs, ys, x_length, y_length):
    fx, fy = mode_frequencies()
    turns = (
        fx[:, :, None, None] * xs[None, None, :, None] / x_length
        + fy[:, :, None, None] * ys[None, None, None, :] / y_length
    )
    return 2.0 * np.pi * turns


def wave_tables():
    fx, fy = mode_frequencies()
    ahead = np.array([0.0, 0.5 * np.pi])[None, None, :, None]
    places = np.arange(16)[:, None, None, None]
    along_x = 2.0 * np.pi * places * fx[None, :, None, :] / NX + ahead
    along_y = 2.0 * np.pi * places * fy[None, :, None, :] / NY + 0.0 * ahead
    tables = [np.cos(along_x), np.sin(along_x), np.cos(along_y), np.sin(along_y)]
    return np.stack(tables).reshape(4, 16, 512).astype(np.float32)


def phase_steps():
    fx, fy = mode_frequencies()
    steps = np.stack([np.stack([2 * fx, 2 * fx], axis=1), np.stack([fy, fy], axis=1)])
    return steps.reshape(2, 512).astype(np.int32)


def z_angles():
    return 2.0 * np.pi * (np.arange(NZ)[:, None] * np.arange(KZ)[None, :] % NZ) / NZ


def split_np(table):
    high = table.astype(BF16)
    low = (table - high.astype(np.float32)).astype(BF16)
    return high, low


def first_z_table():
    c, s = np.cos(z_angles()), np.sin(z_angles())
    parts = np.array([[c, -s], [-s, -c]]).transpose(2, 0, 1, 3).reshape(NZ, 32)
    high, low = split_np(np.repeat(parts, CIN, axis=1).astype(np.float32))
    return np.concatenate([high, high, low], axis=0)


def first_places_table():
    fx, fy = mode_frequencies()
    places = np.arange(16)
    turns = (
        fx[:, :, None, None] * places[:, None] / NX + fy[:, :, None, None] * places[None, :] / NY
    )
    angles = 2.0 * np.pi * turns
    table = np.stack([np.cos(angles), np.sin(angles)], axis=1) / math.sqrt(TOTAL)
    return np.stack(split_np(table.reshape(512, 256).astype(np.float32)))


def inverse_z_table():
    table = np.stack([np.cos(z_angles()), -np.sin(z_angles())], axis=2)
    high, low = split_np(table.reshape(NZ, 16).astype(np.float32))
    ones = np.zeros((16, NZ), BF16)
    ones[:3] = 1.0
    return np.concatenate([high.T, high.T, low.T, ones], axis=0)


def fine_z_table():
    table = np.kron(np.eye(4), inverse_z_table().T.astype(np.float32))
    return table.astype(BF16)


def forward_z_table():
    table = np.stack([np.cos(z_angles()).T, -np.sin(z_angles()).T], axis=0)
    high, low = split_np(table.reshape(16, NZ).astype(np.float32))
    return np.block([[high, high], [low, np.zeros_like(low)]])


def split(x):
    high = x.astype(BF16)
    return high, (x - high.astype(F32)).astype(BF16)


def bias_rows(bias):
    high, less = split(bias)
    least = (bias - high.astype(F32) - less.astype(F32)).astype(BF16)
    row = iota((16, bias.shape[1]), 0)
    rows = [v.astype(F32) for v in (high, less, least)]
    total = jnp.where(row == 0, rows[0], jnp.where(row == 1, rows[1], rows[2]))
    return jnp.where(row < 3, total, 0.0).astype(BF16)


def mm(a, b, dims=((1,), (0,))):
    return lax.dot_general(a, b, (dims, ((), ())), preferred_element_type=F32)


def mm3(a, b, dims=((1,), (0,))):
    ah, al = split(a)
    bh, bl = split(b)
    return mm(ah, bh, dims) + mm(ah, bl, dims) + mm(al, bh, dims)


def exact(a, b, dims=((1,), (0,))):
    return lax.dot_general(
        a, b, (dims, ((), ())), precision=lax.Precision.HIGHEST, preferred_element_type=F32
    )


def iota(shape, dim):
    return lax.broadcasted_iota(jnp.int32, shape, dim)


def ones_where(condition):
    return jnp.where(condition, 1.0, 0.0).astype(F32)


def gelu(x):
    return 0.5 * x * (1.0 + lax.erf(x * math.sqrt(0.5)))


def regroup(rows):
    group = iota(rows[0].shape, 1) // 32
    made = []
    for v in range(4):
        total = rows[v]
        for u in range(4):
            if u != v:
                moved = pltpu.roll(rows[u], ((u - v) % 4) * 32, 1)
                total = jnp.where(group == u, moved, total)
        made.append(total)
    return made


def my_place():
    return lax.axis_index("gx"), lax.axis_index("gy")


def phases(steps, place):
    turns = (steps[0:1] * place[0] + steps[1:2] * place[1]) & 15
    angle = turns.astype(F32) * (2.0 * math.pi / 16)
    return jnp.cos(angle), jnp.sin(angle)


def device_waves(waves, steps, place):
    cos, sin = phases(steps, place)
    return waves[0] * cos - waves[1] * sin, waves[1] * cos + waves[0] * sin


def wave_rows(along_x, cos_y, sin_y, xs):
    cos_x, sin_x = along_x
    real = [cos_x[x : x + 1] * cos_y - sin_x[x : x + 1] * sin_y for x in xs]
    imag = [sin_x[x : x + 1] * cos_y + cos_x[x : x + 1] * sin_y for x in xs]
    return jnp.concatenate(real, axis=0), jnp.concatenate(imag, axis=0)


def first_spectrum(
    fields, ztab_h, ptab_h, steps_h, out, token, fields_v, ztab, ptab, steps, sems,
):
    pairs = [(steps_h, steps), (ztab_h, ztab)]
    pairs += [(fields.at[ch], fields_v.at[ch]) for ch in range(CIN)]
    pairs.append((ptab_h, ptab))
    copies = [
        pltpu.make_async_copy(source, target, sems.at[i])
        for i, (source, target) in enumerate(pairs)
    ]
    for copy in copies:
        copy.start()
    copies[0].wait()
    cos, sin = phases(steps, my_place())
    turn = [v[:, at : at + 128] for at in (0, 256) for v in (cos, sin)]
    turn = jnp.concatenate(turn + [jnp.zeros((124, 128), F32)], axis=0).T
    channel = iota((256, 128), 1) % CIN
    total = jnp.zeros((256, 128), F32)
    copies[1].wait()
    for ch in range(CIN):
        copies[2 + ch].wait()
        fh, fl = split(fields_v[ch].reshape(256, NZ))
        term = mm(jnp.concatenate([fh, fl], axis=1), ztab[:256]) + mm(fh, ztab[256:])
        total = jnp.where(channel == ch, term, total)
    copies[-1].wait()
    th, tl = split(total)
    both = mm(ptab[0], jnp.concatenate([th, tl], axis=1))
    both = both[:, :128] + both[:, 128:] + mm(ptab[1], th)
    low = iota((128, 128), 1) < 64
    rows = []
    for s in range(2):
        part_cos = both[256 * s : 256 * s + 128]
        part_sin = both[256 * s + 128 : 256 * s + 256]
        part_sin = pltpu.roll(part_sin, 64, 1)
        pair = jnp.where(low, part_cos + part_sin, part_cos - part_sin)
        cos_s, sin_s = turn[:, 2 * s : 2 * s + 1], turn[:, 2 * s + 1 : 2 * s + 2]
        rows.append(cos_s * pair + sin_s * pltpu.roll(pair, 64, 1))
    out[...] = jnp.where(low, rows[0], pltpu.roll(rows[1], 64, 1))
    token[...] = rows[0][:8]


def prepare_mix(after, weights, lift, lift_bias, weights_v, lift_wide, bias_column, sem):
    copy = pltpu.make_async_copy(weights, weights_v, sem)
    copy.start()
    lift_wide[...] = exact(lift[...], ones_where(iota((CIN, 128), 0) == iota((CIN, 128), 1) % 4))
    gx, gy = my_place()
    at_zero = (iota((C1, 32), 1) + gx + gy) == 0
    bias_column[...] = jnp.where(at_zero, lift_bias[...] * math.sqrt(TOTAL), 0.0)
    copy.wait()


def prepare(
    after, waves, steps, lift, lift_bias, bypass_in, bias_in, bypass_out, bias_out, project,
    own_t, mate_t, spread_t, pack, fine_t, wide_mix, project_mix, bias_mix,
):
    nt = ((1,), (1,))
    gx, gy = my_place()
    own = device_waves(waves, steps, (gx, gy))
    mate = device_waves(waves, steps, (gx + 1 - 2 * (gx % 2), gy))
    cos_y = jnp.concatenate([waves[2, 2 * q : 2 * q + 1] for q in range(8)], axis=0)
    sin_y = jnp.concatenate([waves[3, 2 * q : 2 * q + 1] for q in range(8)], axis=0)
    tables = [
        jnp.concatenate(wave_rows(along, cos_y, sin_y, range(0, 16, 2)), axis=0)
        for along in (own, mate)
    ]
    own_t[0:128], own_t[128:256] = split(tables[0] * BACK)
    mate_t[0:128], mate_t[128:256] = split(tables[1] * BACK)
    scale = 1.0 / math.sqrt(TOTAL / 4.0)
    for patch in range(2):
        at = slice(128 * patch, 128 * patch + 128)
        high, less = split(tables[patch].T * scale)
        spread_t[0, :, at] = high
        spread_t[1, :, at] = less
    lanes = [
        ones_where(iota((C2, 128), 0) == 32 * h + iota((C2, 128), 1) % 32) for h in range(2)
    ]
    through = exact(lift[...], bypass_in[...], ((0,), (1,)))
    through = exact(ones_where(iota((32, CIN), 0) // 8 == iota((32, CIN), 1)), through)
    offset = bias_in[...] + exact(lift_bias[...], bypass_in[...], nt)
    for t in range(4):
        at = slice(128 * t, 128 * t + 128)
        same = iota((32, 128), 0) % 8 == 4 * (t // 2) + iota((32, 128), 1) // 32
        high, less = split(jnp.where(same, exact(through, lanes[t % 2]), 0.0))
        rows = bias_rows(exact(offset, lanes[t % 2]))
        pack[:, at] = jnp.concatenate([rows, high, less, high], axis=0)
    spread_d = ones_where(iota((C1, 256), 0) == iota((C1, 256), 1) % 32)
    same = iota((128, 256), 0) // 32 == iota((128, 256), 1) // 64
    for h in range(2):
        pick = ones_where(iota((128, C2), 1) == 32 * h + iota((128, C2), 0) % 32)
        wide = exact(exact(pick, bypass_out[...], nt), spread_d)
        high, less = split(jnp.where(same, wide, 0.0))
        wide_mix[128 * h : 128 * h + 128] = jnp.concatenate([high, less], axis=1)
    scaled = (own[0] * BACK, own[1] * BACK)
    for x in range(0, 16, 8):
        pair = wave_rows(scaled, waves[2], waves[3], range(x, x + 8))
        for part in range(2):
            at = slice(256 * part + 16 * x, 256 * part + 16 * x + 128)
            high, less = split(pair[part])
            fine_t[0, at] = high
            fine_t[1, at] = less
    lanes = ones_where(iota((C1, 512), 0) == iota((C1, 512), 1) % 32)
    bias_mix[...] = bias_rows(exact(bias_out[...], lanes))
    pick = ones_where(iota((512, C1), 1) == iota((512, C1), 0) % 32)
    onto = ones_where(iota((CIN, 128), 0) == iota((CIN, 128), 1) % 64 // 16)
    made = exact(exact(pick, project[...], nt), onto)
    lane = iota((512, 128), 1)
    made = jnp.where(iota((512, 128), 0) // 32 == lane % 16, made, 0.0)
    high = made.astype(BF16).astype(F32)
    project_mix[...] = jnp.where(lane < 64, high, made - high).T.astype(BF16)


def bypass(
    after, values, wide_mix_h, fields, lift, lift_bias, project, project_bias, skip, base,
    values_v, skip_v, wide_mix, in_sems, out_sems,
):
    def taken(p):
        return pltpu.make_async_copy(values.at[p], values_v.at[p], in_sems.at[p])

    def given(p):
        return pltpu.make_async_copy(skip_v.at[p], skip.at[p], out_sems.at[p])

    mix_copy = pltpu.make_async_copy(wide_mix_h, wide_mix, in_sems.at[8])
    mix_copy.start()
    for p in range(8):
        taken(p).start()
    across = exact(project[...], lift[...])
    constant = project_bias[...] + exact(project[...], lift_bias[...], ((1,), (1,)))
    mix_copy.wait()

    def step(x, carry):
        for o in range(CIN):
            total = jnp.broadcast_to(constant[o : o + 1], (16, NZ))
            for ch in range(CIN):
                total += across[o : o + 1, ch : ch + 1] * fields[ch, x]
            base[o, x] = total
        return carry

    lax.fori_loop(0, 16, step, 0)

    for group in range(0, 8, 4):
        ps = range(group, group + 4)
        for p in ps:
            taken(p).wait()
        for q in range(2):
            at = slice(256 * q, 256 * q + 256)
            high, less = [
                jnp.concatenate([values_v[p, i, :, at] for p in ps], axis=0) for i in range(2)
            ]
            wide = mm(high, wide_mix[:, :256]) + mm(high, wide_mix[:, 256:])
            wide += mm(less, wide_mix[:, :256])
            for u, p in enumerate(ps):
                skip_v[p, :, at] = wide[128 * u : 128 * u + 128]
        for p in ps:
            given(p).start()
    for p in range(8):
        given(p).wait()


def mixed_row(columns, weights, wide):
    pieces = [[[None] * KZ for _ in range(2)] for _ in range(2)]
    for s in range(2):
        for k in range(KZ):
            real, imag = columns(s, 0, k), columns(s, 1, k)
            wr, wi = weights[s, 0, k], weights[s, 1, k]
            pieces[s][0][k] = jnp.sum(real * wr - imag * wi, axis=0, keepdims=True)
            pieces[s][1][k] = jnp.sum(real * wi + imag * wr, axis=0, keepdims=True)
    per = 128 // wide
    return [
        jnp.concatenate(
            [
                jnp.concatenate(
                    [v[:, at : at + wide] for v in pieces[s][part][k : k + per]], axis=1
                )
                for s in range(2)
                for part in range(2)
                for k in range(0, KZ, per)
            ],
            axis=0,
        )
        for at in range(0, weights.shape[-1], wide)
    ]


def first_mix(arrived, lift_wide, bias_column, weights, out, token, blocks, sems):
    row = jnp.sum(arrived[...], axis=0, keepdims=True)
    source = lax.broadcasted_iota(jnp.int32, (128, 32), 0) // CIN
    pick = (source == lax.broadcasted_iota(jnp.int32, (128, 32), 1)).astype(F32)
    lifted = (
        lax.dot_general(
            lift_wide[...] * row, pick, (((1,), (0,)), ((), ())),
            precision=lax.Precision.HIGHEST, preferred_element_type=F32,
        )
        + bias_column[...]
    )

    def column(s, part, k):
        at = s * 16 + part * 8 + k
        return lifted[:, at : at + 1]

    halves = mixed_row(column, weights, 32)
    token[...] = halves[0]
    copies = []
    for half in range(2):
        for i in range(16):
            blocks[half, i] = halves[half]
        for i in range(half, 8, 2):
            copies.append(
                pltpu.make_async_copy(blocks.at[half], out.at[pl.ds(16 * i, 16)], sems.at[i])
            )
            copies[-1].start()
    for copy in copies:
        copy.wait()


def second_mix(arrived, weights, out):
    sums = [None, None]
    for n in range(OWNERS):
        half = n // 16 % 2
        sums[half] = arrived[n] if sums[half] is None else sums[half] + arrived[n]
    stacked = jnp.concatenate(sums + [jnp.zeros((112, 128), F32)], axis=0).T

    def column(s, part, k):
        at = (s * 2 + part) * 2 + k // 4
        rows = slice(k % 4 * 32, k % 4 * 32 + 32)
        return jnp.concatenate([stacked[rows, at : at + 1], stacked[rows, at + 8 : at + 9]], axis=0)

    (block,) = mixed_row(column, weights, 32)
    for n in range(OWNERS):
        out[n] = block


def invert(arrived, table, out):
    modes = []
    for t in range(4):
        tiles = [arrived[pl.ds(2 * t + u, OWNERS, stride=8), :] for u in range(2)]
        modes.append(jnp.concatenate(tiles, axis=1))
    mh, ml = split(jnp.concatenate(modes, axis=0))
    made = mm(table[...], mh)
    made = made[:128] + made[128:] + mm(table[:128], ml)
    out[0] = made[:, :128]
    out[1] = made[:, 128:]


def coarse_level(
    own, got, pack, fields, z_back, z_fwd,
    kept, sent, values, y_s, rhs_s, g_s, t_s, values_v, sems,
):
    core = lax.axis_index("gx") % 2
    for t in range(2):
        y_s[2 * core + t] = own[t]
        y_s[2 * (1 - core) + t] = got[t]
    for h in range(2):
        for t in range(2):
            for q in range(2):
                made = regroup(
                    [y_s[2 * h + t, pl.ds(4 * q + u, 16, stride=8), :] for u in range(4)]
                )
                for v in range(4):
                    rhs_s[2 * q + h, pl.ds(16 * (4 * t + v), 16), :] = made[v]

    def step(p, carry):
        rows = [rhs_s[t, pl.ds(p, 16, stride=8), :] for t in range(4)]
        high, less = split(jnp.concatenate(rows, axis=1))
        pooled = []
        for ch in range(CIN):
            total = jnp.zeros((8, 128), F32)
            for dx in range(2):
                for dy in range(2):
                    total += fields[ch, 2 * p + dx, pl.ds(dy, 8, stride=2), :]
            pooled.append(total * 0.25)
        ph, pll = split(jnp.concatenate(pooled, axis=0))
        left = jnp.concatenate([z_back[...], ph, ph, pll], axis=0)
        right = jnp.concatenate([high, less, high, pack[...]], axis=0)
        value = gelu(mm(left, right, ((0,), (0,))))
        vh, vl = split(value)
        made = mm(z_fwd[...], jnp.concatenate([vh, vl], axis=0))
        made = made[:16] + made[16:]
        for t in range(4):
            at = slice(128 * t, 128 * t + 128)
            g_s[t, pl.ds(pl.multiple_of(p * 8, 8), 8), :] = made[:8, at]
            g_s[t, pl.ds(pl.multiple_of(p * 8 + 64, 8), 8), :] = made[8:, at]
        values_v[p, 0] = vh
        values_v[p, 1] = vl
        pltpu.make_async_copy(values_v.at[p], values.at[p], sems.at[p]).start()
        return carry

    lax.fori_loop(0, 8, step, 0, unroll=UNROLL)
    for h in range(2):
        for t in range(2):
            for q in range(2):
                made = regroup(
                    [g_s[2 * q + h, pl.ds(4 * t + v, 16, stride=8), :] for v in range(4)]
                )
                for u in range(4):
                    t_s[2 * h + t, pl.ds(4 * q + u, 16, stride=8), :] = made[u]
    for t in range(2):
        kept[t] = t_s[2 * core + t]
        sent[t] = t_s[2 * (1 - core) + t]
    for p in range(8):
        pltpu.make_async_copy(values_v.at[p], values.at[p], sems.at[p]).wait()


def spread(kept, got, table, out, token, out_v, sems):
    rows = [jnp.concatenate([ref[0], ref[1]], axis=1) for ref in (kept, got)]
    th, tl = split(jnp.concatenate(rows, axis=0))
    copies = []
    for j in range(4):
        ah, al = [
            jnp.concatenate([table[i, pl.ds(128 * t + 32 * j, 32)] for t in range(4)], axis=0)
            for i in range(2)
        ]
        made = mm(ah, th) + mm(ah, tl) + mm(al, th)
        for t in range(4):
            for u in range(2):
                piece = made[32 * t : 32 * t + 32, 128 * u : 128 * u + 128]
                out_v[pl.ds(256 * j + 2 * t + u, 32, stride=8), :] = piece
        rows = pl.ds(256 * j, 256)
        copies.append(pltpu.make_async_copy(out_v.at[rows], out.at[rows], sems.at[j]))
        copies[-1].start()
    token[...] = out_v[:8]
    for copy in copies:
        copy.wait()


def fine_level(
    arrived, table, z_back_h, skip, project_h, bias_h, base_h, out, base, out_v,
    y_s, rhs_s, skip_v, z_back, project_mix, bias_mix, sems, base_sems, out_sems,):
    def taken(p):
        rows = pl.ds(2 * p, 2)
        return (
            pltpu.make_async_copy(skip.at[p], skip_v.at[p], sems.at[p]),
            pltpu.make_async_copy(base_h.at[:, rows], base.at[:, rows], base_sems.at[p]),
        )

    def given(p):
        rows = pl.ds(2 * p, 2)
        return pltpu.make_async_copy(out_v.at[:, rows], out.at[:, rows], out_sems.at[p])

    small = [
        pltpu.make_async_copy(source, target, sems.at[i])
        for i, source, target in (
            (8, z_back_h, z_back), (9, project_h, project_mix), (10, bias_h, bias_mix)
        )
    ]
    for copy in small:
        copy.start()
    for p in range(8):
        for copy in taken(p):
            copy.start()
    modes = []
    for t in range(4):
        tiles = [arrived[pl.ds(2 * t + u, OWNERS, stride=8), :] for u in range(2)]
        modes.append(jnp.concatenate(tiles, axis=1))
    mh, ml = split(jnp.concatenate(modes, axis=0))
    for t in range(4):
        at = slice(128 * t, 128 * t + 128)
        made = mm(table[0, at], mh) + mm(table[0, at], ml) + mm(table[1, at], mh)
        y_s[0, at] = made[:, :128]
        y_s[1, at] = made[:, 128:]
    for t in range(2):
        for y in range(4):
            made = regroup([y_s[t, pl.ds(4 * y + u, 32, stride=16), :] for u in range(4)])
            for v in range(4):
                rhs_s[y, pl.ds(32 * (4 * t + v), 32), :] = made[v]
    for copy in small:
        copy.wait()

    def step(i, carry):
        rights = []
        for u in range(FINE_GROUP):
            x = FINE_GROUP * i + u
            rows = [rhs_s[t, pl.ds(x, 16, stride=16), :] for t in range(4)]
            high, less = split(jnp.concatenate(rows, axis=1))
            rights += [high, less, high, bias_mix[...]]
        before = jnp.concatenate(
            [
                mm(z_back[...], jnp.concatenate(rights[at : at + 16], axis=0))
                for at in range(0, 4 * FINE_GROUP, 16)
            ],
            axis=0,
        )
        for v in range(FINE_GROUP // 2):
            p = FINE_GROUP // 2 * i + v
            for copy in taken(p):
                copy.wait()
        skips = [skip_v[FINE_GROUP // 2 * i + u // 2] for u in range(FINE_GROUP)]
        vh, vl = split(gelu(before + jnp.concatenate(skips, axis=0)))
        made = mm(project_mix[...], vh, ((1,), (1,)))
        made = made[:64] + made[64:] + mm(project_mix[:64], vl, ((1,), (1,)))
        for u in range(FINE_GROUP):
            x = FINE_GROUP * i + u
            for o in range(CIN):
                piece = made[16 * o : 16 * o + 16, 128 * u : 128 * u + 128]
                out_v[o, x] = piece + base[o, x]
        for v in range(FINE_GROUP // 2):
            given(FINE_GROUP // 2 * i + v).start()
        return carry

    lax.fori_loop(0, 16 // FINE_GROUP, step, 0)
    for p in range(8):
        given(p).wait()


def exchange(tiles):
    return lax.all_to_all(tiles, AXES, split_axis=0, concat_axis=0, tiled=True)


def between_cores(array):
    return lax.ppermute(array, "gx", [(i, i ^ 1) for i in range(lax.axis_size("gx"))])


def stay(array):
    return pltpu.with_memory_space_constraint(array, pltpu.HBM)


def on_device(
    fields, lift, lift_bias, spectral_in, bypass_in, bias_in, spectral_out, bypass_out, bias_out,
    project, project_bias,
):
    waves, steps = wave_tables(), phase_steps()
    z_back, z_fwd = inverse_z_table(), forward_z_table()
    call = functools.partial(pl.pallas_call, compiler_params=PARAMS)
    shape = jax.ShapeDtypeStruct
    dma = pltpu.SemaphoreType.DMA
    work = pl.CostEstimate(flops=1 << 31, transcendentals=0, bytes_accessed=6 << 20)
    spectrum, token = pl.pallas_call(
        first_spectrum,
        out_shape=(shape((OWNERS, 128), F32), shape((8, 128), F32)),
        in_specs=[HBM] * 4, out_specs=(VMEM, VMEM),
        scratch_shapes=[
            pltpu.VMEM((CIN, 16, 16, NZ), F32), pltpu.VMEM((384, 128), BF16),
            pltpu.VMEM((2, 512, 256), BF16), pltpu.VMEM((2, 512), jnp.int32), dma((7,)),
        ],
        name="first_spectrum", compiler_params=ALONE,
    )(fields, first_z_table(), first_places_table(), steps)
    prepared = call(
        prepare_mix,
        out_shape=(
            shape((2, 2, KZ, C1, C2), F32), shape((C1, 128), F32), shape((C1, 32), F32),
        ),
        in_specs=[VMEM, HBM, VMEM, VMEM], out_specs=(VMEM,) * 3, name="prepare_mix",
        scratch_shapes=[dma(())], cost_estimate=work,
    )(token, stay(spectral_in), lift, lift_bias[:, None])
    arrived, prepared = lax.optimization_barrier((exchange(spectrum), prepared))
    weights, lift_wide, bias_column = prepared
    mixed, token = call(
        first_mix,
        out_shape=(pltpu.HBM((OWNERS, 8, 128), F32), shape((8, 128), F32)),
        in_specs=[VMEM] * 4, out_specs=(HBM, VMEM), name="first_mix",
        scratch_shapes=[pltpu.VMEM((2, 16, 8, 128), F32), dma((8,))],
    )(arrived, lift_wide, bias_column, weights)
    prepared = call(
        prepare,
        out_shape=(
            shape((256, 512), BF16), shape((256, 512), BF16), shape((2, 512, 256), BF16),
            shape((112, 512), BF16), pltpu.HBM((2, 512, 512), BF16), pltpu.HBM((256, 512), BF16),
            pltpu.HBM((128, 512), BF16), pltpu.HBM((16, 512), BF16),
        ),
        in_specs=[VMEM] * 10, out_specs=(VMEM,) * 8, name="prepare", cost_estimate=work,
    )(
        token, waves, steps, lift, lift_bias[None], bypass_in, bias_in[None], bypass_out,
        bias_out[None], project,
    )
    mine, prepared = lax.optimization_barrier((exchange(mixed), prepared))
    own_t, mate_t, spread_t, pack, fine_t, wide_mix, project_mix, bias_mix = prepared
    mine = mine.reshape(OWNERS * 8, 128)
    own, got = [
        call(
            invert, out_shape=shape((2, 128, 128), F32), in_specs=[VMEM] * 2, out_specs=VMEM,
            name=name, cost_estimate=work,
        )(mine, table)
        for name, table in (("invert_own", own_t), ("invert_mate", mate_t))
    ]
    kept, sent, values = call(
        coarse_level,
        out_shape=(
            shape((2, 128, 128), F32), shape((2, 128, 128), F32),
            pltpu.HBM((8, 2, NZ, 512), BF16),
        ),
        in_specs=[VMEM] * 6, out_specs=(VMEM, VMEM, HBM), name="coarse_level",
        scratch_shapes=[pltpu.VMEM((4, 128, 128), F32)] * 4
        + [pltpu.VMEM((8, 2, NZ, 512), BF16), dma((8,))],
    )(
        own, between_cores(got), pack, fields, z_back, z_fwd,
    )
    spectrum, token = call(
        spread,
        out_shape=(pltpu.HBM((OWNERS * 8, 128), F32), shape((8, 128), F32)),
        in_specs=[VMEM] * 3, out_specs=(HBM, VMEM), name="spread",
        scratch_shapes=[pltpu.VMEM((OWNERS * 8, 128), F32), dma((4,))],
    )(kept, between_cores(sent), spread_t)
    prepared = call(
        bypass,
        out_shape=(pltpu.HBM((8, NZ, 512), F32), pltpu.HBM((CIN, 16, 16, NZ), F32)),
        in_specs=[VMEM, HBM, HBM] + [VMEM] * 5, out_specs=(HBM, VMEM), name="bypass",
        scratch_shapes=[
            pltpu.VMEM((8, 2, NZ, 512), BF16), pltpu.VMEM((8, NZ, 512), F32),
            pltpu.VMEM((256, 512), BF16), dma((9,)), dma((8,)),
        ],
        cost_estimate=work,
    )(
        token, stay(values), stay(wide_mix), fields, lift, lift_bias[None], project,
        project_bias[:, None],
    )
    arrived, prepared = lax.optimization_barrier(
        (exchange(spectrum.reshape(OWNERS, 8, 128)), prepared)
    )
    skip, base = prepared
    mixed = call(
        second_mix,
        out_shape=shape((OWNERS, 8, 128), F32),
        in_specs=[VMEM, VMEM], out_specs=VMEM, name="second_mix",
    )(arrived, spectral_out)
    return pl.pallas_call(
        fine_level, compiler_params=pltpu.CompilerParams(vmem_limit_bytes=32 << 20),
        out_shape=shape((CIN, 16, 16, NZ), F32),
        in_specs=[VMEM, VMEM] + [HBM] * 5, out_specs=HBM, name="fine_level",
        scratch_shapes=[
            pltpu.VMEM((CIN, 16, 16, NZ), F32), pltpu.VMEM((CIN, 16, 16, NZ), F32),
            pltpu.VMEM((2, 512, 128), F32), pltpu.VMEM((4, 256, 128), F32),
            pltpu.VMEM((8, NZ, 512), F32), pltpu.VMEM((4 * NZ, 256), BF16),
            pltpu.VMEM((128, 512), BF16), pltpu.VMEM((16, 512), BF16), dma((11,)), dma((8,)),
            dma((8,)),
        ],
    )(
        exchange(mixed).reshape(OWNERS * 8, 128), fine_t, stay(jnp.asarray(fine_z_table())), stay(skip),
        stay(project_mix), stay(bias_mix), stay(base),
    )


def solution(mesh):
    owned = P(AXES, None, None, None, None)
    grid = P(None, "gx", "gy", None)
    in_specs = (grid, P(), P(), owned, P(), P(), owned, P(), P(), P(), P())
    return jax.shard_map(
        on_device, mesh=mesh, in_specs=in_specs, out_specs=grid, check_vma=False
    )
```

```python
import functools
import math

import jax
import jax.numpy as jnp
import numpy as np
from jax import lax
from jax.experimental import pallas as pl
from jax.experimental.pallas import tpu as pltpu
from jax.sharding import PartitionSpec as P

KX, KY, KZ = 16, 16, 8
NX, NY, NZ = 128, 256, 128
CIN, C1, C2 = 4, 32, 64
AXES = ("x", "core", "gy")
CHIPS = ("x", "gy")
OWNERS = 128
TOTAL = NX * NY * NZ
BACK = math.sqrt(2.0 / (KX * KY * KZ))
F32 = jnp.float32
BF16 = jnp.bfloat16
UNROLL = 8
FINE_GROUP = 16
VMEM = pl.BlockSpec(memory_space=pltpu.VMEM)
HBM = pl.BlockSpec(memory_space=pltpu.HBM)
PARAMS = pltpu.CompilerParams(vmem_limit_bytes=16 << 20)
ALONE = pltpu.CompilerParams(vmem_limit_bytes=60 << 20)


def mode_frequencies():
    centered = np.where(np.arange(16) < 8, np.arange(16), np.arange(16) - 16)
    n = np.arange(OWNERS)
    fx = np.stack([centered[n // 8]] * 2)
    fy = np.stack([centered[2 * (n % 8) + s] for s in range(2)])
    return fx, fy


def place_angles(xs, ys, x_length, y_length):
    fx, fy = mode_frequencies()
    turns = (
        fx[:, :, None, None] * xs[None, None, :, None] / x_length
        + fy[:, :, None, None] * ys[None, None, None, :] / y_length
    )
    return 2.0 * np.pi * turns


def wave_tables():
    fx, fy = mode_frequencies()
    ahead = np.array([0.0, 0.5 * np.pi])[None, None, :, None]
    places = np.arange(16)[:, None, None, None]
    along_x = 2.0 * np.pi * places * fx[None, :, None, :] / NX + ahead
    along_y = 2.0 * np.pi * places * fy[None, :, None, :] / NY + 0.0 * ahead
    tables = [np.cos(along_x), np.sin(along_x), np.cos(along_y), np.sin(along_y)]
    return np.stack(tables).reshape(4, 16, 512).astype(np.float32)


def phase_steps():
    fx, fy = mode_frequencies()
    steps = np.stack([np.stack([2 * fx, 2 * fx], axis=1), np.stack([fy, fy], axis=1)])
    return steps.reshape(2, 512).astype(np.int32)


def z_angles():
    return 2.0 * np.pi * (np.arange(NZ)[:, None] * np.arange(KZ)[None, :] % NZ) / NZ


def split_np(table):
    high = table.astype(BF16)
    low = (table - high.astype(np.float32)).astype(BF16)
    return high, low


def first_z_table():
    c, s = np.cos(z_angles()), np.sin(z_angles())
    parts = np.array([[c, -s], [-s, -c]]).transpose(2, 0, 1, 3).reshape(NZ, 32)
    high, low = split_np(np.repeat(parts, CIN, axis=1).astype(np.float32))
    return np.concatenate([high, high, low], axis=0)


def first_places_table():
    fx, fy = mode_frequencies()
    places = np.arange(16)
    turns = (
        fx[:, :, None, None] * places[:, None] / NX + fy[:, :, None, None] * places[None, :] / NY
    )
    angles = 2.0 * np.pi * turns
    table = np.stack([np.cos(angles), np.sin(angles)], axis=1) / math.sqrt(TOTAL)
    return np.stack(split_np(table.reshape(512, 256).astype(np.float32)))


def inverse_z_table():
    table = np.stack([np.cos(z_angles()), -np.sin(z_angles())], axis=2)
    high, low = split_np(table.reshape(NZ, 16).astype(np.float32))
    ones = np.zeros((16, NZ), BF16)
    ones[:3] = 1.0
    return np.concatenate([high.T, high.T, low.T, ones], axis=0)


def fine_z_table():
    table = np.kron(np.eye(4), inverse_z_table().T.astype(np.float32))
    return table.astype(BF16)


def forward_z_table():
    table = np.stack([np.cos(z_angles()).T, -np.sin(z_angles()).T], axis=0)
    high, low = split_np(table.reshape(16, NZ).astype(np.float32))
    return np.block([[high, high], [low, np.zeros_like(low)]])


def split(x):
    high = x.astype(BF16)
    return high, (x - high.astype(F32)).astype(BF16)


def bias_rows(bias):
    high, less = split(bias)
    least = (bias - high.astype(F32) - less.astype(F32)).astype(BF16)
    row = iota((16, bias.shape[1]), 0)
    rows = [v.astype(F32) for v in (high, less, least)]
    total = jnp.where(row == 0, rows[0], jnp.where(row == 1, rows[1], rows[2]))
    return jnp.where(row < 3, total, 0.0).astype(BF16)


def mm(a, b, dims=((1,), (0,))):
    return lax.dot_general(a, b, (dims, ((), ())), preferred_element_type=F32)


def mm3(a, b, dims=((1,), (0,))):
    ah, al = split(a)
    bh, bl = split(b)
    return mm(ah, bh, dims) + mm(ah, bl, dims) + mm(al, bh, dims)


def exact(a, b, dims=((1,), (0,))):
    return lax.dot_general(
        a, b, (dims, ((), ())), precision=lax.Precision.HIGHEST, preferred_element_type=F32
    )


def iota(shape, dim):
    return lax.broadcasted_iota(jnp.int32, shape, dim)


def ones_where(condition):
    return jnp.where(condition, 1.0, 0.0).astype(F32)


def gelu(x):
    return 0.5 * x * (1.0 + lax.erf(x * math.sqrt(0.5)))


def regroup(rows):
    group = iota(rows[0].shape, 1) // 32
    made = []
    for v in range(4):
        total = rows[v]
        for u in range(4):
            if u != v:
                moved = pltpu.roll(rows[u], ((u - v) % 4) * 32, 1)
                total = jnp.where(group == u, moved, total)
        made.append(total)
    return made


def my_place():
    return 2 * lax.axis_index("x") + lax.axis_index("core"), lax.axis_index("gy")


def phases(steps, place):
    turns = (steps[0:1] * place[0] + steps[1:2] * place[1]) & 15
    cos = sin = jnp.zeros(turns.shape, F32)
    for n in range(16):
        here = turns == n
        cos = jnp.where(here, math.cos(2.0 * math.pi * n / 16), cos)
        sin = jnp.where(here, math.sin(2.0 * math.pi * n / 16), sin)
    return cos, sin


def device_waves(waves, steps, place):
    cos, sin = phases(steps, place)
    return waves[0] * cos - waves[1] * sin, waves[1] * cos + waves[0] * sin


def wave_rows(along_x, cos_y, sin_y, xs):
    cos_x, sin_x = along_x
    real = [cos_x[x : x + 1] * cos_y - sin_x[x : x + 1] * sin_y for x in xs]
    imag = [sin_x[x : x + 1] * cos_y + cos_x[x : x + 1] * sin_y for x in xs]
    return jnp.concatenate(real, axis=0), jnp.concatenate(imag, axis=0)


def first_spectrum(
    fields, ztab_h, ptab_h, steps_h, out, token, fields_v, ztab, ptab, steps, sems,
):
    pairs = [(steps_h, steps), (ztab_h, ztab)]
    pairs += [(fields.at[ch], fields_v.at[ch]) for ch in range(CIN)]
    pairs.append((ptab_h, ptab))
    copies = [
        pltpu.make_async_copy(source, target, sems.at[i])
        for i, (source, target) in enumerate(pairs)
    ]
    for copy in copies:
        copy.start()
    copies[0].wait()
    cos, sin = phases(steps, my_place())
    turn = [v[:, at : at + 128] for at in (0, 256) for v in (cos, sin)]
    turn = jnp.concatenate(turn + [jnp.zeros((124, 128), F32)], axis=0).T
    channel = iota((256, 128), 1) % CIN
    total = jnp.zeros((256, 128), F32)
    copies[1].wait()
    for ch in range(CIN):
        copies[2 + ch].wait()
        fh, fl = split(fields_v[ch].reshape(256, NZ))
        term = mm(jnp.concatenate([fh, fl], axis=1), ztab[:256]) + mm(fh, ztab[256:])
        total = jnp.where(channel == ch, term, total)
    copies[-1].wait()
    th, tl = split(total)
    both = mm(ptab[0], jnp.concatenate([th, tl], axis=1))
    both = both[:, :128] + both[:, 128:] + mm(ptab[1], th)
    low = iota((128, 128), 1) < 64
    rows = []
    for s in range(2):
        part_cos = both[256 * s : 256 * s + 128]
        part_sin = both[256 * s + 128 : 256 * s + 256]
        part_sin = pltpu.roll(part_sin, 64, 1)
        pair = jnp.where(low, part_cos + part_sin, part_cos - part_sin)
        cos_s, sin_s = turn[:, 2 * s : 2 * s + 1], turn[:, 2 * s + 1 : 2 * s + 2]
        rows.append(cos_s * pair + sin_s * pltpu.roll(pair, 64, 1))
    out[...] = jnp.where(low, rows[0], pltpu.roll(rows[1], 64, 1))
    token[...] = rows[0][:8]


def prepare_mix(after, weights, lift, lift_bias, weights_v, lift_wide, bias_column, sem):
    copy = pltpu.make_async_copy(weights, weights_v, sem)
    copy.start()
    lift_wide[...] = exact(lift[...], ones_where(iota((CIN, 128), 0) == iota((CIN, 128), 1) % 4))
    gx, gy = my_place()
    at_zero = (iota((C1, 32), 1) + gx + gy) == 0
    bias_column[...] = jnp.where(at_zero, lift_bias[...] * math.sqrt(TOTAL), 0.0)
    copy.wait()


def prepare(
    after, waves, steps, lift, lift_bias, bypass_in, bias_in, bypass_out, bias_out, project,
    own_t, mate_t, spread_t, pack, fine_t, wide_mix, project_mix, bias_mix,
):
    nt = ((1,), (1,))
    gx, gy = my_place()
    own = device_waves(waves, steps, (gx, gy))
    mate = device_waves(waves, steps, (gx + 1 - 2 * (gx % 2), gy))
    cos_y = jnp.concatenate([waves[2, 2 * q : 2 * q + 1] for q in range(8)], axis=0)
    sin_y = jnp.concatenate([waves[3, 2 * q : 2 * q + 1] for q in range(8)], axis=0)
    tables = [
        jnp.concatenate(wave_rows(along, cos_y, sin_y, range(0, 16, 2)), axis=0)
        for along in (own, mate)
    ]
    own_t[0:128], own_t[128:256] = split(tables[0] * BACK)
    mate_t[0:128], mate_t[128:256] = split(tables[1] * BACK)
    scale = 1.0 / math.sqrt(TOTAL / 4.0)
    for patch in range(2):
        at = slice(128 * patch, 128 * patch + 128)
        high, less = split(tables[patch].T * scale)
        spread_t[0, :, at] = high
        spread_t[1, :, at] = less
    lanes = [
        ones_where(iota((C2, 128), 0) == 32 * h + iota((C2, 128), 1) % 32) for h in range(2)
    ]
    through = exact(lift[...], bypass_in[...], ((0,), (1,)))
    through = exact(ones_where(iota((32, CIN), 0) // 8 == iota((32, CIN), 1)), through)
    offset = bias_in[...] + exact(lift_bias[...], bypass_in[...], nt)
    for t in range(4):
        at = slice(128 * t, 128 * t + 128)
        same = iota((32, 128), 0) % 8 == 4 * (t // 2) + iota((32, 128), 1) // 32
        high, less = split(jnp.where(same, exact(through, lanes[t % 2]), 0.0))
        rows = bias_rows(exact(offset, lanes[t % 2]))
        pack[:, at] = jnp.concatenate([rows, high, less, high], axis=0)
    spread_d = ones_where(iota((C1, 256), 0) == iota((C1, 256), 1) % 32)
    same = iota((128, 256), 0) // 32 == iota((128, 256), 1) // 64
    for h in range(2):
        pick = ones_where(iota((128, C2), 1) == 32 * h + iota((128, C2), 0) % 32)
        wide = exact(exact(pick, bypass_out[...], nt), spread_d)
        high, less = split(jnp.where(same, wide, 0.0))
        wide_mix[128 * h : 128 * h + 128] = jnp.concatenate([high, less], axis=1)
    scaled = (own[0] * BACK, own[1] * BACK)
    for x in range(0, 16, 8):
        pair = wave_rows(scaled, waves[2], waves[3], range(x, x + 8))
        for part in range(2):
            at = slice(256 * part + 16 * x, 256 * part + 16 * x + 128)
            high, less = split(pair[part])
            fine_t[0, at] = high
            fine_t[1, at] = less
    lanes = ones_where(iota((C1, 512), 0) == iota((C1, 512), 1) % 32)
    bias_mix[...] = bias_rows(exact(bias_out[...], lanes))
    pick = ones_where(iota((512, C1), 1) == iota((512, C1), 0) % 32)
    onto = ones_where(iota((CIN, 128), 0) == iota((CIN, 128), 1) % 64 // 16)
    made = exact(exact(pick, project[...], nt), onto)
    lane = iota((512, 128), 1)
    made = jnp.where(iota((512, 128), 0) // 32 == lane % 16, made, 0.0)
    high = made.astype(BF16).astype(F32)
    project_mix[...] = jnp.where(lane < 64, high, made - high).T.astype(BF16)


def bypass(
    after, values, wide_mix_h, fields, lift, lift_bias, project, project_bias, skip, base,
    values_v, skip_v, wide_mix, in_sems, out_sems,
):
    def taken(p):
        return pltpu.make_async_copy(values.at[p], values_v.at[p], in_sems.at[p])

    def given(p):
        return pltpu.make_async_copy(skip_v.at[p], skip.at[p], out_sems.at[p])

    mix_copy = pltpu.make_async_copy(wide_mix_h, wide_mix, in_sems.at[8])
    mix_copy.start()
    for p in range(8):
        taken(p).start()
    across = exact(project[...], lift[...])
    constant = project_bias[...] + exact(project[...], lift_bias[...], ((1,), (1,)))
    mix_copy.wait()

    def step(x, carry):
        for o in range(CIN):
            total = jnp.broadcast_to(constant[o : o + 1], (16, NZ))
            for ch in range(CIN):
                total += across[o : o + 1, ch : ch + 1] * fields[ch, x]
            base[o, x] = total
        return carry

    lax.fori_loop(0, 16, step, 0)

    for group in range(0, 8, 4):
        ps = range(group, group + 4)
        for p in ps:
            taken(p).wait()
        for q in range(2):
            at = slice(256 * q, 256 * q + 256)
            high, less = [
                jnp.concatenate([values_v[p, i, :, at] for p in ps], axis=0) for i in range(2)
            ]
            wide = mm(high, wide_mix[:, :256]) + mm(high, wide_mix[:, 256:])
            wide += mm(less, wide_mix[:, :256])
            for u, p in enumerate(ps):
                skip_v[p, :, at] = wide[128 * u : 128 * u + 128]
        for p in ps:
            given(p).start()
    for p in range(8):
        given(p).wait()


def mixed_row(columns, weights, wide):
    pieces = [[[None] * KZ for _ in range(2)] for _ in range(2)]
    for s in range(2):
        for k in range(KZ):
            real, imag = columns(s, 0, k), columns(s, 1, k)
            wr, wi = weights[s, 0, k], weights[s, 1, k]
            pieces[s][0][k] = jnp.sum(real * wr - imag * wi, axis=0, keepdims=True)
            pieces[s][1][k] = jnp.sum(real * wi + imag * wr, axis=0, keepdims=True)
    per = 128 // wide
    return [
        jnp.concatenate(
            [
                jnp.concatenate(
                    [v[:, at : at + wide] for v in pieces[s][part][k : k + per]], axis=1
                )
                for s in range(2)
                for part in range(2)
                for k in range(0, KZ, per)
            ],
            axis=0,
        )
        for at in range(0, weights.shape[-1], wide)
    ]


def first_mix(arrived, lift_wide, bias_column, weights, out, token, blocks, sems):
    row = jnp.sum(arrived[...], axis=0, keepdims=True)
    source = lax.broadcasted_iota(jnp.int32, (128, 32), 0) // CIN
    pick = (source == lax.broadcasted_iota(jnp.int32, (128, 32), 1)).astype(F32)
    lifted = (
        lax.dot_general(
            lift_wide[...] * row, pick, (((1,), (0,)), ((), ())),
            precision=lax.Precision.HIGHEST, preferred_element_type=F32,
        )
        + bias_column[...]
    )

    def column(s, part, k):
        at = s * 16 + part * 8 + k
        return lifted[:, at : at + 1]

    halves = mixed_row(column, weights, 32)
    token[...] = halves[0]
    copies = []
    for half in range(2):
        for i in range(16):
            blocks[half, i] = halves[half]
        for i in range(half, 8, 2):
            copies.append(
                pltpu.make_async_copy(blocks.at[half], out.at[pl.ds(16 * i, 16)], sems.at[i])
            )
            copies[-1].start()
    for copy in copies:
        copy.wait()


def second_mix(arrived, weights, out):
    sums = [None, None]
    for n in range(OWNERS):
        half = n // 16 % 2
        sums[half] = arrived[n] if sums[half] is None else sums[half] + arrived[n]
    stacked = jnp.concatenate(sums + [jnp.zeros((112, 128), F32)], axis=0).T

    def column(s, part, k):
        at = (s * 2 + part) * 2 + k // 4
        rows = slice(k % 4 * 32, k % 4 * 32 + 32)
        return jnp.concatenate([stacked[rows, at : at + 1], stacked[rows, at + 8 : at + 9]], axis=0)

    (block,) = mixed_row(column, weights, 32)
    for n in range(OWNERS // 2):
        out[n] = block


def invert(arrived, table, out):
    modes = []
    for t in range(4):
        tiles = [arrived[pl.ds(2 * t + u, OWNERS, stride=8), :] for u in range(2)]
        modes.append(jnp.concatenate(tiles, axis=1))
    mh, ml = split(jnp.concatenate(modes, axis=0))
    made = mm(table[...], mh)
    made = made[:128] + made[128:] + mm(table[:128], ml)
    out[0] = made[:, :128]
    out[1] = made[:, 128:]


def coarse_level(
    own, got, pack, fields, z_back, z_fwd,
    kept, sent, values, y_s, rhs_s, g_s, t_s, values_v, sems,
):
    core = lax.axis_index("core")
    for t in range(2):
        y_s[2 * core + t] = own[t]
        y_s[2 * (1 - core) + t] = got[t]
    for h in range(2):
        for t in range(2):
            for q in range(2):
                made = regroup(
                    [y_s[2 * h + t, pl.ds(4 * q + u, 16, stride=8), :] for u in range(4)]
                )
                for v in range(4):
                    rhs_s[2 * q + h, pl.ds(16 * (4 * t + v), 16), :] = made[v]

    def step(p, carry):
        rows = [rhs_s[t, pl.ds(p, 16, stride=8), :] for t in range(4)]
        high, less = split(jnp.concatenate(rows, axis=1))
        pooled = []
        for ch in range(CIN):
            total = jnp.zeros((8, 128), F32)
            for dx in range(2):
                for dy in range(2):
                    total += fields[ch, 2 * p + dx, pl.ds(dy, 8, stride=2), :]
            pooled.append(total * 0.25)
        ph, pll = split(jnp.concatenate(pooled, axis=0))
        left = jnp.concatenate([z_back[...], ph, ph, pll], axis=0)
        right = jnp.concatenate([high, less, high, pack[...]], axis=0)
        value = gelu(mm(left, right, ((0,), (0,))))
        vh, vl = split(value)
        made = mm(z_fwd[...], jnp.concatenate([vh, vl], axis=0))
        made = made[:16] + made[16:]
        for t in range(4):
            at = slice(128 * t, 128 * t + 128)
            g_s[t, pl.ds(pl.multiple_of(p * 8, 8), 8), :] = made[:8, at]
            g_s[t, pl.ds(pl.multiple_of(p * 8 + 64, 8), 8), :] = made[8:, at]
        values_v[p, 0] = vh
        values_v[p, 1] = vl
        pltpu.make_async_copy(values_v.at[p], values.at[p], sems.at[p]).start()
        return carry

    lax.fori_loop(0, 8, step, 0, unroll=UNROLL)
    for h in range(2):
        for t in range(2):
            for q in range(2):
                made = regroup(
                    [g_s[2 * q + h, pl.ds(4 * t + v, 16, stride=8), :] for v in range(4)]
                )
                for u in range(4):
                    t_s[2 * h + t, pl.ds(4 * q + u, 16, stride=8), :] = made[u]
    for t in range(2):
        kept[t] = t_s[2 * core + t]
        sent[t] = t_s[2 * (1 - core) + t]
    for p in range(8):
        pltpu.make_async_copy(values_v.at[p], values.at[p], sems.at[p]).wait()


def spread(kept, got, table, out, token, out_v, sems):
    rows = [jnp.concatenate([ref[0], ref[1]], axis=1) for ref in (kept, got)]
    th, tl = split(jnp.concatenate(rows, axis=0))
    copies = []
    for j in range(4):
        ah, al = [
            jnp.concatenate([table[i, pl.ds(128 * t + 32 * j, 32)] for t in range(4)], axis=0)
            for i in range(2)
        ]
        made = mm(ah, th) + mm(ah, tl) + mm(al, th)
        for t in range(4):
            for u in range(2):
                piece = made[32 * t : 32 * t + 32, 128 * u : 128 * u + 128]
                out_v[pl.ds(256 * j + 2 * t + u, 32, stride=8), :] = piece
        rows = pl.ds(256 * j, 256)
        copies.append(pltpu.make_async_copy(out_v.at[rows], out.at[rows], sems.at[j]))
        copies[-1].start()
    token[...] = out_v[:8]
    for copy in copies:
        copy.wait()


def fine_level(
    mine, other, table, z_back_h, skip, project_h, bias_h, base_h, out, base, out_v,
    y_s, rhs_s, skip_v, z_back, project_mix, bias_mix, sems, base_sems, out_sems,):
    def taken(p):
        rows = pl.ds(2 * p, 2)
        return (
            pltpu.make_async_copy(skip.at[p], skip_v.at[p], sems.at[p]),
            pltpu.make_async_copy(base_h.at[:, rows], base.at[:, rows], base_sems.at[p]),
        )

    def given(p):
        rows = pl.ds(2 * p, 2)
        return pltpu.make_async_copy(out_v.at[:, rows], out.at[:, rows], out_sems.at[p])

    small = [
        pltpu.make_async_copy(source, target, sems.at[i])
        for i, source, target in (
            (8, z_back_h, z_back), (9, project_h, project_mix), (10, bias_h, bias_mix)
        )
    ]
    for copy in small:
        copy.start()
    for p in range(8):
        for copy in taken(p):
            copy.start()
    first = lax.axis_index("core") == 0
    modes = []
    for t in range(4):
        tiles = []
        for u in range(2):
            a, b = [ref[pl.ds(2 * t + u, OWNERS // 2, stride=8), :] for ref in (mine, other)]
            cores = jnp.where(first, a, b), jnp.where(first, b, a)
            rows = [cores[c][16 * x : 16 * x + 16] for x in range(4) for c in range(2)]
            tiles.append(jnp.concatenate(rows, axis=0))
        modes.append(jnp.concatenate(tiles, axis=1))
    mh, ml = split(jnp.concatenate(modes, axis=0))
    for t in range(4):
        at = slice(128 * t, 128 * t + 128)
        made = mm(table[0, at], mh) + mm(table[0, at], ml) + mm(table[1, at], mh)
        y_s[0, at] = made[:, :128]
        y_s[1, at] = made[:, 128:]
    for t in range(2):
        for y in range(4):
            made = regroup([y_s[t, pl.ds(4 * y + u, 32, stride=16), :] for u in range(4)])
            for v in range(4):
                rhs_s[y, pl.ds(32 * (4 * t + v), 32), :] = made[v]
    for copy in small:
        copy.wait()

    def step(i, carry):
        rights = []
        for u in range(FINE_GROUP):
            x = FINE_GROUP * i + u
            rows = [rhs_s[t, pl.ds(x, 16, stride=16), :] for t in range(4)]
            high, less = split(jnp.concatenate(rows, axis=1))
            rights += [high, less, high, bias_mix[...]]
        before = jnp.concatenate(
            [
                mm(z_back[...], jnp.concatenate(rights[at : at + 16], axis=0))
                for at in range(0, 4 * FINE_GROUP, 16)
            ],
            axis=0,
        )
        for v in range(FINE_GROUP // 2):
            p = FINE_GROUP // 2 * i + v
            for copy in taken(p):
                copy.wait()
        skips = [skip_v[FINE_GROUP // 2 * i + u // 2] for u in range(FINE_GROUP)]
        vh, vl = split(gelu(before + jnp.concatenate(skips, axis=0)))
        made = mm(project_mix[...], vh, ((1,), (1,)))
        made = made[:64] + made[64:] + mm(project_mix[:64], vl, ((1,), (1,)))
        for u in range(FINE_GROUP):
            x = FINE_GROUP * i + u
            for o in range(CIN):
                piece = made[16 * o : 16 * o + 16, 128 * u : 128 * u + 128]
                out_v[o, x] = piece + base[o, x]
        for v in range(FINE_GROUP // 2):
            given(FINE_GROUP // 2 * i + v).start()
        return carry

    lax.fori_loop(0, 16 // FINE_GROUP, step, 0)
    for p in range(8):
        given(p).wait()


def exchange(tiles, axes=AXES):
    return lax.all_to_all(tiles, axes, split_axis=0, concat_axis=0, tiled=True)


def between_cores(array):
    return lax.ppermute(array, "core", [(0, 1), (1, 0)])


def stay(array):
    return pltpu.with_memory_space_constraint(array, pltpu.HBM)


def on_device(
    fields, lift, lift_bias, spectral_in, bypass_in, bias_in, spectral_out, bypass_out, bias_out,
    project, project_bias,
):
    waves, steps = wave_tables(), phase_steps()
    z_back, z_fwd = inverse_z_table(), forward_z_table()
    call = functools.partial(pl.pallas_call, compiler_params=PARAMS)
    shape = jax.ShapeDtypeStruct
    dma = pltpu.SemaphoreType.DMA
    work = pl.CostEstimate(flops=1 << 31, transcendentals=0, bytes_accessed=6 << 20)
    spectrum, token = pl.pallas_call(
        first_spectrum,
        out_shape=(shape((OWNERS, 128), F32), shape((8, 128), F32)),
        in_specs=[HBM] * 4, out_specs=(VMEM, VMEM),
        scratch_shapes=[
            pltpu.VMEM((CIN, 16, 16, NZ), F32), pltpu.VMEM((384, 128), BF16),
            pltpu.VMEM((2, 512, 256), BF16), pltpu.VMEM((2, 512), jnp.int32), dma((7,)),
        ],
        name="first_spectrum", compiler_params=ALONE,
    )(fields, first_z_table(), first_places_table(), steps)
    prepared = call(
        prepare_mix,
        out_shape=(
            shape((2, 2, KZ, C1, C2), F32), shape((C1, 128), F32), shape((C1, 32), F32),
        ),
        in_specs=[VMEM, HBM, VMEM, VMEM], out_specs=(VMEM,) * 3, name="prepare_mix",
        scratch_shapes=[dma(())], cost_estimate=work,
    )(token, stay(spectral_in), lift, lift_bias[:, None])
    arrived, prepared = lax.optimization_barrier((exchange(spectrum), prepared))
    weights, lift_wide, bias_column = prepared
    mixed, token = call(
        first_mix,
        out_shape=(pltpu.HBM((OWNERS, 8, 128), F32), shape((8, 128), F32)),
        in_specs=[VMEM] * 4, out_specs=(HBM, VMEM), name="first_mix",
        scratch_shapes=[pltpu.VMEM((2, 16, 8, 128), F32), dma((8,))],
    )(arrived, lift_wide, bias_column, weights)
    prepared = call(
        prepare,
        out_shape=(
            shape((256, 512), BF16), shape((256, 512), BF16), shape((2, 512, 256), BF16),
            shape((112, 512), BF16), pltpu.HBM((2, 512, 512), BF16), pltpu.HBM((256, 512), BF16),
            pltpu.HBM((128, 512), BF16), pltpu.HBM((16, 512), BF16),
        ),
        in_specs=[VMEM] * 10, out_specs=(VMEM,) * 8, name="prepare", cost_estimate=work,
    )(
        token, waves, steps, lift, lift_bias[None], bypass_in, bias_in[None], bypass_out,
        bias_out[None], project,
    )
    mine, prepared = lax.optimization_barrier((exchange(mixed), prepared))
    own_t, mate_t, spread_t, pack, fine_t, wide_mix, project_mix, bias_mix = prepared
    mine = mine.reshape(OWNERS * 8, 128)
    own, got = [
        call(
            invert, out_shape=shape((2, 128, 128), F32), in_specs=[VMEM] * 2, out_specs=VMEM,
            name=name, cost_estimate=work,
        )(mine, table)
        for name, table in (("invert_own", own_t), ("invert_mate", mate_t))
    ]
    kept, sent, values = call(
        coarse_level,
        out_shape=(
            shape((2, 128, 128), F32), shape((2, 128, 128), F32),
            pltpu.HBM((8, 2, NZ, 512), BF16),
        ),
        in_specs=[VMEM] * 6, out_specs=(VMEM, VMEM, HBM), name="coarse_level",
        scratch_shapes=[pltpu.VMEM((4, 128, 128), F32)] * 4
        + [pltpu.VMEM((8, 2, NZ, 512), BF16), dma((8,))],
    )(
        own, between_cores(got), pack, fields, z_back, z_fwd,
    )
    spectrum, token = call(
        spread,
        out_shape=(pltpu.HBM((OWNERS * 8, 128), F32), shape((8, 128), F32)),
        in_specs=[VMEM] * 3, out_specs=(HBM, VMEM), name="spread",
        scratch_shapes=[pltpu.VMEM((OWNERS * 8, 128), F32), dma((4,))],
    )(kept, between_cores(sent), spread_t)
    prepared = call(
        bypass,
        out_shape=(pltpu.HBM((8, NZ, 512), F32), pltpu.HBM((CIN, 16, 16, NZ), F32)),
        in_specs=[VMEM, HBM, HBM] + [VMEM] * 5, out_specs=(HBM, VMEM), name="bypass",
        scratch_shapes=[
            pltpu.VMEM((8, 2, NZ, 512), BF16), pltpu.VMEM((8, NZ, 512), F32),
            pltpu.VMEM((256, 512), BF16), dma((9,)), dma((8,)),
        ],
        cost_estimate=work,
    )(
        token, stay(values), stay(wide_mix), fields, lift, lift_bias[None], project,
        project_bias[:, None],
    )
    arrived, prepared = lax.optimization_barrier(
        (exchange(spectrum.reshape(OWNERS, 8, 128)), prepared)
    )
    skip, base = prepared
    mixed = call(
        second_mix,
        out_shape=shape((OWNERS // 2, 8, 128), F32),
        in_specs=[VMEM, VMEM], out_specs=VMEM, name="second_mix",
    )(arrived, spectral_out)
    mine = exchange(mixed, CHIPS).reshape(OWNERS * 4, 128)
    return pl.pallas_call(
        fine_level, compiler_params=pltpu.CompilerParams(vmem_limit_bytes=32 << 20),
        out_shape=shape((CIN, 16, 16, NZ), F32),
        in_specs=[VMEM] * 3 + [HBM] * 5, out_specs=HBM, name="fine_level",
        scratch_shapes=[
            pltpu.VMEM((CIN, 16, 16, NZ), F32), pltpu.VMEM((CIN, 16, 16, NZ), F32),
            pltpu.VMEM((2, 512, 128), F32), pltpu.VMEM((4, 256, 128), F32),
            pltpu.VMEM((8, NZ, 512), F32), pltpu.VMEM((4 * NZ, 256), BF16),
            pltpu.VMEM((128, 512), BF16), pltpu.VMEM((16, 512), BF16), dma((11,)), dma((8,)),
            dma((8,)),
        ],
    )(
        mine, between_cores(mine), fine_t, stay(jnp.asarray(fine_z_table())), stay(skip),
        stay(project_mix), stay(bias_mix), stay(base),
    )


def solution(mesh):
    owned = P(AXES, None, None, None, None)
    grid = P(None, ("x", "core"), "gy", None)
    in_specs = (grid, P(), P(), owned, P(), P(), owned, P(), P(), P(), P())
    cores = jax.sharding.Mesh(mesh.devices.reshape(4, 2, 16), AXES)
    return jax.shard_map(
        on_device, mesh=cores, in_specs=in_specs, out_specs=grid, check_vma=False
    )
```

```python
import functools
import math

import jax
import jax.numpy as jnp
import numpy as np
from jax import lax
from jax.experimental import pallas as pl
from jax.experimental.pallas import tpu as pltpu
from jax.sharding import PartitionSpec as P

KX, KY, KZ = 16, 16, 8
NX, NY, NZ = 128, 256, 128
CIN, C1, C2 = 4, 32, 64
AXES = ("x", "core", "gy")
CHIPS = ("x", "gy")
OWNERS = 128
TOTAL = NX * NY * NZ
BACK = math.sqrt(2.0 / (KX * KY * KZ))
F32 = jnp.float32
BF16 = jnp.bfloat16
UNROLL = 8
FINE_GROUP = 16
VMEM = pl.BlockSpec(memory_space=pltpu.VMEM)
HBM = pl.BlockSpec(memory_space=pltpu.HBM)
PARAMS = pltpu.CompilerParams(vmem_limit_bytes=16 << 20)
ALONE = pltpu.CompilerParams(vmem_limit_bytes=60 << 20)


def mode_frequencies():
    centered = np.where(np.arange(16) < 8, np.arange(16), np.arange(16) - 16)
    n = np.arange(OWNERS)
    fx = np.stack([centered[n // 8]] * 2)
    fy = np.stack([centered[2 * (n % 8) + s] for s in range(2)])
    return fx, fy


def place_angles(xs, ys, x_length, y_length):
    fx, fy = mode_frequencies()
    turns = (
        fx[:, :, None, None] * xs[None, None, :, None] / x_length
        + fy[:, :, None, None] * ys[None, None, None, :] / y_length
    )
    return 2.0 * np.pi * turns


def wave_tables():
    fx, fy = mode_frequencies()
    ahead = np.array([0.0, 0.5 * np.pi])[None, None, :, None]
    places = np.arange(16)[:, None, None, None]
    along_x = 2.0 * np.pi * places * fx[None, :, None, :] / NX + ahead
    along_y = 2.0 * np.pi * places * fy[None, :, None, :] / NY + 0.0 * ahead
    tables = [np.cos(along_x), np.sin(along_x), np.cos(along_y), np.sin(along_y)]
    return np.stack(tables).reshape(4, 16, 512).astype(np.float32)


def phase_steps():
    fx, fy = mode_frequencies()
    steps = np.stack([np.stack([2 * fx, 2 * fx], axis=1), np.stack([fy, fy], axis=1)])
    return steps.reshape(2, 512).astype(np.int32)


def z_angles():
    return 2.0 * np.pi * (np.arange(NZ)[:, None] * np.arange(KZ)[None, :] % NZ) / NZ


def split_np(table):
    high = table.astype(BF16)
    low = (table - high.astype(np.float32)).astype(BF16)
    return high, low


def first_z_table():
    c, s = np.cos(z_angles()), np.sin(z_angles())
    parts = np.array([[c, -s], [-s, -c]]).transpose(2, 0, 1, 3).reshape(NZ, 32)
    high, low = split_np(np.repeat(parts, CIN, axis=1).astype(np.float32))
    return np.concatenate([high, high, low], axis=0)


def first_places_table():
    fx, fy = mode_frequencies()
    places = np.arange(16)
    turns = (
        fx[:, :, None, None] * places[:, None] / NX + fy[:, :, None, None] * places[None, :] / NY
    )
    angles = 2.0 * np.pi * turns
    table = np.stack([np.cos(angles), np.sin(angles)], axis=1) / math.sqrt(TOTAL)
    return np.stack(split_np(table.reshape(512, 256).astype(np.float32)))


def inverse_z_table():
    table = np.stack([np.cos(z_angles()), -np.sin(z_angles())], axis=2)
    high, low = split_np(table.reshape(NZ, 16).astype(np.float32))
    ones = np.zeros((16, NZ), BF16)
    ones[:3] = 1.0
    return np.concatenate([high.T, high.T, low.T, ones], axis=0)


def fine_z_table():
    table = np.kron(np.eye(4), inverse_z_table().T.astype(np.float32))
    return table.astype(BF16)


def forward_z_table():
    table = np.stack([np.cos(z_angles()).T, -np.sin(z_angles()).T], axis=0)
    high, low = split_np(table.reshape(16, NZ).astype(np.float32))
    return np.block([[high, high], [low, np.zeros_like(low)]])


def split(x):
    high = x.astype(BF16)
    return high, (x - high.astype(F32)).astype(BF16)


def bias_rows(bias):
    high, less = split(bias)
    least = (bias - high.astype(F32) - less.astype(F32)).astype(BF16)
    row = iota((16, bias.shape[1]), 0)
    rows = [v.astype(F32) for v in (high, less, least)]
    total = jnp.where(row == 0, rows[0], jnp.where(row == 1, rows[1], rows[2]))
    return jnp.where(row < 3, total, 0.0).astype(BF16)


def mm(a, b, dims=((1,), (0,))):
    return lax.dot_general(a, b, (dims, ((), ())), preferred_element_type=F32)


def mm3(a, b, dims=((1,), (0,))):
    ah, al = split(a)
    bh, bl = split(b)
    return mm(ah, bh, dims) + mm(ah, bl, dims) + mm(al, bh, dims)


def exact(a, b, dims=((1,), (0,))):
    return lax.dot_general(
        a, b, (dims, ((), ())), precision=lax.Precision.HIGHEST, preferred_element_type=F32
    )


def iota(shape, dim):
    return lax.broadcasted_iota(jnp.int32, shape, dim)


def ones_where(condition):
    return jnp.where(condition, 1.0, 0.0).astype(F32)


def gelu(x):
    return 0.5 * x * (1.0 + lax.erf(x * math.sqrt(0.5)))


def regroup(rows):
    group = iota(rows[0].shape, 1) // 32
    made = []
    for v in range(4):
        total = rows[v]
        for u in range(4):
            if u != v:
                moved = pltpu.roll(rows[u], ((u - v) % 4) * 32, 1)
                total = jnp.where(group == u, moved, total)
        made.append(total)
    return made


def my_place():
    return 2 * lax.axis_index("x") + lax.axis_index("core"), lax.axis_index("gy")


def phases(steps, place):
    turns = (steps[0:1] * place[0] + steps[1:2] * place[1]) & 15
    cos = sin = jnp.zeros(turns.shape, F32)
    for n in range(16):
        here = turns == n
        cos = jnp.where(here, math.cos(2.0 * math.pi * n / 16), cos)
        sin = jnp.where(here, math.sin(2.0 * math.pi * n / 16), sin)
    return cos, sin


def device_waves(waves, steps, place):
    cos, sin = phases(steps, place)
    return waves[0] * cos - waves[1] * sin, waves[1] * cos + waves[0] * sin


def wave_rows(along_x, cos_y, sin_y, xs):
    cos_x, sin_x = along_x
    real = [cos_x[x : x + 1] * cos_y - sin_x[x : x + 1] * sin_y for x in xs]
    imag = [sin_x[x : x + 1] * cos_y + cos_x[x : x + 1] * sin_y for x in xs]
    return jnp.concatenate(real, axis=0), jnp.concatenate(imag, axis=0)


def first_spectrum(
    fields, ztab_h, ptab_h, steps_h, out, token, fields_v, ztab, ptab, steps, sems,
):
    pairs = [(steps_h, steps), (ztab_h, ztab)]
    pairs += [(fields.at[ch], fields_v.at[ch]) for ch in range(CIN)]
    pairs.append((ptab_h, ptab))
    copies = [
        pltpu.make_async_copy(source, target, sems.at[i])
        for i, (source, target) in enumerate(pairs)
    ]
    for copy in copies:
        copy.start()
    copies[0].wait()
    cos, sin = phases(steps, my_place())
    turn = [v[:, at : at + 128] for at in (0, 256) for v in (cos, sin)]
    turn = jnp.concatenate(turn + [jnp.zeros((124, 128), F32)], axis=0).T
    channel = iota((256, 128), 1) % CIN
    total = jnp.zeros((256, 128), F32)
    copies[1].wait()
    for ch in range(CIN):
        copies[2 + ch].wait()
        fh, fl = split(fields_v[ch].reshape(256, NZ))
        term = mm(jnp.concatenate([fh, fl], axis=1), ztab[:256]) + mm(fh, ztab[256:])
        total = jnp.where(channel == ch, term, total)
    copies[-1].wait()
    th, tl = split(total)
    both = mm(ptab[0], jnp.concatenate([th, tl], axis=1))
    both = both[:, :128] + both[:, 128:] + mm(ptab[1], th)
    low = iota((128, 128), 1) < 64
    rows = []
    for s in range(2):
        part_cos = both[256 * s : 256 * s + 128]
        part_sin = both[256 * s + 128 : 256 * s + 256]
        part_sin = pltpu.roll(part_sin, 64, 1)
        pair = jnp.where(low, part_cos + part_sin, part_cos - part_sin)
        cos_s, sin_s = turn[:, 2 * s : 2 * s + 1], turn[:, 2 * s + 1 : 2 * s + 2]
        rows.append(cos_s * pair + sin_s * pltpu.roll(pair, 64, 1))
    out[...] = jnp.where(low, rows[0], pltpu.roll(rows[1], 64, 1))
    token[...] = rows[0][:8]


def prepare_mix(after, weights, lift, lift_bias, weights_v, lift_wide, bias_column, sem):
    copy = pltpu.make_async_copy(weights, weights_v, sem)
    copy.start()
    lift_wide[...] = exact(lift[...], ones_where(iota((CIN, 128), 0) == iota((CIN, 128), 1) % 4))
    gx, gy = my_place()
    at_zero = (iota((C1, 32), 1) + gx + gy) == 0
    bias_column[...] = jnp.where(at_zero, lift_bias[...] * math.sqrt(TOTAL), 0.0)
    copy.wait()


def core_columns(table):
    first = lax.axis_index("core") == 0
    lane = iota((table.shape[0], 128), 1)
    made = []
    for t in range(4):
        tile = table[:, 128 * t : 128 * t + 128]
        tile = jnp.where(first, tile, pltpu.roll(tile, 112, 1))
        total = tile
        for x in range(1, 4):
            total = jnp.where(lane // 16 == x, pltpu.roll(tile, 128 - 16 * x, 1), total)
        made.append(total)
    pairs = [jnp.where(lane < 64, made[t], pltpu.roll(made[t + 1], 64, 1)) for t in (0, 2)]
    return jnp.concatenate(pairs, axis=1)


def prepare(
    after, waves, steps, lift, lift_bias, bypass_in, bias_in, bypass_out, bias_out, project,
    own_t, mate_t, spread_t, pack, fine_t, wide_mix, project_mix, bias_mix,
):
    nt = ((1,), (1,))
    gx, gy = my_place()
    own = device_waves(waves, steps, (gx, gy))
    mate = device_waves(waves, steps, (gx + 1 - 2 * (gx % 2), gy))
    cos_y = jnp.concatenate([waves[2, 2 * q : 2 * q + 1] for q in range(8)], axis=0)
    sin_y = jnp.concatenate([waves[3, 2 * q : 2 * q + 1] for q in range(8)], axis=0)
    tables = [
        jnp.concatenate(wave_rows(along, cos_y, sin_y, range(0, 16, 2)), axis=0)
        for along in (own, mate)
    ]
    own_t[0:128], own_t[128:256] = split(core_columns(tables[0]) * BACK)
    mate_t[0:128], mate_t[128:256] = split(core_columns(tables[1]) * BACK)
    scale = 1.0 / math.sqrt(TOTAL / 4.0)
    for patch in range(2):
        at = slice(128 * patch, 128 * patch + 128)
        high, less = split(tables[patch].T * scale)
        spread_t[0, :, at] = high
        spread_t[1, :, at] = less
    lanes = [
        ones_where(iota((C2, 128), 0) == 32 * h + iota((C2, 128), 1) % 32) for h in range(2)
    ]
    through = exact(lift[...], bypass_in[...], ((0,), (1,)))
    through = exact(ones_where(iota((32, CIN), 0) // 8 == iota((32, CIN), 1)), through)
    offset = bias_in[...] + exact(lift_bias[...], bypass_in[...], nt)
    for t in range(4):
        at = slice(128 * t, 128 * t + 128)
        same = iota((32, 128), 0) % 8 == 4 * (t // 2) + iota((32, 128), 1) // 32
        high, less = split(jnp.where(same, exact(through, lanes[t % 2]), 0.0))
        rows = bias_rows(exact(offset, lanes[t % 2]))
        pack[:, at] = jnp.concatenate([rows, high, less, high], axis=0)
    spread_d = ones_where(iota((C1, 256), 0) == iota((C1, 256), 1) % 32)
    same = iota((128, 256), 0) // 32 == iota((128, 256), 1) // 64
    for h in range(2):
        pick = ones_where(iota((128, C2), 1) == 32 * h + iota((128, C2), 0) % 32)
        wide = exact(exact(pick, bypass_out[...], nt), spread_d)
        high, less = split(jnp.where(same, wide, 0.0))
        wide_mix[128 * h : 128 * h + 128] = jnp.concatenate([high, less], axis=1)
    scaled = (own[0] * BACK, own[1] * BACK)
    for x in range(0, 16, 8):
        pair = wave_rows(scaled, waves[2], waves[3], range(x, x + 8))
        for part in range(2):
            at = slice(256 * part + 16 * x, 256 * part + 16 * x + 128)
            high, less = split(pair[part])
            fine_t[0, at] = high
            fine_t[1, at] = less
    lanes = ones_where(iota((C1, 512), 0) == iota((C1, 512), 1) % 32)
    bias_mix[...] = bias_rows(exact(bias_out[...], lanes))
    pick = ones_where(iota((512, C1), 1) == iota((512, C1), 0) % 32)
    onto = ones_where(iota((CIN, 128), 0) == iota((CIN, 128), 1) % 64 // 16)
    made = exact(exact(pick, project[...], nt), onto)
    lane = iota((512, 128), 1)
    made = jnp.where(iota((512, 128), 0) // 32 == lane % 16, made, 0.0)
    high = made.astype(BF16).astype(F32)
    project_mix[...] = jnp.where(lane < 64, high, made - high).T.astype(BF16)


def bypass(
    after, values, wide_mix_h, fields, lift, lift_bias, project, project_bias, skip, base,
    values_v, skip_v, wide_mix, in_sems, out_sems,
):
    def taken(p):
        return pltpu.make_async_copy(values.at[p], values_v.at[p], in_sems.at[p])

    def given(p):
        return pltpu.make_async_copy(skip_v.at[p], skip.at[p], out_sems.at[p])

    mix_copy = pltpu.make_async_copy(wide_mix_h, wide_mix, in_sems.at[8])
    mix_copy.start()
    for p in range(8):
        taken(p).start()
    across = exact(project[...], lift[...])
    constant = project_bias[...] + exact(project[...], lift_bias[...], ((1,), (1,)))
    mix_copy.wait()

    def step(x, carry):
        for o in range(CIN):
            total = jnp.broadcast_to(constant[o : o + 1], (16, NZ))
            for ch in range(CIN):
                total += across[o : o + 1, ch : ch + 1] * fields[ch, x]
            base[o, x] = total
        return carry

    lax.fori_loop(0, 16, step, 0)

    for group in range(0, 8, 4):
        ps = range(group, group + 4)
        for p in ps:
            taken(p).wait()
        for q in range(2):
            at = slice(256 * q, 256 * q + 256)
            high, less = [
                jnp.concatenate([values_v[p, i, :, at] for p in ps], axis=0) for i in range(2)
            ]
            wide = mm(high, wide_mix[:, :256]) + mm(high, wide_mix[:, 256:])
            wide += mm(less, wide_mix[:, :256])
            for u, p in enumerate(ps):
                skip_v[p, :, at] = wide[128 * u : 128 * u + 128]
        for p in ps:
            given(p).start()
    for p in range(8):
        given(p).wait()


def mixed_row(columns, weights, wide):
    pieces = [[[None] * KZ for _ in range(2)] for _ in range(2)]
    for s in range(2):
        for k in range(KZ):
            real, imag = columns(s, 0, k), columns(s, 1, k)
            wr, wi = weights[s, 0, k], weights[s, 1, k]
            pieces[s][0][k] = jnp.sum(real * wr - imag * wi, axis=0, keepdims=True)
            pieces[s][1][k] = jnp.sum(real * wi + imag * wr, axis=0, keepdims=True)
    per = 128 // wide
    return [
        jnp.concatenate(
            [
                jnp.concatenate(
                    [v[:, at : at + wide] for v in pieces[s][part][k : k + per]], axis=1
                )
                for s in range(2)
                for part in range(2)
                for k in range(0, KZ, per)
            ],
            axis=0,
        )
        for at in range(0, weights.shape[-1], wide)
    ]


def first_mix(arrived, lift_wide, bias_column, weights, out, token, blocks, sems):
    row = jnp.sum(arrived[...], axis=0, keepdims=True)
    source = lax.broadcasted_iota(jnp.int32, (128, 32), 0) // CIN
    pick = (source == lax.broadcasted_iota(jnp.int32, (128, 32), 1)).astype(F32)
    lifted = (
        lax.dot_general(
            lift_wide[...] * row, pick, (((1,), (0,)), ((), ())),
            precision=lax.Precision.HIGHEST, preferred_element_type=F32,
        )
        + bias_column[...]
    )

    def column(s, part, k):
        at = s * 16 + part * 8 + k
        return lifted[:, at : at + 1]

    halves = mixed_row(column, weights, 32)
    token[...] = halves[0]
    block = jnp.concatenate(halves, axis=0)
    for i in range(16):
        blocks[i] = block
    copies = [
        pltpu.make_async_copy(blocks, out.at[pl.ds(16 * i, 16)], sems.at[i]) for i in range(4)
    ]
    for copy in copies:
        copy.start()
    for copy in copies:
        copy.wait()


def second_mix(arrived, weights, out):
    sums = [None, None]
    for n in range(OWNERS):
        half = n // 16 % 2
        sums[half] = arrived[n] if sums[half] is None else sums[half] + arrived[n]
    stacked = jnp.concatenate(sums + [jnp.zeros((112, 128), F32)], axis=0).T

    def column(s, part, k):
        at = (s * 2 + part) * 2 + k // 4
        rows = slice(k % 4 * 32, k % 4 * 32 + 32)
        return jnp.concatenate([stacked[rows, at : at + 1], stacked[rows, at + 8 : at + 9]], axis=0)

    (block,) = mixed_row(column, weights, 32)
    for n in range(OWNERS // 2):
        out[n] = block


def invert(arrived, table, out):
    modes = []
    for t in range(4):
        tiles = [
            arrived[pl.ds(8 * h + 2 * t + u, OWNERS // 2, stride=16), :]
            for h in range(2)
            for u in range(2)
        ]
        modes.append(jnp.concatenate(tiles, axis=1))
    mh, ml = split(jnp.concatenate(modes, axis=0))
    made = mm(table[...], mh)
    made = made[:128] + made[128:] + mm(table[:128], ml)
    for j in range(4):
        out[j] = made[:, 128 * j : 128 * j + 128]


def coarse_level(
    own, got, pack, fields, z_back, z_fwd,
    kept, sent, values, y_s, rhs_s, g_s, t_s, values_v, sems,
):
    core = lax.axis_index("core")
    for j in range(4):
        y_s[j] = own[j] + got[j]
    for h in range(2):
        for t in range(2):
            for q in range(2):
                made = regroup(
                    [y_s[2 * h + t, pl.ds(4 * q + u, 16, stride=8), :] for u in range(4)]
                )
                for v in range(4):
                    rhs_s[2 * q + h, pl.ds(16 * (4 * t + v), 16), :] = made[v]

    def step(p, carry):
        rows = [rhs_s[t, pl.ds(p, 16, stride=8), :] for t in range(4)]
        high, less = split(jnp.concatenate(rows, axis=1))
        pooled = []
        for ch in range(CIN):
            total = jnp.zeros((8, 128), F32)
            for dx in range(2):
                for dy in range(2):
                    total += fields[ch, 2 * p + dx, pl.ds(dy, 8, stride=2), :]
            pooled.append(total * 0.25)
        ph, pll = split(jnp.concatenate(pooled, axis=0))
        left = jnp.concatenate([z_back[...], ph, ph, pll], axis=0)
        right = jnp.concatenate([high, less, high, pack[...]], axis=0)
        value = gelu(mm(left, right, ((0,), (0,))))
        vh, vl = split(value)
        made = mm(z_fwd[...], jnp.concatenate([vh, vl], axis=0))
        made = made[:16] + made[16:]
        for t in range(4):
            at = slice(128 * t, 128 * t + 128)
            g_s[t, pl.ds(pl.multiple_of(p * 8, 8), 8), :] = made[:8, at]
            g_s[t, pl.ds(pl.multiple_of(p * 8 + 64, 8), 8), :] = made[8:, at]
        values_v[p, 0] = vh
        values_v[p, 1] = vl
        pltpu.make_async_copy(values_v.at[p], values.at[p], sems.at[p]).start()
        return carry

    lax.fori_loop(0, 8, step, 0, unroll=UNROLL)
    for h in range(2):
        for t in range(2):
            for q in range(2):
                made = regroup(
                    [g_s[2 * q + h, pl.ds(4 * t + v, 16, stride=8), :] for v in range(4)]
                )
                for u in range(4):
                    t_s[2 * h + t, pl.ds(4 * q + u, 16, stride=8), :] = made[u]
    for t in range(2):
        kept[t] = t_s[2 * core + t]
        sent[t] = t_s[2 * (1 - core) + t]
    for p in range(8):
        pltpu.make_async_copy(values_v.at[p], values.at[p], sems.at[p]).wait()


def spread(kept, got, table, out, token, out_v, sems):
    rows = [jnp.concatenate([ref[0], ref[1]], axis=1) for ref in (kept, got)]
    th, tl = split(jnp.concatenate(rows, axis=0))
    copies = []
    for j in range(4):
        ah, al = [
            jnp.concatenate([table[i, pl.ds(128 * t + 32 * j, 32)] for t in range(4)], axis=0)
            for i in range(2)
        ]
        made = mm(ah, th) + mm(ah, tl) + mm(al, th)
        for t in range(4):
            for u in range(2):
                piece = made[32 * t : 32 * t + 32, 128 * u : 128 * u + 128]
                out_v[pl.ds(256 * j + 2 * t + u, 32, stride=8), :] = piece
        rows = pl.ds(256 * j, 256)
        copies.append(pltpu.make_async_copy(out_v.at[rows], out.at[rows], sems.at[j]))
        copies[-1].start()
    token[...] = out_v[:8]
    for copy in copies:
        copy.wait()


def fine_level(
    mine, other, table, z_back_h, skip, project_h, bias_h, base_h, out, base, out_v,
    y_s, rhs_s, skip_v, z_back, project_mix, bias_mix, sems, base_sems, out_sems,):
    def taken(p):
        rows = pl.ds(2 * p, 2)
        return (
            pltpu.make_async_copy(skip.at[p], skip_v.at[p], sems.at[p]),
            pltpu.make_async_copy(base_h.at[:, rows], base.at[:, rows], base_sems.at[p]),
        )

    def given(p):
        rows = pl.ds(2 * p, 2)
        return pltpu.make_async_copy(out_v.at[:, rows], out.at[:, rows], out_sems.at[p])

    small = [
        pltpu.make_async_copy(source, target, sems.at[i])
        for i, source, target in (
            (8, z_back_h, z_back), (9, project_h, project_mix), (10, bias_h, bias_mix)
        )
    ]
    for copy in small:
        copy.start()
    for p in range(8):
        for copy in taken(p):
            copy.start()
    first = lax.axis_index("core") == 0
    modes = []
    for t in range(4):
        tiles = []
        for u in range(2):
            a, b = [ref[pl.ds(2 * t + u, OWNERS // 2, stride=8), :] for ref in (mine, other)]
            cores = jnp.where(first, a, b), jnp.where(first, b, a)
            rows = [cores[c][16 * x : 16 * x + 16] for x in range(4) for c in range(2)]
            tiles.append(jnp.concatenate(rows, axis=0))
        modes.append(jnp.concatenate(tiles, axis=1))
    mh, ml = split(jnp.concatenate(modes, axis=0))
    for t in range(4):
        at = slice(128 * t, 128 * t + 128)
        made = mm(table[0, at], mh) + mm(table[0, at], ml) + mm(table[1, at], mh)
        y_s[0, at] = made[:, :128]
        y_s[1, at] = made[:, 128:]
    for t in range(2):
        for y in range(4):
            made = regroup([y_s[t, pl.ds(4 * y + u, 32, stride=16), :] for u in range(4)])
            for v in range(4):
                rhs_s[y, pl.ds(32 * (4 * t + v), 32), :] = made[v]
    for copy in small:
        copy.wait()

    def step(i, carry):
        rights = []
        for u in range(FINE_GROUP):
            x = FINE_GROUP * i + u
            rows = [rhs_s[t, pl.ds(x, 16, stride=16), :] for t in range(4)]
            high, less = split(jnp.concatenate(rows, axis=1))
            rights += [high, less, high, bias_mix[...]]
        before = jnp.concatenate(
            [
                mm(z_back[...], jnp.concatenate(rights[at : at + 16], axis=0))
                for at in range(0, 4 * FINE_GROUP, 16)
            ],
            axis=0,
        )
        for v in range(FINE_GROUP // 2):
            p = FINE_GROUP // 2 * i + v
            for copy in taken(p):
                copy.wait()
        skips = [skip_v[FINE_GROUP // 2 * i + u // 2] for u in range(FINE_GROUP)]
        vh, vl = split(gelu(before + jnp.concatenate(skips, axis=0)))
        made = mm(project_mix[...], vh, ((1,), (1,)))
        made = made[:64] + made[64:] + mm(project_mix[:64], vl, ((1,), (1,)))
        for u in range(FINE_GROUP):
            x = FINE_GROUP * i + u
            for o in range(CIN):
                piece = made[16 * o : 16 * o + 16, 128 * u : 128 * u + 128]
                out_v[o, x] = piece + base[o, x]
        for v in range(FINE_GROUP // 2):
            given(FINE_GROUP // 2 * i + v).start()
        return carry

    lax.fori_loop(0, 16 // FINE_GROUP, step, 0)
    for p in range(8):
        given(p).wait()


def exchange(tiles, axes=AXES):
    return lax.all_to_all(tiles, axes, split_axis=0, concat_axis=0, tiled=True)


def between_cores(array):
    return lax.ppermute(array, "core", [(0, 1), (1, 0)])


def stay(array):
    return pltpu.with_memory_space_constraint(array, pltpu.HBM)


def on_device(
    fields, lift, lift_bias, spectral_in, bypass_in, bias_in, spectral_out, bypass_out, bias_out,
    project, project_bias,
):
    waves, steps = wave_tables(), phase_steps()
    z_back, z_fwd = inverse_z_table(), forward_z_table()
    call = functools.partial(pl.pallas_call, compiler_params=PARAMS)
    shape = jax.ShapeDtypeStruct
    dma = pltpu.SemaphoreType.DMA
    work = pl.CostEstimate(flops=1 << 31, transcendentals=0, bytes_accessed=6 << 20)
    spectrum, token = pl.pallas_call(
        first_spectrum,
        out_shape=(shape((OWNERS, 128), F32), shape((8, 128), F32)),
        in_specs=[HBM] * 4, out_specs=(VMEM, VMEM),
        scratch_shapes=[
            pltpu.VMEM((CIN, 16, 16, NZ), F32), pltpu.VMEM((384, 128), BF16),
            pltpu.VMEM((2, 512, 256), BF16), pltpu.VMEM((2, 512), jnp.int32), dma((7,)),
        ],
        name="first_spectrum", compiler_params=ALONE,
    )(fields, first_z_table(), first_places_table(), steps)
    prepared = call(
        prepare_mix,
        out_shape=(
            shape((2, 2, KZ, C1, C2), F32), shape((C1, 128), F32), shape((C1, 32), F32),
        ),
        in_specs=[VMEM, HBM, VMEM, VMEM], out_specs=(VMEM,) * 3, name="prepare_mix",
        scratch_shapes=[dma(())], cost_estimate=work,
    )(token, stay(spectral_in), lift, lift_bias[:, None])
    arrived, prepared = lax.optimization_barrier((exchange(spectrum), prepared))
    weights, lift_wide, bias_column = prepared
    mixed, token = call(
        first_mix,
        out_shape=(pltpu.HBM((OWNERS // 2, 16, 128), F32), shape((8, 128), F32)),
        in_specs=[VMEM] * 4, out_specs=(HBM, VMEM), name="first_mix",
        scratch_shapes=[pltpu.VMEM((16, 16, 128), F32), dma((4,))],
    )(arrived, lift_wide, bias_column, weights)
    prepared = call(
        prepare,
        out_shape=(
            shape((256, 256), BF16), shape((256, 256), BF16), shape((2, 512, 256), BF16),
            shape((112, 512), BF16), pltpu.HBM((2, 512, 512), BF16), pltpu.HBM((256, 512), BF16),
            pltpu.HBM((128, 512), BF16), pltpu.HBM((16, 512), BF16),
        ),
        in_specs=[VMEM] * 10, out_specs=(VMEM,) * 8, name="prepare", cost_estimate=work,
    )(
        token, waves, steps, lift, lift_bias[None], bypass_in, bias_in[None], bypass_out,
        bias_out[None], project,
    )
    mine, prepared = lax.optimization_barrier((exchange(mixed, CHIPS), prepared))
    own_t, mate_t, spread_t, pack, fine_t, wide_mix, project_mix, bias_mix = prepared
    mine = mine.reshape(OWNERS * 8, 128)
    own, got = [
        call(
            invert, out_shape=shape((4, 128, 128), F32), in_specs=[VMEM] * 2, out_specs=VMEM,
            name=name, cost_estimate=work,
        )(mine, table)
        for name, table in (("invert_own", own_t), ("invert_mate", mate_t))
    ]
    kept, sent, values = call(
        coarse_level,
        out_shape=(
            shape((2, 128, 128), F32), shape((2, 128, 128), F32),
            pltpu.HBM((8, 2, NZ, 512), BF16),
        ),
        in_specs=[VMEM] * 6, out_specs=(VMEM, VMEM, HBM), name="coarse_level",
        scratch_shapes=[pltpu.VMEM((4, 128, 128), F32)] * 4
        + [pltpu.VMEM((8, 2, NZ, 512), BF16), dma((8,))],
    )(
        own, between_cores(got), pack, fields, z_back, z_fwd,
    )
    spectrum, token = call(
        spread,
        out_shape=(pltpu.HBM((OWNERS * 8, 128), F32), shape((8, 128), F32)),
        in_specs=[VMEM] * 3, out_specs=(HBM, VMEM), name="spread",
        scratch_shapes=[pltpu.VMEM((OWNERS * 8, 128), F32), dma((4,))],
    )(kept, between_cores(sent), spread_t)
    prepared = call(
        bypass,
        out_shape=(pltpu.HBM((8, NZ, 512), F32), pltpu.HBM((CIN, 16, 16, NZ), F32)),
        in_specs=[VMEM, HBM, HBM] + [VMEM] * 5, out_specs=(HBM, VMEM), name="bypass",
        scratch_shapes=[
            pltpu.VMEM((8, 2, NZ, 512), BF16), pltpu.VMEM((8, NZ, 512), F32),
            pltpu.VMEM((256, 512), BF16), dma((9,)), dma((8,)),
        ],
        cost_estimate=work,
    )(
        token, stay(values), stay(wide_mix), fields, lift, lift_bias[None], project,
        project_bias[:, None],
    )
    arrived, prepared = lax.optimization_barrier(
        (exchange(spectrum.reshape(OWNERS, 8, 128)), prepared)
    )
    skip, base = prepared
    mixed = call(
        second_mix,
        out_shape=shape((OWNERS // 2, 8, 128), F32),
        in_specs=[VMEM, VMEM], out_specs=VMEM, name="second_mix",
    )(arrived, spectral_out)
    mine = exchange(mixed, CHIPS).reshape(OWNERS * 4, 128)
    return pl.pallas_call(
        fine_level, compiler_params=pltpu.CompilerParams(vmem_limit_bytes=32 << 20),
        out_shape=shape((CIN, 16, 16, NZ), F32),
        in_specs=[VMEM] * 3 + [HBM] * 5, out_specs=HBM, name="fine_level",
        scratch_shapes=[
            pltpu.VMEM((CIN, 16, 16, NZ), F32), pltpu.VMEM((CIN, 16, 16, NZ), F32),
            pltpu.VMEM((2, 512, 128), F32), pltpu.VMEM((4, 256, 128), F32),
            pltpu.VMEM((8, NZ, 512), F32), pltpu.VMEM((4 * NZ, 256), BF16),
            pltpu.VMEM((128, 512), BF16), pltpu.VMEM((16, 512), BF16), dma((11,)), dma((8,)),
            dma((8,)),
        ],
    )(
        mine, between_cores(mine), fine_t, stay(jnp.asarray(fine_z_table())), stay(skip),
        stay(project_mix), stay(bias_mix), stay(base),
    )


def solution(mesh):
    owned = P(AXES, None, None, None, None)
    grid = P(None, ("x", "core"), "gy", None)
    in_specs = (grid, P(), P(), owned, P(), P(), owned, P(), P(), P(), P())
    cores = jax.sharding.Mesh(mesh.devices.reshape(4, 2, 16), AXES)
    return jax.shard_map(
        on_device, mesh=cores, in_specs=in_specs, out_specs=grid, check_vma=False
    )
```

```python
import functools
import math

import jax
import jax.numpy as jnp
import numpy as np
from jax import lax
from jax.experimental import pallas as pl
from jax.experimental.pallas import tpu as pltpu
from jax.sharding import PartitionSpec as P

KX, KY, KZ = 16, 16, 8
NX, NY, NZ = 128, 256, 128
CIN, C1, C2 = 4, 32, 64
AXES = ("x", "core", "gy")
CHIPS = ("x", "gy")
OWNERS = 128
TOTAL = NX * NY * NZ
BACK = math.sqrt(2.0 / (KX * KY * KZ))
F32 = jnp.float32
BF16 = jnp.bfloat16
UNROLL = 8
FINE_GROUP = 16
VMEM = pl.BlockSpec(memory_space=pltpu.VMEM)
HBM = pl.BlockSpec(memory_space=pltpu.HBM)
PARAMS = pltpu.CompilerParams(vmem_limit_bytes=16 << 20)
ALONE = pltpu.CompilerParams(vmem_limit_bytes=60 << 20)


def mode_frequencies():
    centered = np.where(np.arange(16) < 8, np.arange(16), np.arange(16) - 16)
    n = np.arange(OWNERS)
    fx = np.stack([centered[n // 8]] * 2)
    fy = np.stack([centered[2 * (n % 8) + s] for s in range(2)])
    return fx, fy


def place_angles(xs, ys, x_length, y_length):
    fx, fy = mode_frequencies()
    turns = (
        fx[:, :, None, None] * xs[None, None, :, None] / x_length
        + fy[:, :, None, None] * ys[None, None, None, :] / y_length
    )
    return 2.0 * np.pi * turns


def wave_tables():
    fx, fy = mode_frequencies()
    ahead = np.array([0.0, 0.5 * np.pi])[None, None, :, None]
    places = np.arange(16)[:, None, None, None]
    along_x = 2.0 * np.pi * places * fx[None, :, None, :] / NX + ahead
    along_y = 2.0 * np.pi * places * fy[None, :, None, :] / NY + 0.0 * ahead
    tables = [np.cos(along_x), np.sin(along_x), np.cos(along_y), np.sin(along_y)]
    return np.stack(tables).reshape(4, 16, 512).astype(np.float32)


def phase_steps():
    fx, fy = mode_frequencies()
    steps = np.stack([np.stack([2 * fx, 2 * fx], axis=1), np.stack([fy, fy], axis=1)])
    return steps.reshape(2, 512).astype(np.int32)


def z_angles():
    return 2.0 * np.pi * (np.arange(NZ)[:, None] * np.arange(KZ)[None, :] % NZ) / NZ


def split_np(table):
    high = table.astype(BF16)
    low = (table - high.astype(np.float32)).astype(BF16)
    return high, low


def first_z_table():
    c, s = np.cos(z_angles()), np.sin(z_angles())
    parts = np.array([[c, -s], [-s, -c]]).transpose(2, 0, 1, 3).reshape(NZ, 32)
    high, low = split_np(np.repeat(parts, CIN, axis=1).astype(np.float32))
    return np.concatenate([high, high, low], axis=0)


def first_places_table():
    fx, fy = mode_frequencies()
    places = np.arange(16)
    turns = (
        fx[:, :, None, None] * places[:, None] / NX + fy[:, :, None, None] * places[None, :] / NY
    )
    angles = 2.0 * np.pi * turns
    table = np.stack([np.cos(angles), np.sin(angles)], axis=1) / math.sqrt(TOTAL)
    return np.stack(split_np(table.reshape(512, 256).astype(np.float32)))


def inverse_z_table():
    table = np.stack([np.cos(z_angles()), -np.sin(z_angles())], axis=2)
    high, low = split_np(table.reshape(NZ, 16).astype(np.float32))
    ones = np.zeros((16, NZ), BF16)
    ones[:3] = 1.0
    return np.concatenate([high.T, high.T, low.T, ones], axis=0)


def fine_z_table():
    table = np.kron(np.eye(4), inverse_z_table().T.astype(np.float32))
    return table.astype(BF16)


def forward_z_table():
    table = np.stack([np.cos(z_angles()).T, -np.sin(z_angles()).T], axis=0)
    high, low = split_np(table.reshape(16, NZ).astype(np.float32))
    return np.block([[high, high], [low, np.zeros_like(low)]])


def split(x):
    high = x.astype(BF16)
    return high, (x - high.astype(F32)).astype(BF16)


def bias_rows(bias):
    high, less = split(bias)
    least = (bias - high.astype(F32) - less.astype(F32)).astype(BF16)
    row = iota((16, bias.shape[1]), 0)
    rows = [v.astype(F32) for v in (high, less, least)]
    total = jnp.where(row == 0, rows[0], jnp.where(row == 1, rows[1], rows[2]))
    return jnp.where(row < 3, total, 0.0).astype(BF16)


def mm(a, b, dims=((1,), (0,))):
    return lax.dot_general(a, b, (dims, ((), ())), preferred_element_type=F32)


def mm3(a, b, dims=((1,), (0,))):
    ah, al = split(a)
    bh, bl = split(b)
    return mm(ah, bh, dims) + mm(ah, bl, dims) + mm(al, bh, dims)


def exact(a, b, dims=((1,), (0,))):
    return lax.dot_general(
        a, b, (dims, ((), ())), precision=lax.Precision.HIGHEST, preferred_element_type=F32
    )


def iota(shape, dim):
    return lax.broadcasted_iota(jnp.int32, shape, dim)


def ones_where(condition):
    return jnp.where(condition, 1.0, 0.0).astype(F32)


def gelu(x):
    return 0.5 * x * (1.0 + lax.erf(x * math.sqrt(0.5)))


def regroup(rows):
    group = iota(rows[0].shape, 1) // 32
    made = []
    for v in range(4):
        total = rows[v]
        for u in range(4):
            if u != v:
                moved = pltpu.roll(rows[u], ((u - v) % 4) * 32, 1)
                total = jnp.where(group == u, moved, total)
        made.append(total)
    return made


def my_place():
    return 2 * lax.axis_index("x") + lax.axis_index("core"), lax.axis_index("gy")


def phases(steps, place):
    turns = (steps[0:1] * place[0] + steps[1:2] * place[1]) & 15
    cos = sin = jnp.zeros(turns.shape, F32)
    for n in range(16):
        here = turns == n
        cos = jnp.where(here, math.cos(2.0 * math.pi * n / 16), cos)
        sin = jnp.where(here, math.sin(2.0 * math.pi * n / 16), sin)
    return cos, sin


def device_waves(waves, steps, place):
    cos, sin = phases(steps, place)
    return waves[0] * cos - waves[1] * sin, waves[1] * cos + waves[0] * sin


def wave_rows(along_x, cos_y, sin_y, xs):
    cos_x, sin_x = along_x
    real = [cos_x[x : x + 1] * cos_y - sin_x[x : x + 1] * sin_y for x in xs]
    imag = [sin_x[x : x + 1] * cos_y + cos_x[x : x + 1] * sin_y for x in xs]
    return jnp.concatenate(real, axis=0), jnp.concatenate(imag, axis=0)


def first_spectrum(
    fields, ztab_h, ptab_h, steps_h, out, token, fields_v, ztab, ptab, steps, sems,
):
    pairs = [(steps_h, steps), (ztab_h, ztab)]
    pairs += [(fields.at[ch], fields_v.at[ch]) for ch in range(CIN)]
    pairs.append((ptab_h, ptab))
    copies = [
        pltpu.make_async_copy(source, target, sems.at[i])
        for i, (source, target) in enumerate(pairs)
    ]
    for copy in copies:
        copy.start()
    copies[0].wait()
    cos, sin = phases(steps, my_place())
    turn = [v[:, at : at + 128] for at in (0, 256) for v in (cos, sin)]
    turn = jnp.concatenate(turn + [jnp.zeros((124, 128), F32)], axis=0).T
    channel = iota((256, 128), 1) % CIN
    total = jnp.zeros((256, 128), F32)
    copies[1].wait()
    for ch in range(CIN):
        copies[2 + ch].wait()
        fh, fl = split(fields_v[ch].reshape(256, NZ))
        term = mm(jnp.concatenate([fh, fl], axis=1), ztab[:256]) + mm(fh, ztab[256:])
        total = jnp.where(channel == ch, term, total)
    copies[-1].wait()
    th, tl = split(total)
    both = mm(ptab[0], jnp.concatenate([th, tl], axis=1))
    both = both[:, :128] + both[:, 128:] + mm(ptab[1], th)
    low = iota((128, 128), 1) < 64
    rows = []
    for s in range(2):
        part_cos = both[256 * s : 256 * s + 128]
        part_sin = both[256 * s + 128 : 256 * s + 256]
        part_sin = pltpu.roll(part_sin, 64, 1)
        pair = jnp.where(low, part_cos + part_sin, part_cos - part_sin)
        cos_s, sin_s = turn[:, 2 * s : 2 * s + 1], turn[:, 2 * s + 1 : 2 * s + 2]
        rows.append(cos_s * pair + sin_s * pltpu.roll(pair, 64, 1))
    out[...] = jnp.where(low, rows[0], pltpu.roll(rows[1], 64, 1))
    token[...] = rows[0][:8]


def prepare_mix(after, weights, lift, lift_bias, weights_v, lift_wide, bias_column, sem):
    copy = pltpu.make_async_copy(weights, weights_v, sem)
    copy.start()
    lift_wide[...] = exact(lift[...], ones_where(iota((CIN, 128), 0) == iota((CIN, 128), 1) % 4))
    gx, gy = my_place()
    at_zero = (iota((C1, 32), 1) + gx + gy) == 0
    bias_column[...] = jnp.where(at_zero, lift_bias[...] * math.sqrt(TOTAL), 0.0)
    copy.wait()


def core_columns(table):
    first = lax.axis_index("core") == 0
    lane = iota((table.shape[0], 128), 1)
    made = []
    for t in range(4):
        tile = table[:, 128 * t : 128 * t + 128]
        tile = jnp.where(first, tile, pltpu.roll(tile, 112, 1))
        total = tile
        for x in range(1, 4):
            total = jnp.where(lane // 16 == x, pltpu.roll(tile, 128 - 16 * x, 1), total)
        made.append(total)
    pairs = [jnp.where(lane < 64, made[t], pltpu.roll(made[t + 1], 64, 1)) for t in (0, 2)]
    return jnp.concatenate(pairs, axis=1)


def prepare(
    after, waves, steps, lift, lift_bias, bypass_in, bias_in, bypass_out, bias_out, project,
    own_t, mate_t, spread_t, pack, fine_t, wide_mix, project_mix, bias_mix,
):
    nt = ((1,), (1,))
    gx, gy = my_place()
    own = device_waves(waves, steps, (gx, gy))
    mate = device_waves(waves, steps, (gx + 1 - 2 * (gx % 2), gy))
    cos_y = jnp.concatenate([waves[2, 2 * q : 2 * q + 1] for q in range(8)], axis=0)
    sin_y = jnp.concatenate([waves[3, 2 * q : 2 * q + 1] for q in range(8)], axis=0)
    tables = [
        jnp.concatenate(wave_rows(along, cos_y, sin_y, range(0, 16, 2)), axis=0)
        for along in (own, mate)
    ]
    own_t[0:128], own_t[128:256] = split(core_columns(tables[0]) * BACK)
    mate_t[0:128], mate_t[128:256] = split(core_columns(tables[1]) * BACK)
    scale = 1.0 / math.sqrt(TOTAL / 4.0)
    for patch in range(2):
        at = slice(128 * patch, 128 * patch + 128)
        high, less = split(core_columns(tables[patch]).T * scale)
        spread_t[0, :, at] = high
        spread_t[1, :, at] = less
    lanes = [
        ones_where(iota((C2, 128), 0) == 32 * h + iota((C2, 128), 1) % 32) for h in range(2)
    ]
    through = exact(lift[...], bypass_in[...], ((0,), (1,)))
    through = exact(ones_where(iota((32, CIN), 0) // 8 == iota((32, CIN), 1)), through)
    offset = bias_in[...] + exact(lift_bias[...], bypass_in[...], nt)
    for t in range(4):
        at = slice(128 * t, 128 * t + 128)
        same = iota((32, 128), 0) % 8 == 4 * (t // 2) + iota((32, 128), 1) // 32
        high, less = split(jnp.where(same, exact(through, lanes[t % 2]), 0.0))
        rows = bias_rows(exact(offset, lanes[t % 2]))
        pack[:, at] = jnp.concatenate([rows, high, less, high], axis=0)
    spread_d = ones_where(iota((C1, 256), 0) == iota((C1, 256), 1) % 32)
    same = iota((128, 256), 0) // 32 == iota((128, 256), 1) // 64
    for h in range(2):
        pick = ones_where(iota((128, C2), 1) == 32 * h + iota((128, C2), 0) % 32)
        wide = exact(exact(pick, bypass_out[...], nt), spread_d)
        high, less = split(jnp.where(same, wide, 0.0))
        wide_mix[128 * h : 128 * h + 128] = jnp.concatenate([high, less], axis=1)
    scaled = (own[0] * BACK, own[1] * BACK)
    for x in range(0, 16, 8):
        pair = wave_rows(scaled, waves[2], waves[3], range(x, x + 8))
        for part in range(2):
            at = slice(256 * part + 16 * x, 256 * part + 16 * x + 128)
            high, less = split(pair[part])
            fine_t[0, at] = high
            fine_t[1, at] = less
    lanes = ones_where(iota((C1, 512), 0) == iota((C1, 512), 1) % 32)
    bias_mix[...] = bias_rows(exact(bias_out[...], lanes))
    pick = ones_where(iota((512, C1), 1) == iota((512, C1), 0) % 32)
    onto = ones_where(iota((CIN, 128), 0) == iota((CIN, 128), 1) % 64 // 16)
    made = exact(exact(pick, project[...], nt), onto)
    lane = iota((512, 128), 1)
    made = jnp.where(iota((512, 128), 0) // 32 == lane % 16, made, 0.0)
    high = made.astype(BF16).astype(F32)
    project_mix[...] = jnp.where(lane < 64, high, made - high).T.astype(BF16)


def bypass(
    after, values, wide_mix_h, fields, lift, lift_bias, project, project_bias, skip, base,
    values_v, skip_v, wide_mix, in_sems, out_sems,
):
    def taken(p):
        return pltpu.make_async_copy(values.at[p], values_v.at[p], in_sems.at[p])

    def given(p):
        return pltpu.make_async_copy(skip_v.at[p], skip.at[p], out_sems.at[p])

    mix_copy = pltpu.make_async_copy(wide_mix_h, wide_mix, in_sems.at[8])
    mix_copy.start()
    for p in range(8):
        taken(p).start()
    across = exact(project[...], lift[...])
    constant = project_bias[...] + exact(project[...], lift_bias[...], ((1,), (1,)))
    mix_copy.wait()

    def step(x, carry):
        for o in range(CIN):
            total = jnp.broadcast_to(constant[o : o + 1], (16, NZ))
            for ch in range(CIN):
                total += across[o : o + 1, ch : ch + 1] * fields[ch, x]
            base[o, x] = total
        return carry

    lax.fori_loop(0, 16, step, 0)

    for group in range(0, 8, 4):
        ps = range(group, group + 4)
        for p in ps:
            taken(p).wait()
        for q in range(2):
            at = slice(256 * q, 256 * q + 256)
            high, less = [
                jnp.concatenate([values_v[p, i, :, at] for p in ps], axis=0) for i in range(2)
            ]
            wide = mm(high, wide_mix[:, :256]) + mm(high, wide_mix[:, 256:])
            wide += mm(less, wide_mix[:, :256])
            for u, p in enumerate(ps):
                skip_v[p, :, at] = wide[128 * u : 128 * u + 128]
        for p in ps:
            given(p).start()
    for p in range(8):
        given(p).wait()


def mixed_row(columns, weights, wide):
    pieces = [[[None] * KZ for _ in range(2)] for _ in range(2)]
    for s in range(2):
        for k in range(KZ):
            real, imag = columns(s, 0, k), columns(s, 1, k)
            wr, wi = weights[s, 0, k], weights[s, 1, k]
            pieces[s][0][k] = jnp.sum(real * wr - imag * wi, axis=0, keepdims=True)
            pieces[s][1][k] = jnp.sum(real * wi + imag * wr, axis=0, keepdims=True)
    per = 128 // wide
    return [
        jnp.concatenate(
            [
                jnp.concatenate(
                    [v[:, at : at + wide] for v in pieces[s][part][k : k + per]], axis=1
                )
                for s in range(2)
                for part in range(2)
                for k in range(0, KZ, per)
            ],
            axis=0,
        )
        for at in range(0, weights.shape[-1], wide)
    ]


def first_mix(arrived, lift_wide, bias_column, weights, out, token, blocks, sems):
    row = jnp.sum(arrived[...], axis=0, keepdims=True)
    source = lax.broadcasted_iota(jnp.int32, (128, 32), 0) // CIN
    pick = (source == lax.broadcasted_iota(jnp.int32, (128, 32), 1)).astype(F32)
    lifted = (
        lax.dot_general(
            lift_wide[...] * row, pick, (((1,), (0,)), ((), ())),
            precision=lax.Precision.HIGHEST, preferred_element_type=F32,
        )
        + bias_column[...]
    )

    def column(s, part, k):
        at = s * 16 + part * 8 + k
        return lifted[:, at : at + 1]

    halves = mixed_row(column, weights, 32)
    token[...] = halves[0]
    block = jnp.concatenate(halves, axis=0)
    for i in range(16):
        blocks[i] = block
    copies = [
        pltpu.make_async_copy(blocks, out.at[pl.ds(16 * i, 16)], sems.at[i]) for i in range(4)
    ]
    for copy in copies:
        copy.start()
    for copy in copies:
        copy.wait()


def second_mix(arrived, weights, out):
    rows = arrived[0]
    for n in range(1, OWNERS // 2):
        rows += arrived[n]
    stacked = jnp.concatenate([rows, jnp.zeros((112, 128), F32)], axis=0).T

    def column(s, part, k):
        at = (s * 2 + part) * 2 + k // 4
        rows = slice(k % 4 * 32, k % 4 * 32 + 32)
        return jnp.concatenate([stacked[rows, at : at + 1], stacked[rows, at + 8 : at + 9]], axis=0)

    (block,) = mixed_row(column, weights, 32)
    for n in range(OWNERS // 2):
        out[n] = block


def invert(arrived, table, out):
    modes = []
    for t in range(4):
        tiles = [
            arrived[pl.ds(8 * h + 2 * t + u, OWNERS // 2, stride=16), :]
            for h in range(2)
            for u in range(2)
        ]
        modes.append(jnp.concatenate(tiles, axis=1))
    mh, ml = split(jnp.concatenate(modes, axis=0))
    made = mm(table[...], mh)
    made = made[:128] + made[128:] + mm(table[:128], ml)
    for j in range(4):
        out[j] = made[:, 128 * j : 128 * j + 128]


def coarse_level(
    own, got, pack, fields, z_back, z_fwd,
    shared, values, y_s, rhs_s, g_s, values_v, sems,
):
    for j in range(4):
        y_s[j] = own[j] + got[j]
    for h in range(2):
        for t in range(2):
            for q in range(2):
                made = regroup(
                    [y_s[2 * h + t, pl.ds(4 * q + u, 16, stride=8), :] for u in range(4)]
                )
                for v in range(4):
                    rhs_s[2 * q + h, pl.ds(16 * (4 * t + v), 16), :] = made[v]

    def step(p, carry):
        rows = [rhs_s[t, pl.ds(p, 16, stride=8), :] for t in range(4)]
        high, less = split(jnp.concatenate(rows, axis=1))
        pooled = []
        for ch in range(CIN):
            total = jnp.zeros((8, 128), F32)
            for dx in range(2):
                for dy in range(2):
                    total += fields[ch, 2 * p + dx, pl.ds(dy, 8, stride=2), :]
            pooled.append(total * 0.25)
        ph, pll = split(jnp.concatenate(pooled, axis=0))
        left = jnp.concatenate([z_back[...], ph, ph, pll], axis=0)
        right = jnp.concatenate([high, less, high, pack[...]], axis=0)
        value = gelu(mm(left, right, ((0,), (0,))))
        vh, vl = split(value)
        made = mm(z_fwd[...], jnp.concatenate([vh, vl], axis=0))
        made = made[:16] + made[16:]
        for t in range(4):
            at = slice(128 * t, 128 * t + 128)
            g_s[t, pl.ds(pl.multiple_of(p * 8, 8), 8), :] = made[:8, at]
            g_s[t, pl.ds(pl.multiple_of(p * 8 + 64, 8), 8), :] = made[8:, at]
        values_v[p, 0] = vh
        values_v[p, 1] = vl
        pltpu.make_async_copy(values_v.at[p], values.at[p], sems.at[p]).start()
        return carry

    lax.fori_loop(0, 8, step, 0, unroll=UNROLL)
    for h in range(2):
        for t in range(2):
            for q in range(2):
                made = regroup(
                    [g_s[2 * q + h, pl.ds(4 * t + v, 16, stride=8), :] for v in range(4)]
                )
                for u in range(4):
                    shared[2 * h + t, pl.ds(4 * q + u, 16, stride=8), :] = made[u]
    for p in range(8):
        pltpu.make_async_copy(values_v.at[p], values.at[p], sems.at[p]).wait()


def spread(kept, got, table, out, token, out_v, sems):
    rows = [jnp.concatenate([ref[t] for t in range(4)], axis=1) for ref in (kept, got)]
    th, tl = split(jnp.concatenate(rows, axis=0))
    copies = []
    for j in range(4):
        ah, al = [
            jnp.concatenate([table[i, pl.ds(64 * t + 16 * j, 16)] for t in range(4)], axis=0)
            for i in range(2)
        ]
        made = mm(ah, th) + mm(ah, tl) + mm(al, th)
        for t in range(4):
            for h in range(2):
                for u in range(2):
                    at = 128 * (2 * h + u)
                    piece = made[16 * t : 16 * t + 16, at : at + 128]
                    out_v[pl.ds(256 * j + 8 * h + 2 * t + u, 16, stride=16), :] = piece
        rows = pl.ds(256 * j, 256)
        copies.append(pltpu.make_async_copy(out_v.at[rows], out.at[rows], sems.at[j]))
        copies[-1].start()
    token[...] = out_v[:8]
    for copy in copies:
        copy.wait()


def fine_level(
    mine, other, table, z_back_h, skip, project_h, bias_h, base_h, out, base, out_v,
    y_s, rhs_s, skip_v, z_back, project_mix, bias_mix, sems, base_sems, out_sems,):
    def taken(p):
        rows = pl.ds(2 * p, 2)
        return (
            pltpu.make_async_copy(skip.at[p], skip_v.at[p], sems.at[p]),
            pltpu.make_async_copy(base_h.at[:, rows], base.at[:, rows], base_sems.at[p]),
        )

    def given(p):
        rows = pl.ds(2 * p, 2)
        return pltpu.make_async_copy(out_v.at[:, rows], out.at[:, rows], out_sems.at[p])

    small = [
        pltpu.make_async_copy(source, target, sems.at[i])
        for i, source, target in (
            (8, z_back_h, z_back), (9, project_h, project_mix), (10, bias_h, bias_mix)
        )
    ]
    for copy in small:
        copy.start()
    for p in range(8):
        for copy in taken(p):
            copy.start()
    first = lax.axis_index("core") == 0
    modes = []
    for t in range(4):
        tiles = []
        for u in range(2):
            a, b = [ref[pl.ds(2 * t + u, OWNERS // 2, stride=8), :] for ref in (mine, other)]
            cores = jnp.where(first, a, b), jnp.where(first, b, a)
            rows = [cores[c][16 * x : 16 * x + 16] for x in range(4) for c in range(2)]
            tiles.append(jnp.concatenate(rows, axis=0))
        modes.append(jnp.concatenate(tiles, axis=1))
    mh, ml = split(jnp.concatenate(modes, axis=0))
    for t in range(4):
        at = slice(128 * t, 128 * t + 128)
        made = mm(table[0, at], mh) + mm(table[0, at], ml) + mm(table[1, at], mh)
        y_s[0, at] = made[:, :128]
        y_s[1, at] = made[:, 128:]
    for t in range(2):
        for y in range(4):
            made = regroup([y_s[t, pl.ds(4 * y + u, 32, stride=16), :] for u in range(4)])
            for v in range(4):
                rhs_s[y, pl.ds(32 * (4 * t + v), 32), :] = made[v]
    for copy in small:
        copy.wait()

    def step(i, carry):
        rights = []
        for u in range(FINE_GROUP):
            x = FINE_GROUP * i + u
            rows = [rhs_s[t, pl.ds(x, 16, stride=16), :] for t in range(4)]
            high, less = split(jnp.concatenate(rows, axis=1))
            rights += [high, less, high, bias_mix[...]]
        before = jnp.concatenate(
            [
                mm(z_back[...], jnp.concatenate(rights[at : at + 16], axis=0))
                for at in range(0, 4 * FINE_GROUP, 16)
            ],
            axis=0,
        )
        for v in range(FINE_GROUP // 2):
            p = FINE_GROUP // 2 * i + v
            for copy in taken(p):
                copy.wait()
        skips = [skip_v[FINE_GROUP // 2 * i + u // 2] for u in range(FINE_GROUP)]
        vh, vl = split(gelu(before + jnp.concatenate(skips, axis=0)))
        made = mm(project_mix[...], vh, ((1,), (1,)))
        made = made[:64] + made[64:] + mm(project_mix[:64], vl, ((1,), (1,)))
        for u in range(FINE_GROUP):
            x = FINE_GROUP * i + u
            for o in range(CIN):
                piece = made[16 * o : 16 * o + 16, 128 * u : 128 * u + 128]
                out_v[o, x] = piece + base[o, x]
        for v in range(FINE_GROUP // 2):
            given(FINE_GROUP // 2 * i + v).start()
        return carry

    lax.fori_loop(0, 16 // FINE_GROUP, step, 0)
    for p in range(8):
        given(p).wait()


def exchange(tiles, axes=AXES):
    return lax.all_to_all(tiles, axes, split_axis=0, concat_axis=0, tiled=True)


def between_cores(array):
    return lax.ppermute(array, "core", [(0, 1), (1, 0)])


def stay(array):
    return pltpu.with_memory_space_constraint(array, pltpu.HBM)


def on_device(
    fields, lift, lift_bias, spectral_in, bypass_in, bias_in, spectral_out, bypass_out, bias_out,
    project, project_bias,
):
    waves, steps = wave_tables(), phase_steps()
    z_back, z_fwd = inverse_z_table(), forward_z_table()
    call = functools.partial(pl.pallas_call, compiler_params=PARAMS)
    shape = jax.ShapeDtypeStruct
    dma = pltpu.SemaphoreType.DMA
    work = pl.CostEstimate(flops=1 << 31, transcendentals=0, bytes_accessed=6 << 20)
    spectrum, token = pl.pallas_call(
        first_spectrum,
        out_shape=(shape((OWNERS, 128), F32), shape((8, 128), F32)),
        in_specs=[HBM] * 4, out_specs=(VMEM, VMEM),
        scratch_shapes=[
            pltpu.VMEM((CIN, 16, 16, NZ), F32), pltpu.VMEM((384, 128), BF16),
            pltpu.VMEM((2, 512, 256), BF16), pltpu.VMEM((2, 512), jnp.int32), dma((7,)),
        ],
        name="first_spectrum", compiler_params=ALONE,
    )(fields, first_z_table(), first_places_table(), steps)
    prepared = call(
        prepare_mix,
        out_shape=(
            shape((2, 2, KZ, C1, C2), F32), shape((C1, 128), F32), shape((C1, 32), F32),
        ),
        in_specs=[VMEM, HBM, VMEM, VMEM], out_specs=(VMEM,) * 3, name="prepare_mix",
        scratch_shapes=[dma(())], cost_estimate=work,
    )(token, stay(spectral_in), lift, lift_bias[:, None])
    arrived, prepared = lax.optimization_barrier((exchange(spectrum), prepared))
    weights, lift_wide, bias_column = prepared
    mixed, token = call(
        first_mix,
        out_shape=(pltpu.HBM((OWNERS // 2, 16, 128), F32), shape((8, 128), F32)),
        in_specs=[VMEM] * 4, out_specs=(HBM, VMEM), name="first_mix",
        scratch_shapes=[pltpu.VMEM((16, 16, 128), F32), dma((4,))],
    )(arrived, lift_wide, bias_column, weights)
    prepared = call(
        prepare,
        out_shape=(
            shape((256, 256), BF16), shape((256, 256), BF16), shape((2, 256, 256), BF16),
            shape((112, 512), BF16), pltpu.HBM((2, 512, 512), BF16), pltpu.HBM((256, 512), BF16),
            pltpu.HBM((128, 512), BF16), pltpu.HBM((16, 512), BF16),
        ),
        in_specs=[VMEM] * 10, out_specs=(VMEM,) * 8, name="prepare", cost_estimate=work,
    )(
        token, waves, steps, lift, lift_bias[None], bypass_in, bias_in[None], bypass_out,
        bias_out[None], project,
    )
    mine, prepared = lax.optimization_barrier((exchange(mixed, CHIPS), prepared))
    own_t, mate_t, spread_t, pack, fine_t, wide_mix, project_mix, bias_mix = prepared
    mine = mine.reshape(OWNERS * 8, 128)
    own, got = [
        call(
            invert, out_shape=shape((4, 128, 128), F32), in_specs=[VMEM] * 2, out_specs=VMEM,
            name=name, cost_estimate=work,
        )(mine, table)
        for name, table in (("invert_own", own_t), ("invert_mate", mate_t))
    ]
    shared, values = call(
        coarse_level,
        out_shape=(
            shape((4, 128, 128), F32), pltpu.HBM((8, 2, NZ, 512), BF16),
        ),
        in_specs=[VMEM] * 6, out_specs=(VMEM, HBM), name="coarse_level",
        scratch_shapes=[pltpu.VMEM((4, 128, 128), F32)] * 3
        + [pltpu.VMEM((8, 2, NZ, 512), BF16), dma((8,))],
    )(
        own, between_cores(got), pack, fields, z_back, z_fwd,
    )
    spectrum, token = call(
        spread,
        out_shape=(pltpu.HBM((OWNERS * 8, 128), F32), shape((8, 128), F32)),
        in_specs=[VMEM] * 3, out_specs=(HBM, VMEM), name="spread",
        scratch_shapes=[pltpu.VMEM((OWNERS * 8, 128), F32), dma((4,))],
    )(shared, between_cores(shared), spread_t)
    prepared = call(
        bypass,
        out_shape=(pltpu.HBM((8, NZ, 512), F32), pltpu.HBM((CIN, 16, 16, NZ), F32)),
        in_specs=[VMEM, HBM, HBM] + [VMEM] * 5, out_specs=(HBM, VMEM), name="bypass",
        scratch_shapes=[
            pltpu.VMEM((8, 2, NZ, 512), BF16), pltpu.VMEM((8, NZ, 512), F32),
            pltpu.VMEM((256, 512), BF16), dma((9,)), dma((8,)),
        ],
        cost_estimate=work,
    )(
        token, stay(values), stay(wide_mix), fields, lift, lift_bias[None], project,
        project_bias[:, None],
    )
    arrived, prepared = lax.optimization_barrier(
        (exchange(spectrum.reshape(OWNERS // 2, 16, 128), CHIPS), prepared)
    )
    skip, base = prepared
    mixed = call(
        second_mix,
        out_shape=shape((OWNERS // 2, 8, 128), F32),
        in_specs=[VMEM, VMEM], out_specs=VMEM, name="second_mix",
    )(arrived, spectral_out)
    mine = exchange(mixed, CHIPS).reshape(OWNERS * 4, 128)
    return pl.pallas_call(
        fine_level, compiler_params=pltpu.CompilerParams(vmem_limit_bytes=32 << 20),
        out_shape=shape((CIN, 16, 16, NZ), F32),
        in_specs=[VMEM] * 3 + [HBM] * 5, out_specs=HBM, name="fine_level",
        scratch_shapes=[
            pltpu.VMEM((CIN, 16, 16, NZ), F32), pltpu.VMEM((CIN, 16, 16, NZ), F32),
            pltpu.VMEM((2, 512, 128), F32), pltpu.VMEM((4, 256, 128), F32),
            pltpu.VMEM((8, NZ, 512), F32), pltpu.VMEM((4 * NZ, 256), BF16),
            pltpu.VMEM((128, 512), BF16), pltpu.VMEM((16, 512), BF16), dma((11,)), dma((8,)),
            dma((8,)),
        ],
    )(
        mine, between_cores(mine), fine_t, stay(jnp.asarray(fine_z_table())), stay(skip),
        stay(project_mix), stay(bias_mix), stay(base),
    )


def solution(mesh):
    owned = P(AXES, None, None, None, None)
    grid = P(None, ("x", "core"), "gy", None)
    in_specs = (grid, P(), P(), owned, P(), P(), owned, P(), P(), P(), P())
    cores = jax.sharding.Mesh(mesh.devices.reshape(4, 2, 16), AXES)
    return jax.shard_map(
        on_device, mesh=cores, in_specs=in_specs, out_specs=grid, check_vma=False
    )
```
